32 devices in a mesh: wide: 8 (over y, x, core), narrow: 4 (over z).
Axes of the slice: x: 2, y: 2, z: 4, core: 2. Of those that a mesh axis runs over, the one named last changes fastest.
Arguments:
- inputs: bfloat16 [8192, 1024], P(('wide', 'narrow')), may hold values from -6 to 6
- memory: bfloat16 [64, 1024, 1024], P(('wide', 'narrow')), may hold values from -6 to 6
- mem_lengths: int32 [64], P(('wide', 'narrow')), may hold values from 1 to 1024, 40960 in all
- self_qkv: bfloat16 [3, 1024, 1024], P(None, ('wide', 'narrow')), may hold values from -0.1875 to 0.1875
- self_out: bfloat16 [1024, 1024], P(('wide', 'narrow')), may hold values from -0.5 to 0.5
- self_bias: bfloat16 [4, 1024], P(None, ('wide', 'narrow')), may hold values from -3 to 3
- self_gain: bfloat16 [1024], P(('wide', 'narrow')), may hold values from 0.25 to 1.75
- cross_qkv: bfloat16 [3, 1024, 1024], P(None, ('wide', 'narrow')), may hold values from -0.1875 to 0.1875
- cross_out: bfloat16 [1024, 1024], P(('wide', 'narrow')), may hold values from -1 to 1
- cross_bias: bfloat16 [4, 1024], P(None, ('wide', 'narrow')), may hold values from -3 to 3
- cross_gain: bfloat16 [1024], P(('wide', 'narrow')), may hold values from 0.25 to 1.75
- ffn_in: bfloat16 [1024, 4096], P(('wide', 'narrow')), may hold values from -0.1875 to 0.1875
- ffn_out: bfloat16 [4096, 1024], P(('wide', 'narrow')), may hold values from -0.09375 to 0.09375
- ffn_bias_in: bfloat16 [4096], P(('wide', 'narrow')), may hold values from -3 to 3
- ffn_bias_out: bfloat16 [2, 1024], P(None, ('wide', 'narrow')), may hold values from -3 to 3
- ffn_gain: bfloat16 [1024], P(('wide', 'narrow')), may hold values from 0.25 to 1.75
- out_grad: bfloat16 [8192, 1024], P(('wide', 'narrow')), may hold values from -6 to 6
Outputs:
- layer_out: bfloat16 [8192, 1024], P(('wide', 'narrow'))
- input_grad: float32 [8192, 1024], P(('wide', 'narrow'))
- memory_grad: float32 [64, 1024, 1024], P(('wide', 'narrow'))
- self_qkv_grad: float32 [3, 1024, 1024], P(None, ('wide', 'narrow'))
- self_out_grad: float32 [1024, 1024], P(('wide', 'narrow'))
- self_bias_grad: float32 [4, 1024], P(None, ('wide', 'narrow'))
- self_gain_grad: float32 [1024], P(('wide', 'narrow'))
- cross_qkv_grad: float32 [3, 1024, 1024], P(None, ('wide', 'narrow'))
- cross_out_grad: float32 [1024, 1024], P(('wide', 'narrow'))
- cross_bias_grad: float32 [4, 1024], P(None, ('wide', 'narrow'))
- cross_gain_grad: float32 [1024], P(('wide', 'narrow'))
- ffn_in_grad: float32 [1024, 4096], P(('wide', 'narrow'))
- ffn_out_grad: float32 [4096, 1024], P(('wide', 'narrow'))
- ffn_bias_in_grad: float32 [4096], P(('wide', 'narrow'))
- ffn_bias_out_grad: float32 [2, 1024], P(None, ('wide', 'narrow'))
- ffn_gain_grad: float32 [1024], P(('wide', 'narrow'))
The draws below stay inside these ranges and needn't reach their ends.
Inputs may be any that keep to these rules, and one draw needn't show every extreme that they name: Item b's first mem_lengths[b] memory slots are live, the rest padding; the longest item has exactly 1024.
All inputs are finite; a program needn't handle non-finite values. No bound on the sum of `mem_lengths` on one device may be relied on, other than what follows from the above.
Results may differ from the reference program's by a relative error of at most 0.02.
The reference program's roundings to bfloat16 on the way count: a program that leaves them out, or rounds other values in their place, can miss the bound.
Values may be sent and summed in bfloat16 or wider, within the bound.
No kernel may reach another device: no remote copies, remote signals or barrier semaphores. Data moves between devices by JAX's collectives and lax.ppermute only.
A program may use at most 256 MiB of HBM per device.

```python
import math
import jax
import jax.numpy as jnp
import numpy as np
from jax import lax

D = 1024
H = 16
HD = 64
FF = 4096
DEC = 128
MEM_CAP = 1024
ITEMS = 64
TOKENS = 8192


def with_spikes(values, rng, source, target, parts, factor):
    owner, partner = [(jnp.arange(values.shape[axis_at]) // (values.shape[axis_at] // parts)).reshape([-1 if axis == axis_at else 1 for axis in range(values.ndim)]) for axis_at in (source, target)]
    chosen = jax.random.permutation(rng, parts)[partner]
    strong = (owner == chosen) | (owner == (partner + parts // 2) % parts)
    return jnp.where(strong, factor * values, values)


def steps_of(own_key, shape, split, low, largest):
    gain, own = 1.0, jax.random.fold_in(own_key, 6)
    for position, parts in split:
        draws = jnp.exp(jax.random.uniform(jax.random.fold_in(own, position), (parts,), jnp.float32, low / len(split), largest / len(split)))
        gain = gain * jnp.repeat(draws, shape[position] // parts).reshape([-1 if axis == position else 1 for axis in range(len(shape))])
    return gain


def length_profile(amount, total, limit, skew):
    loads = [(1 << 20) // math.isqrt(rank ** skew) + 1 for rank in range(2, amount + 1)]
    surplus, holding = total - limit - (amount - 1), [1] * (amount - 1)
    while surplus > 0:
        movable = [i for i in range(amount - 1) if holding[i] < limit]
        whole, left = sum([loads[i] for i in movable]), surplus
        for i in movable:
            extra = min(limit - holding[i], max(1, left * loads[i] // whole), surplus)
            holding[i] = holding[i] + extra
            surplus = surplus - extra
    return np.array([limit] + holding)


def ragged_sizes(stream_key, count, total, most, skew):
    if count == 2:
        one = jax.random.randint(stream_key, (), max(1, total - most), min(most, total - 1) + 1)
        return jnp.stack([one, total - one])
    tallies = jnp.asarray(length_profile(count, total, most, skew), jnp.int32)
    pairs = (count - 1) // 2
    donor, sink = tallies[1:1 + 2 * pairs:2], tallies[2:2 + 2 * pairs:2]
    room = jnp.minimum(donor - 1, most - sink)
    shifted = jax.random.randint(jax.random.fold_in(stream_key, 1), (pairs,), 0, 1 << 20) % (room + 1)
    tallies = tallies.at[1:1 + 2 * pairs:2].set(donor - shifted).at[2:2 + 2 * pairs:2].set(sink + shifted)
    return tallies[jax.random.permutation(jax.random.fold_in(stream_key, 2), count)]


def normal_values(rng, extent, width, bound, pieces=(), kind=jnp.bfloat16):
    array = jax.random.normal(rng, extent, jnp.float32) * width
    if len(pieces) > 0:
        array = steps_of(rng, extent, pieces, -0.22, 0.18) * array
    return jnp.clip(array, min=-bound, max=bound).astype(kind)


def gaussian_with(key, shape, scale, reach, pieces, heavy, kind=jnp.bfloat16):
    values = scale * jax.random.normal(key, shape, jnp.float32)
    if pieces:
        values = values * steps_of(key, shape, pieces, -0.22, 0.18)
    return jnp.clip(with_spikes(values, jax.random.fold_in(key, 3), *heavy), -reach, reach).astype(kind)


def setup_inputs(seed: int = 0) -> dict:
    key_list = jax.random.split(jax.random.key(seed), 18)
    return {
        "inputs": gaussian_with(key_list[0], (TOKENS, D), 1.0, 6.0, ((0, 32),), (0, 1, 32, 2.75)),
        "memory": gaussian_with(key_list[1], (ITEMS, MEM_CAP, D), 1.0, 6.0, ((0, 32),), (0, 2, 32, 2.75)),
        "mem_lengths": ragged_sizes(key_list[2], ITEMS, ITEMS * MEM_CAP * 5 // 8, MEM_CAP, 2).astype(jnp.int32),
        "self_qkv": normal_values(key_list[3], (3, D, D), D ** -0.5, 0.1875, ((1, 32),)),
        "self_out": normal_values(key_list[4], (D, D), (D // 8) ** -0.5, 0.5, ((0, 32),)),
        "self_bias": normal_values(key_list[5], (4, D), 0.5, 3.0, ((1, 32),)),
        "self_gain": jnp.clip(1.0 + 0.15 * jax.random.normal(key_list[6], (D,), jnp.float32), 0.25, 1.75).astype(jnp.bfloat16),
        "cross_qkv": normal_values(key_list[7], (3, D, D), D ** -0.5, 0.1875, ((1, 32),)),
        "cross_out": normal_values(key_list[8], (D, D), (D // 32) ** -0.5, 1.0, ((0, 32),)),
        "cross_bias": normal_values(key_list[9], (4, D), 0.5, 3.0, ((1, 32),)),
        "cross_gain": jnp.clip(1.0 + 0.15 * jax.random.normal(key_list[10], (D,), jnp.float32), 0.25, 1.75).astype(jnp.bfloat16),
        "ffn_in": normal_values(key_list[11], (D, FF), D ** -0.5, 0.1875, ((0, 32),)),
        "ffn_out": normal_values(key_list[12], (FF, D), FF ** -0.5, 0.09375, ((0, 32),)),
        "ffn_bias_in": normal_values(key_list[13], (FF,), 0.5, 3.0, ((0, 32),)),
        "ffn_bias_out": normal_values(key_list[14], (2, D), 0.5, 3.0, ((1, 32),)),
        "ffn_gain": jnp.clip(1.0 + 0.15 * jax.random.normal(key_list[15], (D,), jnp.float32), 0.25, 1.75).astype(jnp.bfloat16),
        "out_grad": normal_values(key_list[16], (TOKENS, D), 1.0, 6.0, ((0, 32),)),
    }


@jax.custom_vjp
def low(v):
    return lax.optimization_barrier(v.astype(jnp.bfloat16)).astype(jnp.float32)

@jax.custom_vjp
def low_back(v):
    return v

def low_keep(v):
    return (low(v), None)

def low_pass(kept, grad):
    return (grad,)

def back_keep(v):
    return (v, None)

def back_low(kept, grad):
    return (low(grad),)
low.defvjp(low_keep, low_pass)
low_back.defvjp(back_keep, back_low)
EPSILON = 1e-05
MASKED = -1e+30

def round_both(value):
    return low(low_back(value))

def product(left_rows, right_rows):
    return jnp.dot(left_rows, right_rows, precision=lax.Precision.HIGHEST, preferred_element_type=jnp.float32)

def layer_norm(hidden, gain_row, shift_row):
    average = lax.optimization_barrier(jnp.mean(hidden, axis=-1, keepdims=True))
    centred = hidden - average
    variance = lax.optimization_barrier(jnp.mean(centred * centred, axis=-1, keepdims=True))
    return centred * lax.rsqrt(variance + EPSILON) * gain_row + shift_row

def attend_item(queries, key_rows, values, allowed):
    scores = low_back(jnp.einsum('thd,shd->hts', queries, key_rows, precision=lax.Precision.HIGHEST))
    scores = jnp.where(allowed, scores, MASKED)
    chances = jax.nn.softmax(scores, axis=-1)
    context = jnp.einsum('hts,shd->thd', low(chances), values, precision=lax.Precision.HIGHEST)
    return round_both(context)

def self_block(packed):
    queries, key_rows, values = packed
    causal = jnp.arange(DEC, dtype=jnp.int32)[:, None] >= jnp.arange(DEC, dtype=jnp.int32)[None, :]
    return attend_item(queries, key_rows, values, causal)

def reference(inputs, memory, mem_lengths, self_qkv, self_out, self_bias, self_gain, cross_qkv, cross_out, cross_bias, cross_gain, ffn_in, ffn_out, ffn_bias_in, ffn_bias_out, ffn_gain, out_grad):
    scaling = HD ** (-0.5)
    head_split = (ITEMS, DEC, H, HD)

    def forward(x_in, mem_in, sqkv, sout, sbias, sgain, cqkv, cout, cbias, cgain, fin, fout, fbin, fbout, fgain):
        queries = round_both((product(x_in, sqkv[0]) + sbias[0]) * scaling)
        key_rows = round_both(product(x_in, sqkv[1]))
        values = round_both(product(x_in, sqkv[2]) + sbias[1])
        context = lax.map(jax.checkpoint(self_block), (queries.reshape(head_split), key_rows.reshape(head_split), values.reshape(head_split)))
        context = context.reshape(ITEMS * DEC, D)
        branch_one = low_back(product(context, sout) + sbias[2])
        first = layer_norm(x_in + branch_one, sgain, sbias[3])
        first_low = low(first)
        queries_two = round_both((product(first_low, cqkv[0]) + cbias[0]) * scaling)

        def cross_block(packed):
            item_q, item_mem, item_len = packed
            item_k = round_both(product(item_mem, cqkv[1])).reshape(MEM_CAP, H, HD)
            item_v = round_both(product(item_mem, cqkv[2]) + cbias[1]).reshape(MEM_CAP, H, HD)
            allowed = (jnp.arange(MEM_CAP, dtype=jnp.int32) < item_len)[None, :]
            return attend_item(item_q, item_k, item_v, allowed)
        context_two = lax.map(jax.checkpoint(cross_block), (queries_two.reshape(head_split), mem_in, mem_lengths))
        context_two = context_two.reshape(ITEMS * DEC, D)
        branch_two = low_back(product(context_two, cout) + cbias[2])
        second = layer_norm(first + branch_two, cgain, cbias[3])
        second_low = low(second)
        pre_gelu = low_back(product(second_low, fin) + fbin)
        hidden_low = low(jax.nn.gelu(pre_gelu, approximate=False))
        branch_three = low_back(product(hidden_low, fout) + fbout[0])
        return layer_norm(second + branch_three, fgain, fbout[1])
    floats = [arr.astype(jnp.float32) for arr in (inputs, memory, self_qkv, self_out, self_bias, self_gain, cross_qkv, cross_out, cross_bias, cross_gain, ffn_in, ffn_out, ffn_bias_in, ffn_bias_out, ffn_gain)]
    result, puller = jax.vjp(forward, *floats)
    grads = puller(out_grad.astype(jnp.float32))
    return (result.astype(jnp.bfloat16), grads[0], grads[1], grads[2], grads[3], grads[4], grads[5], grads[6], grads[7], grads[8], grads[9], grads[10], grads[11], grads[12], grads[13], grads[14])
```

```python
import jax
import jax.numpy as jnp
from jax import lax
from jax.sharding import PartitionSpec as P

HD = 64
EPSILON = 1e-05
MASKED = -1e30
AXES = ("wide", "narrow")
BF = jnp.bfloat16
F32 = jnp.float32


def project(left_rows, weight):
    return jnp.dot(left_rows, weight, preferred_element_type=F32)


def project_back(gradient, weight):
    return lax.dot_general(gradient, weight, (((1,), (1,)), ((), ())), preferred_element_type=F32)


def weight_grad(left_rows, gradient):
    return lax.dot_general(left_rows, gradient, (((0,), (0,)), ((), ())), preferred_element_type=F32)


def column_sums(gradient):
    return jnp.sum(gradient.astype(F32), axis=0)


def layer_norm(hidden, gain_row, shift_row):
    average = jnp.mean(hidden, axis=-1, keepdims=True)
    centred = hidden - average
    variance = jnp.mean(centred * centred, axis=-1, keepdims=True)
    return centred * lax.rsqrt(variance + EPSILON) * gain_row + shift_row


def gelu_exact(pre_gelu):
    return jax.nn.gelu(pre_gelu, approximate=False)


def attend(queries, key_rows, values, allowed):
    scores = jnp.einsum("thd,shd->hts", queries, key_rows, preferred_element_type=F32)
    scores = jnp.where(allowed, scores, MASKED)
    log_total = jax.nn.logsumexp(scores, axis=-1, keepdims=True)
    chances = jnp.exp(scores - log_total).astype(BF)
    context = jnp.einsum("hts,shd->thd", chances, values, preferred_element_type=F32)
    return (context.astype(BF), log_total)


def attend_back(queries, key_rows, values, log_total, d_context, allowed):
    scores = jnp.einsum("thd,shd->hts", queries, key_rows, preferred_element_type=F32)
    scores = jnp.where(allowed, scores, MASKED)
    chances = jnp.exp(scores - log_total)
    d_chances = jnp.einsum("thd,shd->hts", d_context, values, preferred_element_type=F32)
    d_scores = (
        chances * (d_chances - jnp.sum(d_chances * chances, axis=-1, keepdims=True))
    ).astype(BF)
    d_queries = jnp.einsum("hts,shd->thd", d_scores, key_rows, preferred_element_type=F32)
    d_keys = jnp.einsum("hts,thd->shd", d_scores, queries, preferred_element_type=F32)
    d_values = jnp.einsum("hts,thd->shd", chances.astype(BF), d_context, preferred_element_type=F32)
    return (d_queries.astype(BF), d_keys.astype(BF), d_values.astype(BF))


class Plan:
    def __init__(self):
        self.wide = lax.axis_size("wide")
        self.narrow = lax.axis_size("narrow")
        self.count = self.wide * self.narrow
        self.w = lax.axis_index("wide")
        self.z = lax.axis_index("narrow")
        self.me = self.w * self.narrow + self.z
        bits = self.wide.bit_length() - 1
        rest = [1 << b for b in range(1, bits)]
        half = len(rest) // 2
        self.xs, self.ys = rest[:half], rest[half:]
        self.zs = [1 << b for b in range(self.narrow.bit_length() - 1)]
        self.order = [r for r in range(self.wide) if r % 2 == 0] + [
            r for r in range(self.wide) if r % 2 == 1
        ]

    def swap(self, value, mask):
        return lax.ppermute(value, AXES, [(i, i ^ mask) for i in range(self.count)])

    def swap_wide(self, value, mask):
        return self.swap(value, mask * self.narrow)

    def bit(self, index, mask):
        return (index // mask) % 2

    def gather_z(self, part):
        k, rows, n = part.shape
        have = part.reshape(k, 1, rows, n)
        for mask in reversed(self.zs):
            other = self.swap(have, mask)
            mine_low = self.bit(self.z, mask) == 0
            low = jnp.where(mine_low, have, other)
            high = jnp.where(mine_low, other, have)
            have = jnp.stack([low, high], axis=2).reshape(k, -1, rows, n)
        return have.reshape(k, -1, n)

    def gather_wide(self, part, route):
        first, second = (self.xs, self.ys) if route == 0 else (self.ys, self.xs)
        pieces = {0: part}
        for mask in [*first, *second, 1]:
            pieces.update({r ^ mask: self.swap_wide(a, mask) for r, a in list(pieces.items())})
        return jnp.concatenate([pieces[r] for r in self.order], axis=1)

    def relative(self, rows):
        size = rows.shape[1] // self.wide
        return jnp.concatenate(
            [
                lax.dynamic_slice_in_dim(rows, (jnp.int32(r) ^ self.w) * size, size, axis=1)
                for r in self.order
            ],
            axis=1,
        )

    def natural(self, rows):
        size = rows.shape[1] // self.wide
        pieces = []
        for i in range(self.wide):
            r = jnp.int32(i) ^ self.w
            place = (r % 2) * (self.wide // 2) + r // 2
            pieces.append(lax.dynamic_slice_in_dim(rows, place * size, size, axis=1))
        return jnp.concatenate(pieces, axis=1)

    def scatter(self, left_rel, right, route):
        half = left_rel.shape[1] // 2
        keep = weight_grad(left_rel[:, :half], right).astype(BF)
        send = weight_grad(left_rel[:, half:], right).astype(BF)
        n = right.shape[1]
        blocks = self.wide // 2
        rows = half // blocks
        first, second = (self.xs, self.ys) if route == 0 else (self.ys, self.xs)
        acc = keep.astype(F32) + self.swap_wide(send, 1).astype(F32)
        bits = len(self.xs) + len(self.ys)
        acc = acc.reshape((2,) * bits + (rows, n))
        left = sorted((m for m in [*self.xs, *self.ys]), reverse=True)
        for mask in reversed([*first, *second]):
            axis = left.index(mask)
            left.pop(axis)
            keep = lax.index_in_dim(acc, 0, axis, keepdims=False)
            send = lax.index_in_dim(acc, 1, axis, keepdims=False).astype(BF)
            acc = keep + self.swap_wide(send, mask).astype(F32)
        own = rows // self.narrow
        acc = acc.reshape((2,) * len(self.zs) + (own, n))
        for mask in self.zs:
            axis = len(acc.shape) - 3
            place = self.bit(self.z, mask)
            keep = lax.dynamic_index_in_dim(acc, place, axis, keepdims=False)
            send = lax.dynamic_index_in_dim(acc, 1 - place, axis, keepdims=False).astype(BF)
            acc = keep + self.swap(send, mask).astype(F32)
        return acc

    def gather_small(self, vector):
        n = vector.shape[0]
        have = vector.reshape(1, n // 128, 128)
        masks = [1 << b for b in range(self.count.bit_length() - 1)]
        for mask in masks:
            other = self.swap(have, mask)
            low = self.bit(self.me, mask) == 0
            have = jnp.concatenate(
                [jnp.where(low, have, other), jnp.where(low, other, have)], axis=0
            )
        return have.reshape(self.count, n)

    def scatter_small(self, table):
        n = table.shape[1]
        have = table.reshape(self.count, n // 128, 128)
        masks = [1 << b for b in range(self.count.bit_length() - 1)]
        for mask in reversed(masks):
            size = mask
            place = self.bit(self.me, mask)
            keep = lax.dynamic_slice_in_dim(have, place * size, size, axis=0)
            send = lax.dynamic_slice_in_dim(have, (1 - place) * size, size, axis=0)
            have = keep + self.swap(send, mask)
        return have.reshape(n)


def pack(vectors, parts):
    rows = []
    for v in vectors:
        lead = v.reshape(-1, parts, v.shape[-1] // parts)
        rows.append(jnp.moveaxis(lead, 1, 0).reshape(parts, -1))
    table = jnp.concatenate(rows, axis=1)
    return jnp.pad(table, ((0, 0), (0, -table.shape[1] % 1024)))


def unpack(table, shapes):
    parts, at, found = table.shape[0], 0, []
    for shape in shapes:
        size = 1
        for d in shape:
            size *= d
        piece = table[:, at : at + size].reshape((parts,) + shape)
        piece = jnp.moveaxis(piece, 0, -2)
        found.append(piece.reshape(shape[:-1] + (parts * shape[-1],)))
        at += size
    return found


def local(
    inputs,
    memory,
    mem_lengths,
    self_qkv,
    self_out,
    self_bias,
    self_gain,
    cross_qkv,
    cross_out,
    cross_bias,
    cross_gain,
    ffn_in,
    ffn_out,
    ffn_bias_in,
    ffn_bias_out,
    ffn_gain,
    out_grad,
):
    plan = Plan()
    scaling = HD ** (-0.5)
    item_count, mem_slots, model_width = memory.shape
    row_count = inputs.shape[0]
    seq_len = row_count // item_count
    head_count = model_width // HD
    head_split = (item_count, seq_len, head_count, HD)
    mem_split = (item_count, mem_slots, head_count, HD)
    causal = lax.broadcasted_iota(jnp.int32, (seq_len, seq_len), 0) >= lax.broadcasted_iota(
        jnp.int32, (seq_len, seq_len), 1
    )
    key_slots = lax.broadcasted_iota(jnp.int32, (1, mem_slots), 1)
    inputs_f = inputs.astype(F32)

    vectors = [self_bias, self_gain, cross_bias, cross_gain, ffn_bias_in, ffn_bias_out, ffn_gain]
    small = pack([v for v in vectors], 1)[0]
    table = plan.gather_small(small)
    sbias, sgain, cbias, cgain, fbin, fbout, fgain = unpack(
        table.astype(F32), [v.shape for v in vectors]
    )
    self_z = plan.gather_z(jnp.concatenate([self_qkv, self_out[None]], axis=0))
    sqk = plan.gather_wide(self_z[:2], 0)
    svo = plan.gather_wide(self_z[2:], 1)
    cross_z = plan.gather_z(jnp.concatenate([cross_qkv, cross_out[None]], axis=0))
    cqk = plan.gather_wide(cross_z[:2], 0)
    cvo = plan.gather_wide(cross_z[2:], 1)
    fin = plan.gather_wide(plan.gather_z(ffn_in[None]), 0)[0]
    fout = plan.gather_wide(plan.gather_z(ffn_out[None]), 1)[0]

    x_rel = plan.relative(inputs)
    queries = (((project(x_rel, sqk[0]) + sbias[0]) * scaling).astype(BF)).reshape(head_split)
    key_rows = project(x_rel, sqk[1]).astype(BF).reshape(head_split)
    values = (project(x_rel, svo[0]) + sbias[1]).astype(BF).reshape(head_split)
    self_ctx, self_lse = jax.vmap(attend, in_axes=(0, 0, 0, None))(
        queries, key_rows, values, causal
    )
    self_rel = plan.relative(self_ctx.reshape(row_count, model_width))
    first_pre = inputs_f + (project(self_rel, svo[1]) + sbias[2])
    first = layer_norm(first_pre, sgain, sbias[3])
    first_rel = plan.relative(first.astype(BF))

    queries_two = (
        ((project(first_rel, cqk[0]) + cbias[0]) * scaling).astype(BF).reshape(head_split)
    )
    mem_rel = plan.relative(memory.reshape(item_count * mem_slots, model_width))
    mem_keys = project(mem_rel, cqk[1]).astype(BF).reshape(mem_split)
    mem_values = (project(mem_rel, cvo[0]) + cbias[1]).astype(BF).reshape(mem_split)

    def cross_item(packed):
        item_q, item_k, item_v, item_len = packed
        return attend(item_q, item_k, item_v, key_slots < item_len)

    cross_ctx, cross_lse = lax.map(cross_item, (queries_two, mem_keys, mem_values, mem_lengths))
    cross_rel = plan.relative(cross_ctx.reshape(row_count, model_width))
    second_pre = first + (project(cross_rel, cvo[1]) + cbias[2])
    second = layer_norm(second_pre, cgain, cbias[3])
    second_rel = plan.relative(second.astype(BF))

    pre_gelu = project(second_rel, fin) + fbin
    hidden, gelu_pull = jax.vjp(gelu_exact, pre_gelu)
    hidden_rel = plan.relative(hidden.astype(BF))
    third_pre = second + (project(hidden_rel, fout) + fbout[0])
    layer_out, norm_pull = jax.vjp(layer_norm, third_pre, fgain, fbout[1])

    d_third, g_fgain, g_fshift = norm_pull(out_grad.astype(F32))
    e_three = d_third.astype(BF)
    g_fout = plan.scatter(hidden_rel, e_three, 1)
    d_pre = gelu_pull(plan.natural(project_back(e_three, fout)))[0].astype(BF)
    g_fin = plan.scatter(second_rel, d_pre, 0)
    g_fbin = column_sums(d_pre)
    g_fbout = jnp.stack([column_sums(e_three), g_fshift])
    d_second = d_third + plan.natural(project_back(d_pre, fin))

    _, norm_pull_two = jax.vjp(layer_norm, second_pre, cgain, cbias[3])
    d_second_pre, g_cgain, g_cshift = norm_pull_two(d_second)
    e_two = d_second_pre.astype(BF)
    g_cout = plan.scatter(cross_rel, e_two, 1)
    d_cross_ctx = plan.natural(project_back(e_two, cvo[1]).astype(BF)).reshape(head_split)

    def cross_back(packed):
        item_q, item_k, item_v, item_lse, item_d, item_len = packed
        return attend_back(item_q, item_k, item_v, item_lse, item_d, key_slots < item_len)

    dq_two, dk_two, dv_two = lax.map(
        cross_back, (queries_two, mem_keys, mem_values, cross_lse, d_cross_ctx, mem_lengths)
    )
    dq_scaled = dq_two.reshape(row_count, model_width) * scaling
    dk_flat = dk_two.reshape(item_count * mem_slots, model_width)
    dv_flat = dv_two.reshape(item_count * mem_slots, model_width)
    g_cv = plan.scatter(mem_rel, dv_flat, 1)
    g_ck = plan.scatter(mem_rel, dk_flat, 0)
    g_cq = plan.scatter(first_rel, dq_scaled, 0)
    g_cbias = jnp.stack(
        [column_sums(dq_scaled), column_sums(dv_flat), column_sums(e_two), g_cshift]
    )
    memory_grad = plan.natural(
        project_back(dk_flat, cqk[1]) + project_back(dv_flat, cvo[0])
    ).reshape(item_count, mem_slots, model_width)
    d_first = d_second_pre + plan.natural(project_back(dq_scaled, cqk[0]))

    _, norm_pull_one = jax.vjp(layer_norm, first_pre, sgain, sbias[3])
    d_first_pre, g_sgain, g_sshift = norm_pull_one(d_first)
    e_one = d_first_pre.astype(BF)
    g_sout = plan.scatter(self_rel, e_one, 1)
    d_self_ctx = plan.natural(project_back(e_one, svo[1]).astype(BF)).reshape(head_split)
    dq_one, dk_one, dv_one = jax.vmap(attend_back, in_axes=(0, 0, 0, 0, 0, None))(
        queries, key_rows, values, self_lse, d_self_ctx, causal
    )
    dq_self = dq_one.reshape(row_count, model_width) * scaling
    dk_self = dk_one.reshape(row_count, model_width)
    dv_self = dv_one.reshape(row_count, model_width)
    g_sv = plan.scatter(x_rel, dv_self, 1)
    g_sk = plan.scatter(x_rel, dk_self, 0)
    g_sq = plan.scatter(x_rel, dq_self, 0)
    g_sbias = jnp.stack([column_sums(dq_self), column_sums(dv_self), column_sums(e_one), g_sshift])
    input_grad = d_first_pre + plan.natural(
        project_back(dq_self, sqk[0])
        + project_back(dk_self, sqk[1])
        + project_back(dv_self, svo[0])
    )

    grads = [g_sbias, g_sgain, g_cbias, g_cgain, g_fbin, g_fbout, g_fgain]
    sums = plan.scatter_small(pack(grads, plan.count))
    found = unpack(sums[None], [v.shape for v in vectors])
    return (
        layer_out.astype(BF),
        input_grad,
        memory_grad,
        jnp.stack([g_sq, g_sk, g_sv]),
        g_sout,
        found[0],
        found[1],
        jnp.stack([g_cq, g_ck, g_cv]),
        g_cout,
        found[2],
        found[3],
        g_fin,
        g_fout,
        found[4],
        found[5],
        found[6],
    )


def solution(mesh):
    both = ("wide", "narrow")
    placed = (
        P(both, None),
        P(both, None, None),
        P(both),
        P(None, both, None),
        P(both, None),
        P(None, both),
        P(both),
        P(None, both, None),
        P(both, None),
        P(None, both),
        P(both),
        P(both, None),
        P(both, None),
        P(both),
        P(None, both),
        P(both),
        P(both, None),
    )
    return jax.shard_map(
        local,
        mesh=mesh,
        in_specs=placed,
        out_specs=(
            P(both, None),
            P(both, None),
            P(both, None, None),
            P(None, both, None),
            P(both, None),
            P(None, both),
            P(both),
            P(None, both, None),
            P(both, None),
            P(None, both),
            P(both),
            P(both, None),
            P(both, None),
            P(both),
            P(None, both),
            P(both),
        ),
        check_vma=False,
    )
```

```python
import jax
import jax.numpy as jnp
from jax import lax
from jax.experimental import pallas as pl
from jax.experimental.pallas import tpu as pltpu
from jax.sharding import PartitionSpec as P

HD = 64
EPSILON = 1e-05
MASKED = -1e30
AXES = ("wide", "narrow")
BF = jnp.bfloat16
F32 = jnp.float32


def project(left_rows, weight):
    return jnp.dot(left_rows, weight, preferred_element_type=F32)


def project_back(gradient, weight):
    return lax.dot_general(gradient, weight, (((1,), (1,)), ((), ())), preferred_element_type=F32)


def weight_grad(left_rows, gradient):
    return lax.dot_general(left_rows, gradient, (((0,), (0,)), ((), ())), preferred_element_type=F32)


def column_sums(gradient):
    return jnp.sum(gradient.astype(F32), axis=0)


def layer_norm(hidden, gain_row, shift_row):
    average = jnp.mean(hidden, axis=-1, keepdims=True)
    centred = hidden - average
    variance = jnp.mean(centred * centred, axis=-1, keepdims=True)
    return centred * lax.rsqrt(variance + EPSILON) * gain_row + shift_row


def gelu_exact(pre_gelu):
    return jax.nn.gelu(pre_gelu, approximate=False)


def pair_stack(rows):
    lane = lax.broadcasted_iota(jnp.int32, rows.shape, 1)
    zero = jnp.zeros_like(rows)
    return jnp.concatenate(
        [jnp.where(lane < HD, rows, zero), jnp.where(lane >= HD, rows, zero)], axis=0
    )


def pair_merge(stacked):
    t = stacked.shape[0] // 2
    lane = lax.broadcasted_iota(jnp.int32, (t, 2 * HD), 1)
    return jnp.where(lane < HD, stacked[:t], stacked[t:])


def dot_nt(a, b):
    return lax.dot_general(a, b, (((1,), (1,)), ((), ())), preferred_element_type=F32)


def dot_tn(a, b):
    return lax.dot_general(a, b, (((0,), (0,)), ((), ())), preferred_element_type=F32)


def dot_nn(a, b):
    return lax.dot_general(a, b, (((1,), (0,)), ((), ())), preferred_element_type=F32)


def masked_scores(k, qs, length):
    scores = dot_nt(k, qs)
    slot = lax.broadcasted_iota(jnp.int32, scores.shape, 0)
    if length is None:
        seen = lax.broadcasted_iota(jnp.int32, scores.shape, 1) % (scores.shape[1] // 2)
        return jnp.where(slot <= seen, scores, MASKED)
    return jnp.where(slot < length, scores, MASKED)


def attend_pair(q, k, v, length):
    scores = masked_scores(k, pair_stack(q), length)
    top = jnp.max(scores, axis=0, keepdims=True)
    weights = jnp.exp(scores - top)
    total = jnp.sum(weights, axis=0, keepdims=True)
    chances = (weights * (1.0 / total)).astype(BF)
    return pair_merge(dot_tn(chances, v)).astype(BF), top + jnp.log(total)


def attend_pair_back(q, k, v, lse, d_out, length):
    qs, ds_out = pair_stack(q), pair_stack(d_out)
    chances = jnp.exp(masked_scores(k, qs, length) - lse)
    d_chances = dot_nt(v, ds_out)
    row = jnp.sum(d_chances * chances, axis=0, keepdims=True)
    d_scores = (chances * (d_chances - row)).astype(BF)
    d_q = pair_merge(dot_tn(d_scores, k)).astype(BF)
    d_k = dot_nn(d_scores, qs).astype(BF)
    d_v = dot_nn(chances.astype(BF), ds_out).astype(BF)
    return d_q, d_k, d_v


PAIR = 2 * HD


def cross_kernel(place, lengths, q, k, v, out, lse):
    out[...], lse[0, 0] = attend_pair(q[...], k[...], v[...], lengths[pl.program_id(0)])


def cross_back_kernel(place, lengths, q, k, v, lse, d_out, d_q, d_k, d_v):
    d_q[...], d_k[...], d_v[...] = attend_pair_back(
        q[...], k[...], v[...], lse[0, 0], d_out[...], lengths[pl.program_id(0)]
    )
    d_q[...] = d_q[...] * jnp.asarray(HD**-0.5, BF)


def cross_attend(q, k, v, lengths, place):
    items = lengths.shape[0]
    t, s, pairs = q.shape[0] // items, k.shape[0] // items, q.shape[1] // PAIR
    rows = pl.BlockSpec((t, PAIR), lambda b, j, *_: (b, j))
    slots = pl.BlockSpec((s, PAIR), lambda b, j, *_: (b, j))
    placed = pl.BlockSpec((t, PAIR), lambda b, j, place, lengths: (b, place[j]))
    lse = pl.BlockSpec((1, 1, 1, 2 * t), lambda b, j, *_: (b, j, 0, 0))
    return pl.pallas_call(
        cross_kernel,
        grid_spec=pltpu.PrefetchScalarGridSpec(
            num_scalar_prefetch=2,
            grid=(items, pairs),
            in_specs=[rows, slots, slots],
            out_specs=[placed, lse],
        ),
        out_shape=[
            jax.ShapeDtypeStruct(q.shape, BF),
            jax.ShapeDtypeStruct((items, pairs, 1, 2 * t), F32),
        ],
        name="cross_attend",
    )(place, lengths, q, k, v)


def cross_attend_back(q, k, v, lse, d_out, lengths, place):
    items = lengths.shape[0]
    t, s, pairs = q.shape[0] // items, k.shape[0] // items, q.shape[1] // PAIR
    rows = pl.BlockSpec((t, PAIR), lambda b, j, *_: (b, j))
    slots = pl.BlockSpec((s, PAIR), lambda b, j, *_: (b, j))
    placed = pl.BlockSpec((t, PAIR), lambda b, j, place, lengths: (b, place[j]))
    lse_spec = pl.BlockSpec((1, 1, 1, 2 * t), lambda b, j, *_: (b, j, 0, 0))
    return pl.pallas_call(
        cross_back_kernel,
        grid_spec=pltpu.PrefetchScalarGridSpec(
            num_scalar_prefetch=2,
            grid=(items, pairs),
            in_specs=[rows, slots, slots, lse_spec, placed],
            out_specs=[rows, slots, slots],
        ),
        out_shape=[
            jax.ShapeDtypeStruct(q.shape, BF),
            jax.ShapeDtypeStruct(k.shape, BF),
            jax.ShapeDtypeStruct(k.shape, BF),
        ],
        name="cross_attend_back",
    )(place, lengths, q, k, v, lse, d_out)


def lanes(ref, at):
    return ref[:, pl.ds(pl.multiple_of(at * PAIR, PAIR), PAIR)]


def self_kernel(place, q, k, v, out, lse):
    for j in range(q.shape[1] // PAIR):
        cut = slice(j * PAIR, (j + 1) * PAIR)
        found, lse[0, j] = attend_pair(q[:, cut], k[:, cut], v[:, cut], None)
        out[:, pl.ds(pl.multiple_of(place[j] * PAIR, PAIR), PAIR)] = found


def self_back_kernel(place, q, k, v, lse, d_out, d_q, d_k, d_v):
    for j in range(q.shape[1] // PAIR):
        cut = slice(j * PAIR, (j + 1) * PAIR)
        found = attend_pair_back(
            q[:, cut], k[:, cut], v[:, cut], lse[0, j], lanes(d_out, place[j]), None
        )
        d_q[:, cut] = found[0] * jnp.asarray(HD**-0.5, BF)
        d_k[:, cut] = found[1]
        d_v[:, cut] = found[2]


def self_attend(q, k, v, items, place):
    t, width = q.shape[0] // items, q.shape[1]
    rows = pl.BlockSpec((t, width), lambda b, *_: (b, 0))
    lse = pl.BlockSpec((1, width // PAIR, 1, 2 * t), lambda b, *_: (b, 0, 0, 0))
    return pl.pallas_call(
        self_kernel,
        grid_spec=pltpu.PrefetchScalarGridSpec(
            num_scalar_prefetch=1,
            grid=(items,),
            in_specs=[rows] * 3,
            out_specs=[rows, lse],
        ),
        out_shape=[
            jax.ShapeDtypeStruct(q.shape, BF),
            jax.ShapeDtypeStruct((items, width // PAIR, 1, 2 * t), F32),
        ],
        name="self_attend",
    )(place, q, k, v)


def self_attend_back(q, k, v, lse, d_out, items, place):
    t, width = q.shape[0] // items, q.shape[1]
    rows = pl.BlockSpec((t, width), lambda b, *_: (b, 0))
    lse_spec = pl.BlockSpec((1, width // PAIR, 1, 2 * t), lambda b, *_: (b, 0, 0, 0))
    return pl.pallas_call(
        self_back_kernel,
        grid_spec=pltpu.PrefetchScalarGridSpec(
            num_scalar_prefetch=1,
            grid=(items,),
            in_specs=[rows] * 3 + [lse_spec, rows],
            out_specs=[rows] * 3,
        ),
        out_shape=[jax.ShapeDtypeStruct(q.shape, BF)] * 3,
        name="self_attend_back",
    )(place, q, k, v, lse, d_out)


def back_kernel(place, *refs):
    count = (len(refs) - 1) // 2
    out = refs[-1]
    total = dot_nt(refs[0][...], refs[count][...])
    for i in range(1, count):
        total = total + dot_nt(refs[i][...], refs[count + i][...])
    size = total.shape[1] // place.shape[0]
    for i in range(place.shape[0]):
        at = pl.ds(pl.multiple_of(place[i] * size, 128), size)
        out[:, at] = total[:, i * size : (i + 1) * size]


def back_natural(lefts, weights, place, block):
    m, k = lefts[0].shape
    n = weights[0].shape[0]
    whole = pl.BlockSpec((n, k), lambda i, *_: (0, 0), pipeline_mode=pl.Buffered(1))
    return pl.pallas_call(
        back_kernel,
        grid_spec=pltpu.PrefetchScalarGridSpec(
            num_scalar_prefetch=1,
            grid=(m // block,),
            in_specs=[pl.BlockSpec((block, k), lambda i, *_: (i, 0))] * len(lefts)
            + [whole] * len(weights),
            out_specs=pl.BlockSpec((block, n), lambda i, *_: (i, 0)),
        ),
        out_shape=jax.ShapeDtypeStruct((m, n), F32),
        name="back_natural",
    )(place, *lefts, *weights)


class Plan:
    def __init__(self):
        self.wide = lax.axis_size("wide")
        self.narrow = lax.axis_size("narrow")
        self.count = self.wide * self.narrow
        self.w = lax.axis_index("wide")
        self.z = lax.axis_index("narrow")
        self.me = self.w * self.narrow + self.z
        bits = self.wide.bit_length() - 1
        rest = [1 << b for b in range(1, bits)]
        half = len(rest) // 2
        self.xs, self.ys = rest[:half], rest[half:]
        self.zs = [1 << b for b in range(self.narrow.bit_length() - 1)]
        self.order = [r for r in range(self.wide) if r % 2 == 0] + [
            r for r in range(self.wide) if r % 2 == 1
        ]

    def swap(self, value, mask):
        return lax.ppermute(value, AXES, [(i, i ^ mask) for i in range(self.count)])

    def swap_wide(self, value, mask):
        return self.swap(value, mask * self.narrow)

    def bit(self, index, mask):
        return (index // mask) % 2

    def gather_z(self, part):
        k, rows, n = part.shape
        have = part.reshape(k, 1, rows, n)
        for mask in reversed(self.zs):
            other = self.swap(have, mask)
            mine_low = self.bit(self.z, mask) == 0
            low = jnp.where(mine_low, have, other)
            high = jnp.where(mine_low, other, have)
            have = jnp.stack([low, high], axis=2).reshape(k, -1, rows, n)
        return have.reshape(k, -1, n)

    def gather_wide(self, part, route):
        first, second = (self.xs, self.ys) if route == 0 else (self.ys, self.xs)
        pieces = {0: part}
        for mask in [*first, *second, 1]:
            pieces.update({r ^ mask: self.swap_wide(a, mask) for r, a in list(pieces.items())})
        return jnp.concatenate([pieces[r] for r in self.order], axis=1)

    def relative(self, rows):
        size = rows.shape[1] // self.wide
        return jnp.concatenate(
            [
                lax.dynamic_slice_in_dim(rows, (jnp.int32(r) ^ self.w) * size, size, axis=1)
                for r in self.order
            ],
            axis=1,
        )

    def natural(self, rows):
        size = rows.shape[1] // self.wide
        pieces = []
        for i in range(self.wide):
            r = jnp.int32(i) ^ self.w
            place = (r % 2) * (self.wide // 2) + r // 2
            pieces.append(lax.dynamic_slice_in_dim(rows, place * size, size, axis=1))
        return jnp.concatenate(pieces, axis=1)

    def places(self):
        r = lax.iota(jnp.int32, self.wide) ^ self.w
        return (r % 2) * (self.wide // 2) + r // 2

    def blocks(self):
        return jnp.array(self.order, jnp.int32) ^ self.w

    def scatter(self, left_rel, right, route):
        half = left_rel.shape[1] // 2
        keep = weight_grad(left_rel[:, :half], right).astype(BF)
        send = weight_grad(left_rel[:, half:], right).astype(BF)
        n = right.shape[1]
        blocks = self.wide // 2
        rows = half // blocks
        first, second = (self.xs, self.ys) if route == 0 else (self.ys, self.xs)
        acc = keep.astype(F32) + self.swap_wide(send, 1).astype(F32)
        bits = len(self.xs) + len(self.ys)
        acc = acc.reshape((2,) * bits + (rows, n))
        left = sorted((m for m in [*self.xs, *self.ys]), reverse=True)
        for mask in reversed([*first, *second]):
            axis = left.index(mask)
            left.pop(axis)
            keep = lax.index_in_dim(acc, 0, axis, keepdims=False)
            send = lax.index_in_dim(acc, 1, axis, keepdims=False).astype(BF)
            acc = keep + self.swap_wide(send, mask).astype(F32)
        own = rows // self.narrow
        acc = acc.reshape((2,) * len(self.zs) + (own, n))
        for mask in self.zs:
            axis = len(acc.shape) - 3
            place = self.bit(self.z, mask)
            keep = lax.dynamic_index_in_dim(acc, place, axis, keepdims=False)
            send = lax.dynamic_index_in_dim(acc, 1 - place, axis, keepdims=False).astype(BF)
            acc = keep + self.swap(send, mask).astype(F32)
        return acc

    def gather_small(self, vector):
        n = vector.shape[0]
        have = vector.reshape(1, n // 128, 128)
        masks = [1 << b for b in range(self.count.bit_length() - 1)]
        for mask in masks:
            other = self.swap(have, mask)
            low = self.bit(self.me, mask) == 0
            have = jnp.concatenate(
                [jnp.where(low, have, other), jnp.where(low, other, have)], axis=0
            )
        return have.reshape(self.count, n)

    def scatter_small(self, table):
        n = table.shape[1]
        have = table.reshape(self.count, n // 128, 128)
        masks = [1 << b for b in range(self.count.bit_length() - 1)]
        for mask in reversed(masks):
            size = mask
            place = self.bit(self.me, mask)
            keep = lax.dynamic_slice_in_dim(have, place * size, size, axis=0)
            send = lax.dynamic_slice_in_dim(have, (1 - place) * size, size, axis=0)
            have = keep + self.swap(send, mask)
        return have.reshape(n)


def pack(vectors, parts):
    rows = []
    for v in vectors:
        lead = v.reshape(-1, parts, v.shape[-1] // parts)
        rows.append(jnp.moveaxis(lead, 1, 0).reshape(parts, -1))
    table = jnp.concatenate(rows, axis=1)
    return jnp.pad(table, ((0, 0), (0, -table.shape[1] % 1024)))


def unpack(table, shapes):
    parts, at, found = table.shape[0], 0, []
    for shape in shapes:
        size = 1
        for d in shape:
            size *= d
        piece = table[:, at : at + size].reshape((parts,) + shape)
        piece = jnp.moveaxis(piece, 0, -2)
        found.append(piece.reshape(shape[:-1] + (parts * shape[-1],)))
        at += size
    return found


def local(
    inputs,
    memory,
    mem_lengths,
    self_qkv,
    self_out,
    self_bias,
    self_gain,
    cross_qkv,
    cross_out,
    cross_bias,
    cross_gain,
    ffn_in,
    ffn_out,
    ffn_bias_in,
    ffn_bias_out,
    ffn_gain,
    out_grad,
):
    plan = Plan()
    scaling = HD ** (-0.5)
    item_count, mem_slots, model_width = memory.shape
    row_count = inputs.shape[0]
    pairs = model_width // PAIR
    paired = plan.wide == pairs
    place = plan.places() if paired else lax.iota(jnp.int32, pairs)

    def to_relative(context):
        return context if paired else plan.relative(context)

    def from_relative(context):
        return context if paired else plan.natural(context)

    def back(lefts, weights, block):
        if (model_width // plan.wide) % 128 == 0:
            return back_natural(lefts, weights, plan.blocks(), block)
        total = project_back(lefts[0], weights[0])
        for left, weight in zip(lefts[1:], weights[1:]):
            total = total + project_back(left, weight)
        return plan.natural(total)

    inputs_f = inputs.astype(F32)

    vectors = [self_bias, self_gain, cross_bias, cross_gain, ffn_bias_in, ffn_bias_out, ffn_gain]
    small = pack([v for v in vectors], 1)[0]
    table = plan.gather_small(small)
    sbias, sgain, cbias, cgain, fbin, fbout, fgain = unpack(
        table.astype(F32), [v.shape for v in vectors]
    )
    self_z = plan.gather_z(jnp.concatenate([self_qkv, self_out[None]], axis=0))
    sqk = plan.gather_wide(self_z[:2], 0)
    svo = plan.gather_wide(self_z[2:], 1)
    cross_z = plan.gather_z(jnp.concatenate([cross_qkv, cross_out[None]], axis=0))
    cqk = plan.gather_wide(cross_z[:2], 0)
    cvo = plan.gather_wide(cross_z[2:], 1)
    fin = plan.gather_wide(plan.gather_z(ffn_in[None]), 0)[0]
    fout = plan.gather_wide(plan.gather_z(ffn_out[None]), 1)[0]

    x_rel = plan.relative(inputs)
    queries = ((project(x_rel, sqk[0]) + sbias[0]) * scaling).astype(BF)
    key_rows = project(x_rel, sqk[1]).astype(BF)
    values = (project(x_rel, svo[0]) + sbias[1]).astype(BF)
    self_ctx, self_lse = self_attend(queries, key_rows, values, item_count, place)
    self_rel = to_relative(self_ctx)
    first_pre = inputs_f + (project(self_rel, svo[1]) + sbias[2])
    first = layer_norm(first_pre, sgain, sbias[3])
    first_rel = plan.relative(first.astype(BF))

    queries_two = ((project(first_rel, cqk[0]) + cbias[0]) * scaling).astype(BF)
    mem_rel = plan.relative(memory.reshape(item_count * mem_slots, model_width))
    mem_keys = project(mem_rel, cqk[1]).astype(BF)
    mem_values = (project(mem_rel, cvo[0]) + cbias[1]).astype(BF)
    cross_ctx, cross_lse = cross_attend(queries_two, mem_keys, mem_values, mem_lengths, place)
    cross_rel = to_relative(cross_ctx)
    second_pre = first + (project(cross_rel, cvo[1]) + cbias[2])
    second = layer_norm(second_pre, cgain, cbias[3])
    second_rel = plan.relative(second.astype(BF))

    pre_gelu = project(second_rel, fin) + fbin
    hidden, gelu_pull = jax.vjp(gelu_exact, pre_gelu)
    hidden_rel = plan.relative(hidden.astype(BF))
    third_pre = second + (project(hidden_rel, fout) + fbout[0])
    layer_out, norm_pull = jax.vjp(layer_norm, third_pre, fgain, fbout[1])

    d_third, g_fgain, g_fshift = norm_pull(out_grad.astype(F32))
    e_three = d_third.astype(BF)
    g_fout = plan.scatter(hidden_rel, e_three, 1)
    d_pre = gelu_pull(plan.natural(project_back(e_three, fout)))[0].astype(BF)
    g_fin = plan.scatter(second_rel, d_pre, 0)
    g_fbin = column_sums(d_pre)
    g_fbout = jnp.stack([column_sums(e_three), g_fshift])
    d_second = d_third + back([d_pre], [fin], row_count)

    _, norm_pull_two = jax.vjp(layer_norm, second_pre, cgain, cbias[3])
    d_second_pre, g_cgain, g_cshift = norm_pull_two(d_second)
    e_two = d_second_pre.astype(BF)
    g_cout = plan.scatter(cross_rel, e_two, 1)
    d_cross_ctx = from_relative(project_back(e_two, cvo[1]).astype(BF))
    dq_scaled, dk_flat, dv_flat = cross_attend_back(
        queries_two, mem_keys, mem_values, cross_lse, d_cross_ctx, mem_lengths, place
    )
    g_cv = plan.scatter(mem_rel, dv_flat, 1)
    g_ck = plan.scatter(mem_rel, dk_flat, 0)
    g_cq = plan.scatter(first_rel, dq_scaled, 0)
    g_cbias = jnp.stack(
        [column_sums(dq_scaled), column_sums(dv_flat), column_sums(e_two), g_cshift]
    )
    memory_grad = back([dk_flat, dv_flat], [cqk[1], cvo[0]], 512).reshape(memory.shape)
    d_first = d_second_pre + back([dq_scaled], [cqk[0]], row_count)

    _, norm_pull_one = jax.vjp(layer_norm, first_pre, sgain, sbias[3])
    d_first_pre, g_sgain, g_sshift = norm_pull_one(d_first)
    e_one = d_first_pre.astype(BF)
    g_sout = plan.scatter(self_rel, e_one, 1)
    d_self_ctx = from_relative(project_back(e_one, svo[1]).astype(BF))
    dq_self, dk_self, dv_self = self_attend_back(
        queries, key_rows, values, self_lse, d_self_ctx, item_count, place
    )
    g_sv = plan.scatter(x_rel, dv_self, 1)
    g_sk = plan.scatter(x_rel, dk_self, 0)
    g_sq = plan.scatter(x_rel, dq_self, 0)
    g_sbias = jnp.stack([column_sums(dq_self), column_sums(dv_self), column_sums(e_one), g_sshift])
    input_grad = d_first_pre + back(
        [dq_self, dk_self, dv_self], [sqk[0], sqk[1], svo[0]], row_count
    )

    grads = [g_sbias, g_sgain, g_cbias, g_cgain, g_fbin, g_fbout, g_fgain]
    sums = plan.scatter_small(pack(grads, plan.count))
    found = unpack(sums[None], [v.shape for v in vectors])
    return (
        layer_out.astype(BF),
        input_grad,
        memory_grad,
        jnp.stack([g_sq, g_sk, g_sv]),
        g_sout,
        found[0],
        found[1],
        jnp.stack([g_cq, g_ck, g_cv]),
        g_cout,
        found[2],
        found[3],
        g_fin,
        g_fout,
        found[4],
        found[5],
        found[6],
    )


def solution(mesh):
    both = ("wide", "narrow")
    placed = (
        P(both, None),
        P(both, None, None),
        P(both),
        P(None, both, None),
        P(both, None),
        P(None, both),
        P(both),
        P(None, both, None),
        P(both, None),
        P(None, both),
        P(both),
        P(both, None),
        P(both, None),
        P(both),
        P(None, both),
        P(both),
        P(both, None),
    )
    return jax.shard_map(
        local,
        mesh=mesh,
        in_specs=placed,
        out_specs=(
            P(both, None),
            P(both, None),
            P(both, None, None),
            P(None, both, None),
            P(both, None),
            P(None, both),
            P(both),
            P(None, both, None),
            P(both, None),
            P(None, both),
            P(both),
            P(both, None),
            P(both, None),
            P(both),
            P(None, both),
            P(both),
        ),
        check_vma=False,
    )
```

```python
import functools

import jax
import jax.numpy as jnp
from jax import lax
from jax.experimental import pallas as pl
from jax.experimental.pallas import tpu as pltpu
from jax.sharding import PartitionSpec as P

HD = 64
EPSILON = 1e-05
MASKED = -1e30
AXES = ("wide", "narrow")
BF = jnp.bfloat16
F32 = jnp.float32


def project(left_rows, weight):
    return jnp.dot(left_rows, weight, preferred_element_type=F32)


def project_back(gradient, weight):
    return lax.dot_general(gradient, weight, (((1,), (1,)), ((), ())), preferred_element_type=F32)


def weight_grad(left_rows, gradient):
    return lax.dot_general(left_rows, gradient, (((0,), (0,)), ((), ())), preferred_element_type=F32)


def column_sums(gradient):
    return jnp.sum(gradient.astype(F32), axis=0)


def layer_norm(hidden, gain_row, shift_row):
    average = jnp.mean(hidden, axis=-1, keepdims=True)
    centred = hidden - average
    variance = jnp.mean(centred * centred, axis=-1, keepdims=True)
    return centred * lax.rsqrt(variance + EPSILON) * gain_row + shift_row


def gelu_exact(pre_gelu):
    return jax.nn.gelu(pre_gelu, approximate=False)


def pair_stack(rows):
    lane = lax.broadcasted_iota(jnp.int32, rows.shape, 1)
    zero = jnp.zeros_like(rows)
    return jnp.concatenate(
        [jnp.where(lane < HD, rows, zero), jnp.where(lane >= HD, rows, zero)], axis=0
    )


def pair_merge(stacked):
    t = stacked.shape[0] // 2
    lane = lax.broadcasted_iota(jnp.int32, (t, 2 * HD), 1)
    return jnp.where(lane < HD, stacked[:t], stacked[t:])


def dot_nt(a, b):
    return lax.dot_general(a, b, (((1,), (1,)), ((), ())), preferred_element_type=F32)


def dot_tn(a, b):
    return lax.dot_general(a, b, (((0,), (0,)), ((), ())), preferred_element_type=F32)


def dot_nn(a, b):
    return lax.dot_general(a, b, (((1,), (0,)), ((), ())), preferred_element_type=F32)


def masked_scores(k, qs, length):
    scores = dot_nt(k, qs)
    slot = lax.broadcasted_iota(jnp.int32, scores.shape, 0)
    if length is None:
        seen = lax.broadcasted_iota(jnp.int32, scores.shape, 1) % (scores.shape[1] // 2)
        return jnp.where(slot <= seen, scores, MASKED)
    return jnp.where(slot < length, scores, MASKED)


def attend_pair(q, k, v, length):
    scores = masked_scores(k, pair_stack(q), length)
    top = jnp.max(scores, axis=0, keepdims=True)
    weights = jnp.exp(scores - top)
    total = jnp.sum(weights, axis=0, keepdims=True)
    chances = (weights * (1.0 / total)).astype(BF)
    return pair_merge(dot_tn(chances, v)).astype(BF), top + jnp.log(total)


def attend_pair_back(q, k, v, lse, d_out, length):
    qs, ds_out = pair_stack(q), pair_stack(d_out)
    chances = jnp.exp(masked_scores(k, qs, length) - lse)
    d_chances = dot_nt(v, ds_out)
    row = jnp.sum(d_chances * chances, axis=0, keepdims=True)
    d_scores = (chances * (d_chances - row)).astype(BF)
    d_q = pair_merge(dot_tn(d_scores, k)).astype(BF)
    d_k = dot_nn(d_scores, qs).astype(BF)
    d_v = dot_nn(chances.astype(BF), ds_out).astype(BF)
    return d_q, d_k, d_v


PAIR = 2 * HD


def cross_kernel(place, length, q, k, v, *refs):
    out, lse = refs[-2:]
    out[...], lse[0, 0] = attend_pair(q[...], k[...], v[...], length[0])


def cross_back_kernel(place, length, q, k, v, lse, d_out, *refs):
    d_q, d_k, d_v = refs[-3:]
    d_q[...], d_k[...], d_v[...] = attend_pair_back(
        q[...], k[...], v[...], lse[0, 0], d_out[...], length[0]
    )
    d_q[...] = d_q[...] * jnp.asarray(HD**-0.5, BF)


def cross_call(kernel, q, k, lengths, place, item, values, in_specs, out_specs, out_shape, so_far):
    return pl.pallas_call(
        kernel,
        grid_spec=pltpu.PrefetchScalarGridSpec(
            num_scalar_prefetch=2,
            grid=(q.shape[1] // PAIR,),
            in_specs=in_specs + [pl.BlockSpec(memory_space=pl.ANY)] * len(so_far),
            out_specs=out_specs,
        ),
        out_shape=out_shape,
        input_output_aliases={2 + len(values) + i: i for i in range(len(so_far))},
        name="cross_attend",
    )(place, lax.slice_in_dim(lengths, item, item + 1), *values, *so_far)


def cross_specs(q, k, items, item):
    t, s = q.shape[0] // items, k.shape[0] // items
    rows = pl.BlockSpec((t, PAIR), lambda j, *_: (item, j))
    slots = pl.BlockSpec((s, PAIR), lambda j, *_: (item, j))
    placed = pl.BlockSpec((t, PAIR), lambda j, place, length: (item, place[j]))
    lse = pl.BlockSpec((1, 1, 1, 2 * t), lambda j, *_: (item, j, 0, 0))
    return rows, slots, placed, lse


def cross_attend(q, k, v, lengths, place, item, so_far):
    items = lengths.shape[0]
    rows, slots, placed, lse = cross_specs(q, k, items, item)
    out_shape = [
        jax.ShapeDtypeStruct(q.shape, BF),
        jax.ShapeDtypeStruct((items, q.shape[1] // PAIR, 1, 2 * q.shape[0] // items), F32),
    ]
    return cross_call(
        cross_kernel, q, k, lengths, place, item, (q, k, v),
        [rows, slots, slots], [placed, lse], out_shape, so_far,
    )


def cross_attend_back(q, k, v, lse, d_out, lengths, place, item, so_far):
    rows, slots, placed, lse_spec = cross_specs(q, k, lengths.shape[0], item)
    out_shape = [jax.ShapeDtypeStruct(a.shape, BF) for a in (q, k, k)]
    return cross_call(
        cross_back_kernel, q, k, lengths, place, item, (q, k, v, lse, d_out),
        [rows, slots, slots, lse_spec, placed], [rows, slots, slots], out_shape, so_far,
    )


def lanes(ref, at):
    return ref[:, pl.ds(pl.multiple_of(at * PAIR, PAIR), PAIR)]


def self_kernel(place, q, k, v, out, lse):
    for j in range(q.shape[1] // PAIR):
        cut = slice(j * PAIR, (j + 1) * PAIR)
        found, lse[0, j] = attend_pair(q[:, cut], k[:, cut], v[:, cut], None)
        out[:, pl.ds(pl.multiple_of(place[j] * PAIR, PAIR), PAIR)] = found


def self_back_kernel(place, q, k, v, lse, d_out, d_q, d_k, d_v):
    for j in range(q.shape[1] // PAIR):
        cut = slice(j * PAIR, (j + 1) * PAIR)
        found = attend_pair_back(
            q[:, cut], k[:, cut], v[:, cut], lse[0, j], lanes(d_out, place[j]), None
        )
        d_q[:, cut] = found[0] * jnp.asarray(HD**-0.5, BF)
        d_k[:, cut] = found[1]
        d_v[:, cut] = found[2]


def self_attend(qkv, items, place):
    _, rows, width = qkv.shape
    t = rows // items

    def part(i):
        return pl.BlockSpec((None, t, width), lambda b, *_: (i, b, 0))

    lse = pl.BlockSpec((1, width // PAIR, 1, 2 * t), lambda b, *_: (b, 0, 0, 0))
    return pl.pallas_call(
        self_kernel,
        grid_spec=pltpu.PrefetchScalarGridSpec(
            num_scalar_prefetch=1,
            grid=(items,),
            in_specs=[part(0), part(1), part(2)],
            out_specs=[pl.BlockSpec((t, width), lambda b, *_: (b, 0)), lse],
        ),
        out_shape=[
            jax.ShapeDtypeStruct((rows, width), BF),
            jax.ShapeDtypeStruct((items, width // PAIR, 1, 2 * t), F32),
        ],
        name="self_attend",
    )(place, qkv, qkv, qkv)


def self_attend_back(qkv, lse, d_out, items, place):
    _, m, width = qkv.shape
    t = m // items

    def part(i):
        return pl.BlockSpec((None, t, width), lambda b, *_: (i, b, 0))

    rows = pl.BlockSpec((t, width), lambda b, *_: (b, 0))
    lse_spec = pl.BlockSpec((1, width // PAIR, 1, 2 * t), lambda b, *_: (b, 0, 0, 0))
    return pl.pallas_call(
        self_back_kernel,
        grid_spec=pltpu.PrefetchScalarGridSpec(
            num_scalar_prefetch=1,
            grid=(items,),
            in_specs=[part(0), part(1), part(2), lse_spec, rows],
            out_specs=[rows] * 3,
        ),
        out_shape=[jax.ShapeDtypeStruct((m, width), BF)] * 3,
        name="self_attend_back",
    )(place, qkv, qkv, qkv, lse, d_out)


def stacked(array, i, **kw):
    return pl.BlockSpec((None,) + array.shape[1:], lambda *_: (i, 0, 0), **kw)


def project_kernel(scales, x0, x1, near, far, bias, out):
    total = dot_nn(x0[...], near[...]) + dot_nn(x1[...], far[...]) + bias[...]
    j = pl.program_id(0)
    scale = scales[0]
    for i in range(1, len(scales)):
        scale = jnp.where(j == i, scales[i], scale)
    out[...] = (total * scale).astype(out.dtype)


def stack_project(rows, weights, first, bias, scales, dtype):
    near, far = weights
    m, h = rows[0].shape
    n = near.shape[2]
    count = len(scales)
    whole = pl.BlockSpec((m, h), lambda j: (0, 0))
    weight = pl.BlockSpec((None, h, n), lambda j: (first + j, 0, 0))
    return pl.pallas_call(
        functools.partial(project_kernel, scales),
        grid=(count,),
        in_specs=[whole, whole, weight, weight, pl.BlockSpec((None, 1, n), lambda j: (j, 0, 0))],
        out_specs=pl.BlockSpec((None, m, n), lambda j: (j, 0, 0)),
        out_shape=jax.ShapeDtypeStruct((count, m, n), dtype),
        name="stack_project",
    )(*rows, near, far, bias)


def grads_kernel(products, *refs):
    ins, (keep, send) = refs[:-2], refs[-2:]
    for i, (left, right, start) in enumerate(products):

        @pl.when(pl.program_id(0) == i)
        def _():
            to = ins[right][:, start : start + keep.shape[1]]
            keep[...] = dot_tn(ins[left][...], to).astype(BF)
            send[...] = dot_tn(ins[left + 1][...], to).astype(BF)


def stack_grads(lefts, rights, products):
    arrays = [half for left in lefts for half in left] + list(rights)
    n = products[0][3]
    r = lefts[0][0].shape[1]
    table = [(2 * left, 2 * len(lefts) + right, start) for left, right, start, _ in products]
    out = pl.BlockSpec((None, r, n), lambda i: (i, 0, 0))
    shape = jax.ShapeDtypeStruct((len(products), r, n), BF)
    return pl.pallas_call(
        functools.partial(grads_kernel, table),
        grid=(len(products),),
        in_specs=[
            pl.BlockSpec(a.shape, lambda i: (0, 0), pipeline_mode=pl.Buffered(1)) for a in arrays
        ],
        out_specs=[out, out],
        out_shape=[shape, shape],
        name="stack_grads",
    )(*arrays)


def back_kernel(blocks, *refs):
    count = (len(refs) - 1) // 3
    out = refs[-1]
    size = out.shape[1] // blocks.shape[0]
    for half in range(2):
        total = dot_nt(refs[0][...], refs[count + half][...])
        for i in range(1, count):
            total = total + dot_nt(refs[i][...], refs[count + 2 * i + half][...])
        for i in range(total.shape[1] // size):
            to = blocks[half * (blocks.shape[0] // 2) + i]
            at = pl.ds(pl.multiple_of(to * size, 128), size)
            out[:, at] = total[:, i * size : (i + 1) * size].astype(out.dtype)


def back_natural(lefts, weights, picks, blocks, rows, dtype):
    m = lefts[0].shape[0]
    near, far = weights
    if picks is None:
        near, far, picks = near[None], far[None], [0]
    n = 2 * near.shape[1]
    in_specs = [pl.BlockSpec((rows, a.shape[1]), lambda i, *_: (i, 0)) for a in lefts]
    values = []
    for p in picks:
        in_specs += [stacked(near, p, pipeline_mode=pl.Buffered(1))] * 2
        values += [near, far]
    return pl.pallas_call(
        back_kernel,
        grid_spec=pltpu.PrefetchScalarGridSpec(
            num_scalar_prefetch=1,
            grid=(m // rows,),
            in_specs=in_specs,
            out_specs=pl.BlockSpec((rows, n), lambda i, *_: (i, 0)),
        ),
        out_shape=jax.ShapeDtypeStruct((m, n), dtype),
        name="back_natural",
    )(blocks, *lefts, *values)


def memory_kernel(x0, x1, k0, k1, v0, v1, bias, keys, values):
    keys[...] = (dot_nn(x0[...], k0[...]) + dot_nn(x1[...], k1[...])).astype(BF)
    total = dot_nn(x0[...], v0[...]) + dot_nn(x1[...], v1[...])
    values[...] = (total + bias[...]).astype(BF)


def memory_project(rows, weights, key_pick, value_pick, bias, block):
    near, far = weights
    m, h = rows[0].shape
    n = near.shape[2]
    once = pl.Buffered(1)
    return pl.pallas_call(
        memory_kernel,
        grid=(m // block,),
        in_specs=[pl.BlockSpec((block, h), lambda i: (i, 0))] * 2
        + [stacked(near, key_pick, pipeline_mode=once)] * 2
        + [stacked(near, value_pick, pipeline_mode=once)] * 2
        + [pl.BlockSpec((1, n), lambda i: (0, 0))],
        out_specs=[pl.BlockSpec((block, n), lambda i: (i, 0))] * 2,
        out_shape=[jax.ShapeDtypeStruct((m, n), BF)] * 2,
        name="memory_project",
    )(*rows, near, far, near, far, bias)


def add_split_kernel(*refs):
    count = len(refs) // 6
    for i in range(count):
        keep_s, got_s, keep_k, got_k = refs[4 * i : 4 * i + 4]
        send, keep = refs[4 * count + 2 * i : 4 * count + 2 * i + 2]
        send[...] = (keep_s[...].astype(F32) + got_s[...].astype(F32)).astype(BF)
        keep[...] = (keep_k[...].astype(F32) + got_k[...].astype(F32)).astype(BF)


def add_split(parts):
    in_specs, out_specs, shapes, values = [], [], [], []
    for keep, got, first, count, low in parts:
        _, blocks, rows, n = keep.shape

        def spec(value, first=first, low=low, rows=rows, n=n):
            def index(i, j):
                high, rest = j >> low, j & ((1 << low) - 1)
                return first + i, (high << (low + 1)) | (value << low) | rest, 0, 0

            return pl.BlockSpec((None, None, rows, n), index)

        in_specs += [spec(1), spec(1), spec(0), spec(0)]
        values += [keep, got, keep, got]
        out_specs += [pl.BlockSpec((None, None, rows, n), lambda i, j: (i, j, 0, 0))] * 2
        shapes += [jax.ShapeDtypeStruct((count, blocks // 2, rows, n), BF)] * 2
    found = pl.pallas_call(
        add_split_kernel,
        grid=shapes[0].shape[:2],
        in_specs=in_specs,
        out_specs=out_specs,
        out_shape=shapes,
        name="add_split",
    )(*values)
    return found[0::2], found[1::2]


class Plan:
    def __init__(self):
        self.wide = lax.axis_size("wide")
        self.narrow = lax.axis_size("narrow")
        self.count = self.wide * self.narrow
        self.w = lax.axis_index("wide")
        self.z = lax.axis_index("narrow")
        self.me = self.w * self.narrow + self.z
        bits = self.wide.bit_length() - 1
        rest = [1 << b for b in range(1, bits)]
        half = len(rest) // 2
        self.core = self.narrow
        xs = [m * self.narrow for m in rest[:half]]
        ys = [m * self.narrow for m in rest[half:]]
        self.across = sorted([*xs, *ys], reverse=True)
        self.routes = ([*xs, *ys], [*ys, *xs])
        self.zs = [1 << b for b in range(self.narrow.bit_length() - 1)]
        self.order = [r for r in range(self.wide) if r % 2 == 0] + [
            r for r in range(self.wide) if r % 2 == 1
        ]

    def bit(self, index, mask):
        return (index // mask) % 2

    def step(self, stream, after=None, during=None):
        sends = [value for value, _ in stream.sends]
        if after is not None:
            sends, _ = lax.optimization_barrier((sends, after))
        got = [
            lax.ppermute(v, AXES, [(i, i ^ m) for i in range(self.count)])
            for v, (_, m) in zip(sends, stream.sends)
        ]
        if during is not None:
            got, _ = lax.optimization_barrier((got, during))
        stream.feed(got)
        return got

    def across_steps(self, stream, after, during=None):
        for _ in self.across[1:]:
            after = self.step(stream, after, during)
        return after

    def finish(self, stream):
        while stream.result is None:
            self.step(stream)

    def relative(self, rows):
        size = rows.shape[1] // self.wide
        pieces = [
            lax.dynamic_slice_in_dim(rows, (jnp.int32(r) ^ self.w) * size, size, axis=1)
            for r in self.order
        ]
        half = self.wide // 2
        return jnp.concatenate(pieces[:half], axis=1), jnp.concatenate(pieces[half:], axis=1)

    def natural(self, rows):
        size = rows.shape[1] // self.wide
        pieces = []
        for i in range(self.wide):
            r = jnp.int32(i) ^ self.w
            place = (r % 2) * (self.wide // 2) + r // 2
            pieces.append(lax.dynamic_slice_in_dim(rows, place * size, size, axis=1))
        return jnp.concatenate(pieces, axis=1)

    def places(self):
        r = lax.iota(jnp.int32, self.wide) ^ self.w
        return (r % 2) * (self.wide // 2) + r // 2

    def blocks(self):
        return jnp.array(self.order, jnp.int32) ^ self.w

    def gather(self, part, split, join):
        k, rows, n = part.shape
        have = part.reshape(k, 1, rows, n)
        for mask in reversed(self.zs):
            (other,) = yield [(have, mask)]
            low = self.bit(self.z, mask) == 0
            have = jnp.stack(
                [jnp.where(low, have, other), jnp.where(low, other, have)], axis=2
            ).reshape(k, -1, rows, n)
        sets = [piece for piece in split(have.reshape(k, -1, n))]
        bits = len(self.across)
        for step in range(bits):
            got = yield [(s, route[step]) for s, route in zip(sets, self.routes)]
            sets = [jnp.stack([s, g]) for s, g in zip(sets, got)]
        whole = []
        for s, route in zip(sets, self.routes):
            axes = [list(reversed(route)).index(mask) for mask in self.across]
            s = jnp.transpose(s, [bits, *axes, bits + 1, bits + 2])
            whole.append(s.reshape(s.shape[0], -1, s.shape[-1]))
        near = join(*whole)
        (far,) = yield [(near, self.core)]
        return near, far

    def scatter(self, lefts, rights, products):
        keep, send = stack_grads(lefts, rights, products)
        (got,) = yield [(send, self.core)]
        count, r, n = keep.shape
        bits = len(self.across)
        shape = (count, 1 << bits, r >> bits, n)
        keep, got = keep.reshape(shape), got.reshape(shape)
        pairs = [(keep, got, 0, count // 2), (keep, got, count // 2, count // 2)]
        lefts = [list(self.across) for _ in pairs]
        for step in reversed(range(bits)):
            masks, parts = [], []
            for i, pair in enumerate(pairs):
                mask = self.routes[i][step]
                axis = lefts[i].index(mask)
                parts.append((*pair, len(lefts[i]) - 1 - axis))
                lefts[i].pop(axis)
                masks.append(mask)
            sends, keeps = add_split(parts)
            gots = yield list(zip(sends, masks))
            pairs = [(k, g, 0, count // 2) for k, g in zip(keeps, gots)]
        acc = jnp.concatenate([k.astype(F32) + g.astype(F32) for k, g, _, _ in pairs], axis=0)
        own = (r >> bits) // self.narrow
        acc = acc.reshape((count,) + (2,) * len(self.zs) + (own, n))
        for mask in self.zs:
            axis = len(acc.shape) - 3
            place = self.bit(self.z, mask)
            send = lax.dynamic_index_in_dim(acc, 1 - place, axis, keepdims=False).astype(BF)
            acc = lax.dynamic_index_in_dim(acc, place, axis, keepdims=False)
            (got,) = yield [(send, mask)]
            acc = acc + got.astype(F32)
        return acc

    def gather_small(self, vector):
        n = vector.shape[0]
        have = vector.reshape(1, n // 128, 128)
        for mask in [1 << b for b in range(self.count.bit_length() - 1)]:
            (other,) = yield [(have, mask)]
            low = self.bit(self.me, mask) == 0
            have = jnp.concatenate(
                [jnp.where(low, have, other), jnp.where(low, other, have)], axis=0
            )
        return have.reshape(self.count, n)

    def scatter_small(self, table):
        n = table.shape[1]
        have = table.reshape(self.count, n // 128, 128)
        for mask in [1 << b for b in reversed(range(self.count.bit_length() - 1))]:
            place = self.bit(self.me, mask)
            keep = lax.dynamic_slice_in_dim(have, place * mask, mask, axis=0)
            send = lax.dynamic_slice_in_dim(have, (1 - place) * mask, mask, axis=0)
            (got,) = yield [(send, mask)]
            have = keep + got
        return have.reshape(n)


class Stream:
    def __init__(self, steps):
        self.steps, self.result = steps, None
        self.sends = next(steps)

    def feed(self, got):
        try:
            self.sends = self.steps.send(list(got))
        except StopIteration as end:
            self.result = end.value


def pad_lanes(table):
    return jnp.pad(table, ((0, 0), (0, -table.shape[1] % 1024)))


def local(
    inputs,
    memory,
    mem_lengths,
    self_qkv,
    self_out,
    self_bias,
    self_gain,
    cross_qkv,
    cross_out,
    cross_bias,
    cross_gain,
    ffn_in,
    ffn_out,
    ffn_bias_in,
    ffn_bias_out,
    ffn_gain,
    out_grad,
):
    plan = Plan()
    scaling = HD ** (-0.5)
    item_count, mem_slots, model_width = memory.shape
    row_count = inputs.shape[0]
    pairs = model_width // PAIR
    paired = plan.wide == pairs
    place = plan.places() if paired else lax.iota(jnp.int32, pairs)

    def context_back(rows, weights):
        if paired:
            here = lax.iota(jnp.int32, plan.wide)
            return back_natural([rows], weights, [3], here, row_count, BF)
        return plan.natural(backward(rows, (weights[0][3], weights[1][3]))).astype(BF)

    def to_relative(context):
        half = model_width // 2
        return (context[:, :half], context[:, half:]) if paired else plan.relative(context)

    def back(lefts, weights, picks, rows, dtype=F32):
        if (model_width // plan.wide) % 128 == 0:
            return back_natural(lefts, weights, picks, plan.blocks(), rows, dtype)
        total = 0.0
        for i, left in enumerate(lefts):
            near, far = weights if picks is None else (weights[0][picks[i]], weights[1][picks[i]])
            total = total + backward(left, (near, far))
        return plan.natural(total).astype(dtype)

    def forward(rows, weight):
        return project(rows[0], weight[0]) + project(rows[1], weight[1])

    def backward(rows, weight):
        return jnp.concatenate(
            [project_back(rows, weight[0]), project_back(rows, weight[1])], axis=1
        )

    inputs_f = inputs.astype(F32)

    share, hidden_share = self_gain.shape[0], ffn_bias_in.shape[0]
    small_rows = jnp.concatenate(
        [self_bias, self_gain[None], cross_bias, cross_gain[None], ffn_bias_out, ffn_gain[None]],
        axis=0,
    )
    vector_count = small_rows.shape[0]
    small = Stream(
        plan.gather_small(
            pad_lanes(jnp.concatenate([small_rows.reshape(1, -1), ffn_bias_in[None]], axis=1))[0]
        )
    )

    def four(have):
        return have[:2], have[2:]

    def each(a, b):
        return jnp.concatenate([a, b], axis=0)

    def columns(have):
        half = have.shape[-1] // 2
        return have[..., :half], have[..., half:]

    def one(a, b):
        return jnp.concatenate([a[0], b[0]], axis=1)

    selfs = Stream(
        plan.gather(jnp.concatenate([self_qkv, self_out[None]], axis=0), four, each)
    )
    crosses = Stream(
        plan.gather(jnp.concatenate([cross_qkv, cross_out[None]], axis=0), four, each)
    )
    fins = Stream(plan.gather(ffn_in[None], columns, one))
    fouts = Stream(plan.gather(ffn_out[None], columns, one))
    after = plan.step(small)
    for _ in plan.zs:
        after = (plan.step(selfs, after), plan.step(small))
    after = (after, plan.step(small))
    for _ in plan.across[2:]:
        after = plan.step(selfs, after)
    last = plan.step(selfs, after)
    plan.finish(small)
    cross_z = plan.step(crosses, after)
    last = plan.step(selfs, (last, cross_z, small.result))
    for _ in plan.zs[1:]:
        cross_z = plan.step(crosses, cross_z)
    self_core = plan.step(selfs, cross_z)
    last = plan.step(crosses, last)
    fin_z = plan.step(fins, cross_z)
    table = small.result.astype(F32)
    vectors = table[:, : vector_count * share].reshape(plan.count, vector_count, share)
    vectors = jnp.swapaxes(vectors, 0, 1).reshape(vector_count, model_width)
    sbias, sgain, cbias, cgain, fbout, fgain = (
        vectors[:4],
        vectors[4],
        vectors[5:9],
        vectors[9],
        vectors[10:12],
        vectors[12],
    )
    fbin = table[:, vector_count * share :][:, :hidden_share].reshape(-1)

    x_rel = plan.relative(inputs)
    no_bias = jnp.zeros((model_width,), F32)
    qkv = stack_project(
        x_rel,
        selfs.result,
        0,
        jnp.stack([sbias[0], no_bias, sbias[1]])[:, None],
        (scaling, 1.0, 1.0),
        BF,
    )
    self_ctx, self_lse = self_attend(qkv, item_count, place)
    self_rel = to_relative(self_ctx)
    first_pre = inputs_f + stack_project(self_rel, selfs.result, 3, sbias[None, 2:3], (1.0,), F32)[0]
    first = layer_norm(first_pre, sgain, sbias[3])
    first_rel = plan.relative(first.astype(BF))
    last = plan.across_steps(crosses, (last, self_core, fin_z), first_rel)
    for _ in plan.zs[1:]:
        fin_z = plan.step(fins, fin_z)
    fout_z = plan.step(fouts, fin_z)
    cross_core = plan.step(crosses)
    last = plan.step(fins, (last, fout_z))
    for _ in plan.zs[1:]:
        fout_z = plan.step(fouts, fout_z)
    queries_two = stack_project(first_rel, crosses.result, 0, cbias[None, 0:1], (scaling,), BF)[0]
    mem_rel = plan.relative(memory.reshape(item_count * mem_slots, model_width))
    mem_keys, mem_values = memory_project(mem_rel, crosses.result, 1, 2, cbias[1:2], 512)
    last = plan.across_steps(
        fins, (last, cross_core, fout_z), (queries_two, mem_keys, mem_values)
    )
    fin_core = plan.step(fins)
    cross_out = ()
    for item in range(item_count):
        cross_out = cross_attend(
            queries_two, mem_keys, mem_values, mem_lengths, place, item, cross_out
        )
        if item == 0:
            last = plan.step(fouts, last, cross_out)
    cross_ctx, cross_lse = cross_out
    fin = fins.result
    cross_rel = to_relative(cross_ctx)
    second_pre = first + stack_project(cross_rel, crosses.result, 3, cbias[None, 2:3], (1.0,), F32)[0]
    second = layer_norm(second_pre, cgain, cbias[3])
    second_rel = plan.relative(second.astype(BF))
    plan.across_steps(fouts, (last, fin_core), second_rel)

    pre_gelu = forward(second_rel, fin) + fbin
    hidden, gelu_pull = jax.vjp(gelu_exact, pre_gelu)
    hidden_rel = plan.relative(hidden.astype(BF))
    plan.step(fouts, None, hidden_rel)
    fout = fouts.result
    third_pre = second + (forward(hidden_rel, fout) + fbout[0])
    layer_out, norm_pull = jax.vjp(layer_norm, third_pre, fgain, fbout[1])

    d_third, g_fgain, g_fshift = norm_pull(out_grad.astype(F32))
    e_three = d_third.astype(BF)
    half = model_width // 2
    to_fout = Stream(
        plan.scatter([hidden_rel], [e_three], [(0, 0, 0, half), (0, 0, half, half)])
    )
    d_pre = gelu_pull(plan.natural(backward(e_three, fout)))[0].astype(BF)
    plan.step(to_fout, None, d_pre)
    half = d_pre.shape[1] // 2
    to_fin = Stream(plan.scatter([second_rel], [d_pre], [(0, 0, 0, half), (0, 0, half, half)]))
    g_fbin = column_sums(d_pre)
    d_second = d_third + back([d_pre], fin, None, row_count)

    _, norm_pull_two = jax.vjp(layer_norm, second_pre, cgain, cbias[3])
    d_second_pre, g_cgain, g_cshift = norm_pull_two(d_second)
    e_two = d_second_pre.astype(BF)
    last = plan.step(to_fout, None, (e_two, [v for v, _ in to_fin.sends]))
    plan.step(to_fin)
    d_cross_ctx = context_back(e_two, crosses.result)
    cross_back = ()
    for item in range(item_count):
        cross_back = cross_attend_back(
            queries_two, mem_keys, mem_values, cross_lse, d_cross_ctx, mem_lengths, place,
            item, cross_back,
        )
        if item == 0:
            last = plan.across_steps(to_fout, last, cross_back)
    dq_scaled, dk_flat, dv_flat = cross_back
    to_cross = Stream(
        plan.scatter(
            [first_rel, mem_rel, cross_rel],
            [dq_scaled, dk_flat, dv_flat, e_two],
            [(0, 0, 0, model_width), (1, 1, 0, model_width), (1, 2, 0, model_width), (2, 3, 0, model_width)],
        )
    )
    last = plan.step(to_fin, last, [v for v, _ in to_cross.sends])
    plan.step(to_cross)
    for _ in plan.zs:
        fout_last = plan.step(to_fout)
    d_first = d_second_pre + back([dq_scaled], crosses.result, [0], row_count)

    _, norm_pull_one = jax.vjp(layer_norm, first_pre, sgain, sbias[3])
    d_first_pre, g_sgain, g_sshift = norm_pull_one(d_first)
    e_one = d_first_pre.astype(BF)
    d_self_ctx = context_back(e_one, selfs.result)
    last = plan.across_steps(to_fin, (last, fout_last), d_self_ctx)
    dq_self, dk_self, dv_self = self_attend_back(qkv, self_lse, d_self_ctx, item_count, place)
    to_self = Stream(
        plan.scatter(
            [x_rel, self_rel],
            [dq_self, dk_self, dv_self, e_one],
            [(0, 0, 0, model_width), (0, 1, 0, model_width), (0, 2, 0, model_width), (1, 3, 0, model_width)],
        )
    )
    last = plan.step(to_cross, last, [v for v, _ in to_self.sends])
    plan.step(to_self)
    for _ in plan.zs:
        fin_last = plan.step(to_fin)
    input_grad = d_first_pre + back(
        [dq_self, dk_self, dv_self], selfs.result, [0, 1, 2], row_count
    )
    last = plan.across_steps(to_cross, (last, fin_last), input_grad)
    memory_grad = back([dk_flat, dv_flat], crosses.result, [1, 2], 512).reshape(memory.shape)
    last = plan.step(to_self, last, memory_grad)
    for _ in plan.zs:
        cross_last = plan.step(to_cross)
    plan.across_steps(to_self, (last, cross_last))
    plan.finish(to_self)
    grads = jnp.stack(
        [
            column_sums(dq_self),
            column_sums(dv_self),
            column_sums(e_one),
            g_sshift,
            g_sgain,
            column_sums(dq_scaled),
            column_sums(dv_flat),
            column_sums(e_two),
            g_cshift,
            g_cgain,
            column_sums(e_three),
            g_fshift,
            g_fgain,
        ]
    )
    grads = jnp.swapaxes(grads.reshape(vector_count, plan.count, share), 0, 1)
    to_small = Stream(
        plan.scatter_small(
            pad_lanes(
                jnp.concatenate(
                    [grads.reshape(plan.count, -1), g_fbin.reshape(plan.count, -1)], axis=1
                )
            )
        )
    )
    plan.finish(to_small)
    small_sums = to_small.result
    found = small_sums[: vector_count * share].reshape(vector_count, share)
    g_hidden = small_sums[vector_count * share :][:hidden_share]
    g_self, g_cross = to_self.result, to_cross.result
    g_fout = jnp.concatenate([to_fout.result[0], to_fout.result[1]], axis=1)
    g_fin = jnp.concatenate([to_fin.result[0], to_fin.result[1]], axis=1)
    return (
        layer_out.astype(BF),
        input_grad,
        memory_grad,
        g_self[:3],
        g_self[3],
        found[:4],
        found[4],
        g_cross[:3],
        g_cross[3],
        found[5:9],
        found[9],
        g_fin,
        g_fout,
        g_hidden,
        found[10:12],
        found[12],
    )


def solution(mesh):
    both = ("wide", "narrow")
    placed = (
        P(both, None),
        P(both, None, None),
        P(both),
        P(None, both, None),
        P(both, None),
        P(None, both),
        P(both),
        P(None, both, None),
        P(both, None),
        P(None, both),
        P(both),
        P(both, None),
        P(both, None),
        P(both),
        P(None, both),
        P(both),
        P(both, None),
    )
    return jax.shard_map(
        local,
        mesh=mesh,
        in_specs=placed,
        out_specs=(
            P(both, None),
            P(both, None),
            P(both, None, None),
            P(None, both, None),
            P(both, None),
            P(None, both),
            P(both),
            P(None, both, None),
            P(both, None),
            P(None, both),
            P(both),
            P(both, None),
            P(both, None),
            P(both),
            P(None, both),
            P(both),
        ),
        check_vma=False,
    )
```

```python
import functools
import math

import jax
import jax.numpy as jnp
from jax import lax
from jax.experimental import pallas as pl
from jax.experimental.pallas import tpu as pltpu
from jax.sharding import PartitionSpec as P

HD = 64
EPSILON = 1e-05
MASKED = -1e30
AXES = ("wide", "narrow")
BF = jnp.bfloat16
F32 = jnp.float32


def project(left_rows, weight):
    return jnp.dot(left_rows, weight, preferred_element_type=F32)


def project_back(gradient, weight):
    return lax.dot_general(gradient, weight, (((1,), (1,)), ((), ())), preferred_element_type=F32)


def weight_grad(left_rows, gradient):
    return lax.dot_general(left_rows, gradient, (((0,), (0,)), ((), ())), preferred_element_type=F32)


def column_sums(gradient):
    return jnp.sum(gradient.astype(F32), axis=0)


def layer_norm(hidden, gain_row, shift_row):
    average = jnp.mean(hidden, axis=-1, keepdims=True)
    centred = hidden - average
    variance = jnp.mean(centred * centred, axis=-1, keepdims=True)
    return centred * lax.rsqrt(variance + EPSILON) * gain_row + shift_row


def pair_stack(rows):
    lane = lax.broadcasted_iota(jnp.int32, rows.shape, 1)
    zero = jnp.zeros_like(rows)
    return jnp.concatenate(
        [jnp.where(lane < HD, rows, zero), jnp.where(lane >= HD, rows, zero)], axis=0
    )


def pair_merge(stacked):
    t = stacked.shape[0] // 2
    lane = lax.broadcasted_iota(jnp.int32, (t, 2 * HD), 1)
    return jnp.where(lane < HD, stacked[:t], stacked[t:])


def dot_nt(a, b):
    return lax.dot_general(a, b, (((1,), (1,)), ((), ())), preferred_element_type=F32)


def dot_tn(a, b):
    return lax.dot_general(a, b, (((0,), (0,)), ((), ())), preferred_element_type=F32)


def dot_nn(a, b):
    return lax.dot_general(a, b, (((1,), (0,)), ((), ())), preferred_element_type=F32)


def masked_scores(k, qs, length):
    scores = dot_nt(k, qs)
    slot = lax.broadcasted_iota(jnp.int32, scores.shape, 0)
    if length is None:
        seen = lax.broadcasted_iota(jnp.int32, scores.shape, 1) % (scores.shape[1] // 2)
        return jnp.where(slot <= seen, scores, MASKED)
    return jnp.where(slot < length, scores, MASKED)


def attend_pair(q, k, v, length):
    scores = masked_scores(k, pair_stack(q), length)
    top = jnp.max(scores, axis=0, keepdims=True)
    weights = jnp.exp(scores - top)
    total = jnp.sum(weights, axis=0, keepdims=True)
    chances = (weights * (1.0 / total)).astype(BF)
    return pair_merge(dot_tn(chances, v)).astype(BF), top + jnp.log(total)


def attend_pair_back(q, k, v, lse, d_out, length):
    qs, ds_out = pair_stack(q), pair_stack(d_out)
    chances = jnp.exp(masked_scores(k, qs, length) - lse)
    d_chances = dot_nt(v, ds_out)
    row = jnp.sum(d_chances * chances, axis=0, keepdims=True)
    d_scores = (chances * (d_chances - row)).astype(BF)
    d_q = pair_merge(dot_tn(d_scores, k)).astype(BF)
    d_k = dot_nn(d_scores, qs).astype(BF)
    d_v = dot_nn(chances.astype(BF), ds_out).astype(BF)
    return d_q, d_k, d_v


PAIR = 2 * HD
UNROLL = 2


def lane_block(at):
    return pl.ds(pl.multiple_of(at * PAIR, PAIR), PAIR)


def cross_kernel(place, length, q, k, v, *refs):
    out, lse = refs[-2:]
    for u in range(UNROLL):
        cut = slice(u * PAIR, (u + 1) * PAIR)
        found, lse[0, u] = attend_pair(q[:, cut], k[:, cut], v[:, cut], length[0])
        out[:, lane_block(place[pl.program_id(0) * UNROLL + u])] = found


def cross_back_kernel(place, length, q, k, v, lse, d_out, *refs):
    d_q, d_k, d_v = refs[-3:]
    for u in range(UNROLL):
        cut = slice(u * PAIR, (u + 1) * PAIR)
        cotangent = d_out[:, lane_block(place[pl.program_id(0) * UNROLL + u])]
        found = attend_pair_back(
            q[:, cut], k[:, cut], v[:, cut], lse[0, u], cotangent, length[0]
        )
        d_q[:, cut] = found[0] * jnp.asarray(HD**-0.5, BF)
        d_k[:, cut] = found[1]
        d_v[:, cut] = found[2]


def cross_call(kernel, q, k, lengths, place, item, values, in_specs, out_specs, out_shape, so_far):
    return pl.pallas_call(
        kernel,
        grid_spec=pltpu.PrefetchScalarGridSpec(
            num_scalar_prefetch=2,
            grid=(q.shape[1] // PAIR // UNROLL,),
            in_specs=in_specs + [pl.BlockSpec(memory_space=pl.ANY)] * len(so_far),
            out_specs=out_specs,
        ),
        out_shape=out_shape,
        input_output_aliases={2 + len(values) + i: i for i in range(len(so_far))},
        name="cross_attend",
    )(place, lax.slice_in_dim(lengths, item, item + 1), *values, *so_far)


def cross_specs(q, k, items, item):
    t, s, n = q.shape[0] // items, k.shape[0] // items, PAIR * UNROLL
    rows = pl.BlockSpec((t, n), lambda j, *_: (item, j))
    slots = pl.BlockSpec((s, n), lambda j, *_: (item, j))
    placed = pl.BlockSpec((t, q.shape[1]), lambda j, *_: (item, 0))
    lse = pl.BlockSpec((1, UNROLL, 1, 2 * t), lambda j, *_: (item, j, 0, 0))
    return rows, slots, placed, lse


def cross_attend(q, k, v, lengths, place, item, so_far):
    items = lengths.shape[0]
    rows, slots, placed, lse = cross_specs(q, k, items, item)
    out_shape = [
        jax.ShapeDtypeStruct(q.shape, BF),
        jax.ShapeDtypeStruct((items, q.shape[1] // PAIR, 1, 2 * q.shape[0] // items), F32),
    ]
    return cross_call(
        cross_kernel, q, k, lengths, place, item, (q, k, v),
        [rows, slots, slots], [placed, lse], out_shape, so_far,
    )


def cross_attend_back(q, k, v, lse, d_out, lengths, place, item, so_far):
    rows, slots, placed, lse_spec = cross_specs(q, k, lengths.shape[0], item)
    out_shape = [jax.ShapeDtypeStruct(a.shape, BF) for a in (q, k, k)]
    return cross_call(
        cross_back_kernel, q, k, lengths, place, item, (q, k, v, lse, d_out),
        [rows, slots, slots, lse_spec, placed], [rows, slots, slots], out_shape, so_far,
    )


def lanes(ref, at):
    return ref[:, pl.ds(pl.multiple_of(at * PAIR, PAIR), PAIR)]


def self_kernel(place, q, k, v, out, lse):
    for j in range(q.shape[1] // PAIR):
        cut = slice(j * PAIR, (j + 1) * PAIR)
        found, lse[0, j] = attend_pair(q[:, cut], k[:, cut], v[:, cut], None)
        out[:, pl.ds(pl.multiple_of(place[j] * PAIR, PAIR), PAIR)] = found


def self_back_kernel(place, q, k, v, lse, d_out, d_q, d_k, d_v):
    for j in range(q.shape[1] // PAIR):
        cut = slice(j * PAIR, (j + 1) * PAIR)
        found = attend_pair_back(
            q[:, cut], k[:, cut], v[:, cut], lse[0, j], lanes(d_out, place[j]), None
        )
        d_q[:, cut] = found[0] * jnp.asarray(HD**-0.5, BF)
        d_k[:, cut] = found[1]
        d_v[:, cut] = found[2]


def self_attend(qkv, items, place):
    _, rows, width = qkv.shape
    t = rows // items

    def part(i):
        return pl.BlockSpec((None, t, width), lambda b, *_: (i, b, 0))

    lse = pl.BlockSpec((1, width // PAIR, 1, 2 * t), lambda b, *_: (b, 0, 0, 0))
    return pl.pallas_call(
        self_kernel,
        grid_spec=pltpu.PrefetchScalarGridSpec(
            num_scalar_prefetch=1,
            grid=(items,),
            in_specs=[part(0), part(1), part(2)],
            out_specs=[pl.BlockSpec((t, width), lambda b, *_: (b, 0)), lse],
        ),
        out_shape=[
            jax.ShapeDtypeStruct((rows, width), BF),
            jax.ShapeDtypeStruct((items, width // PAIR, 1, 2 * t), F32),
        ],
        name="self_attend",
    )(place, qkv, qkv, qkv)


def self_attend_back(qkv, lse, d_out, items, place):
    _, m, width = qkv.shape
    t = m // items

    def part(i):
        return pl.BlockSpec((None, t, width), lambda b, *_: (i, b, 0))

    rows = pl.BlockSpec((t, width), lambda b, *_: (b, 0))
    lse_spec = pl.BlockSpec((1, width // PAIR, 1, 2 * t), lambda b, *_: (b, 0, 0, 0))
    return pl.pallas_call(
        self_back_kernel,
        grid_spec=pltpu.PrefetchScalarGridSpec(
            num_scalar_prefetch=1,
            grid=(items,),
            in_specs=[part(0), part(1), part(2), lse_spec, rows],
            out_specs=[rows] * 3,
        ),
        out_shape=[jax.ShapeDtypeStruct((m, width), BF)] * 3,
        name="self_attend_back",
    )(place, qkv, qkv, qkv, lse, d_out)


def stacked(array, i, **kw):
    return pl.BlockSpec((None,) + array.shape[1:], lambda *_: (i, 0, 0), **kw)


def project_kernel(scales, x0, x1, near, far, bias, out):
    total = dot_nn(x0[...], near[...]) + dot_nn(x1[...], far[...]) + bias[...]
    j = pl.program_id(0)
    scale = scales[0]
    for i in range(1, len(scales)):
        scale = jnp.where(j == i, scales[i], scale)
    out[...] = (total * scale).astype(out.dtype)


def stack_project(rows, weights, first, bias, scales, dtype):
    near, far = weights
    m, h = rows[0].shape
    n = near.shape[2]
    count = len(scales)
    whole = pl.BlockSpec((m, h), lambda j: (0, 0))
    weight = pl.BlockSpec((None, h, n), lambda j: (first + j, 0, 0))
    return pl.pallas_call(
        functools.partial(project_kernel, scales),
        grid=(count,),
        in_specs=[whole, whole, weight, weight, pl.BlockSpec((None, 1, n), lambda j: (j, 0, 0))],
        out_specs=pl.BlockSpec((None, m, n), lambda j: (j, 0, 0)),
        out_shape=jax.ShapeDtypeStruct((count, m, n), dtype),
        name="stack_project",
    )(*rows, near, far, bias)


def grads_kernel(products, *refs):
    ins, (keep, send) = refs[:-2], refs[-2:]
    for i, (left, right, start) in enumerate(products):

        @pl.when(pl.program_id(0) == i)
        def _():
            to = ins[right][:, start : start + keep.shape[1]]
            keep[...] = dot_tn(ins[left][...], to).astype(BF)
            send[...] = dot_tn(ins[left + 1][...], to).astype(BF)


def stack_grads(lefts, rights, products):
    arrays = [half for left in lefts for half in left] + list(rights)
    n = products[0][3]
    r = lefts[0][0].shape[1]
    table = [(2 * left, 2 * len(lefts) + right, start) for left, right, start, _ in products]
    out = pl.BlockSpec((None, r, n), lambda i: (i, 0, 0))
    shape = jax.ShapeDtypeStruct((len(products), r, n), BF)
    return pl.pallas_call(
        functools.partial(grads_kernel, table),
        grid=(len(products),),
        in_specs=[
            pl.BlockSpec(a.shape, lambda i: (0, 0), pipeline_mode=pl.Buffered(1)) for a in arrays
        ],
        out_specs=[out, out],
        out_shape=[shape, shape],
        name="stack_grads",
    )(*arrays)


def back_kernel(blocks, *refs):
    count = (len(refs) - 1) // 3
    out = refs[-1]
    size = out.shape[1] // blocks.shape[0]
    for half in range(2):
        total = dot_nt(refs[0][...], refs[count + half][...])
        for i in range(1, count):
            total = total + dot_nt(refs[i][...], refs[count + 2 * i + half][...])
        for i in range(total.shape[1] // size):
            to = blocks[half * (blocks.shape[0] // 2) + i]
            at = pl.ds(pl.multiple_of(to * size, 128), size)
            out[:, at] = total[:, i * size : (i + 1) * size].astype(out.dtype)


def back_natural(lefts, weights, picks, blocks, rows, dtype):
    m = lefts[0].shape[0]
    near, far = weights
    if picks is None:
        near, far, picks = near[None], far[None], [0]
    n = 2 * near.shape[1]
    in_specs = [pl.BlockSpec((rows, a.shape[1]), lambda i, *_: (i, 0)) for a in lefts]
    values = []
    for p in picks:
        in_specs += [stacked(near, p, pipeline_mode=pl.Buffered(1))] * 2
        values += [near, far]
    return pl.pallas_call(
        back_kernel,
        grid_spec=pltpu.PrefetchScalarGridSpec(
            num_scalar_prefetch=1,
            grid=(m // rows,),
            in_specs=in_specs,
            out_specs=pl.BlockSpec((rows, n), lambda i, *_: (i, 0)),
        ),
        out_shape=jax.ShapeDtypeStruct((m, n), dtype),
        name="back_natural",
    )(blocks, *lefts, *values)


def normed(hidden):
    centred = hidden - jnp.mean(hidden, axis=-1, keepdims=True)
    scale = lax.rsqrt(jnp.mean(centred * centred, axis=-1, keepdims=True) + EPSILON)
    return centred * scale, scale


def norm_kernel(blocks, branch, residual, gain, shift, pre, out, rel0, rel1):
    pre[...] = residual[...].astype(F32) + branch[...]
    out[...] = normed(pre[...])[0] * gain[...] + shift[...]
    half = blocks.shape[0] // 2
    size = out.shape[1] // blocks.shape[0]
    for i in range(2 * half):
        rel, at = (rel0, i) if i < half else (rel1, i - half)
        block = out[:, pl.ds(pl.multiple_of(blocks[i] * size, 128), size)]
        rel[:, at * size : (at + 1) * size] = block.astype(BF)


def norm(branch, residual, gain, shift, blocks):
    m, n = branch.shape
    rows = m // 2
    full = pl.BlockSpec((rows, n), lambda i, *_: (i, 0))
    halves = pl.BlockSpec((rows, n // 2), lambda i, *_: (i, 0))
    row = pl.BlockSpec((1, n), lambda i, *_: (0, 0))
    pre, out, rel0, rel1 = pl.pallas_call(
        norm_kernel,
        grid_spec=pltpu.PrefetchScalarGridSpec(
            num_scalar_prefetch=1,
            grid=(2,),
            in_specs=[full, full, row, row],
            out_specs=[full, full, halves, halves],
        ),
        out_shape=[
            jax.ShapeDtypeStruct((m, n), F32),
            jax.ShapeDtypeStruct((m, n), F32),
            jax.ShapeDtypeStruct((m, n // 2), BF),
            jax.ShapeDtypeStruct((m, n // 2), BF),
        ],
        name="norm",
    )(blocks, branch, residual, gain, shift)
    return pre, out, (rel0, rel1)


def norm_back_kernel(count, *refs):
    pre, gain = refs[count : count + 2]
    d_pre, low, sums = refs[-3:]
    cotangent = refs[0][...].astype(F32)
    for ref in refs[1:count]:
        cotangent = cotangent + ref[...]
    z, scale = normed(pre[...])
    if len(refs) > count + 5:
        shift, out = refs[count + 2], refs[-4]
        out[...] = (z * gain[...] + shift[...]).astype(BF)
    inner = cotangent * gain[...]
    found = scale * (
        inner
        - jnp.mean(inner, axis=-1, keepdims=True)
        - z * jnp.mean(inner * z, axis=-1, keepdims=True)
    )
    d_pre[...] = found
    low[...] = found.astype(BF)

    @pl.when(pl.program_id(0) == 0)
    def _():
        sums[...] = jnp.zeros_like(sums)

    rows = [found.astype(BF).astype(F32), cotangent, cotangent * z]
    for i, value in enumerate(rows):
        sums[i : i + 1, :] += jnp.sum(value, axis=0, keepdims=True)


def norm_back(cotangents, pre, gain, shift=None):
    m, n = pre.shape
    rows = m // 2
    full = pl.BlockSpec((rows, n), lambda i: (i, 0))
    row = pl.BlockSpec((1, n), lambda i: (0, 0))
    extra = [] if shift is None else [shift]
    out_specs = [full, full, pl.BlockSpec((8, n), lambda i: (0, 0))]
    out_shape = [
        jax.ShapeDtypeStruct((m, n), F32),
        jax.ShapeDtypeStruct((m, n), BF),
        jax.ShapeDtypeStruct((8, n), F32),
    ]
    if shift is not None:
        out_specs, out_shape = [full] + out_specs, [jax.ShapeDtypeStruct((m, n), BF)] + out_shape
    return pl.pallas_call(
        functools.partial(norm_back_kernel, len(cotangents)),
        grid=(2,),
        in_specs=[full] * (len(cotangents) + 1) + [row] * (1 + len(extra)),
        out_specs=out_specs,
        out_shape=out_shape,
        name="norm_back",
    )(*cotangents, pre, gain, *extra)


def gelu_parts(u):
    half_erf = 0.5 * (1.0 + lax.erf(u * (0.5**0.5)))
    return u * half_erf, half_erf + u * jnp.exp(-0.5 * u * u) * (0.5 / math.pi) ** 0.5


def ffn_up_kernel(places, x0, x1, near, far, bias, hidden, slope):
    u = dot_nn(x0[...], near[...]) + dot_nn(x1[...], far[...]) + bias[...]
    value, slope[...] = gelu_parts(u)
    hidden[...] = value.astype(BF)


def ffn_up(rows, weight, bias, places):
    near, far = weight
    m, h = rows[0].shape
    n = near.shape[1]
    size = n // places.shape[0]
    whole = pl.BlockSpec((m, h), lambda j, *_: (0, 0))
    columns = pl.BlockSpec((h, size), lambda j, *_: (0, j))
    return pl.pallas_call(
        ffn_up_kernel,
        grid_spec=pltpu.PrefetchScalarGridSpec(
            num_scalar_prefetch=1,
            grid=(n // size,),
            in_specs=[whole, whole, columns, columns, pl.BlockSpec((1, size), lambda j, *_: (0, j))],
            out_specs=[
                pl.BlockSpec((m, size), lambda j, places: (0, places[j])),
                pl.BlockSpec((m, size), lambda j, places: (0, j)),
            ],
        ),
        out_shape=[jax.ShapeDtypeStruct((m, n), BF), jax.ShapeDtypeStruct((m, n), F32)],
        name="ffn_up",
    )(places, *rows, near, far, bias)


def ffn_down_back_kernel(blocks, cotangent, near, far, slope, out):
    chosen = pl.program_id(0) < pl.num_programs(0) // 2

    @pl.when(chosen)
    def _():
        out[...] = (dot_nt(cotangent[...], near[...]) * slope[...]).astype(BF)

    @pl.when(jnp.logical_not(chosen))
    def _():
        out[...] = (dot_nt(cotangent[...], far[...]) * slope[...]).astype(BF)


def ffn_down_back(cotangent, weight, slope, blocks):
    near, far = weight
    m, k = cotangent.shape
    count = blocks.shape[0]
    half = count // 2
    size = near.shape[0] // half
    natural = pl.BlockSpec((m, size), lambda j, blocks: (0, blocks[j]))
    return pl.pallas_call(
        ffn_down_back_kernel,
        grid_spec=pltpu.PrefetchScalarGridSpec(
            num_scalar_prefetch=1,
            grid=(count,),
            in_specs=[
                pl.BlockSpec((m, k), lambda j, *_: (0, 0)),
                pl.BlockSpec((size, k), lambda j, *_: (jnp.minimum(j, half - 1), 0)),
                pl.BlockSpec((size, k), lambda j, *_: (jnp.maximum(j - half, 0), 0)),
                natural,
            ],
            out_specs=natural,
        ),
        out_shape=jax.ShapeDtypeStruct((m, count * size), BF),
        name="ffn_down_back",
    )(blocks, cotangent, near, far, slope)


def memory_kernel(x0, x1, k0, k1, v0, v1, bias, keys, values):
    keys[...] = (dot_nn(x0[...], k0[...]) + dot_nn(x1[...], k1[...])).astype(BF)
    total = dot_nn(x0[...], v0[...]) + dot_nn(x1[...], v1[...])
    values[...] = (total + bias[...]).astype(BF)


def memory_project(rows, weights, key_pick, value_pick, bias, block):
    near, far = weights
    m, h = rows[0].shape
    n = near.shape[2]
    once = pl.Buffered(1)
    return pl.pallas_call(
        memory_kernel,
        grid=(m // block,),
        in_specs=[pl.BlockSpec((block, h), lambda i: (i, 0))] * 2
        + [stacked(near, key_pick, pipeline_mode=once)] * 2
        + [stacked(near, value_pick, pipeline_mode=once)] * 2
        + [pl.BlockSpec((1, n), lambda i: (0, 0))],
        out_specs=[pl.BlockSpec((block, n), lambda i: (i, 0))] * 2,
        out_shape=[jax.ShapeDtypeStruct((m, n), BF)] * 2,
        name="memory_project",
    )(*rows, near, far, near, far, bias)


def add_split_kernel(*refs):
    count = len(refs) // 6
    for i in range(count):
        keep_s, got_s, keep_k, got_k = refs[4 * i : 4 * i + 4]
        send, keep = refs[4 * count + 2 * i : 4 * count + 2 * i + 2]
        send[...] = (keep_s[...].astype(F32) + got_s[...].astype(F32)).astype(BF)
        keep[...] = (keep_k[...].astype(F32) + got_k[...].astype(F32)).astype(BF)


def add_split(parts):
    in_specs, out_specs, shapes, values = [], [], [], []
    for keep, got, first, count, low in parts:
        _, blocks, rows, n = keep.shape

        def spec(value, first=first, low=low, rows=rows, n=n):
            def index(i, j):
                high, rest = j >> low, j & ((1 << low) - 1)
                return first + i, (high << (low + 1)) | (value << low) | rest, 0, 0

            return pl.BlockSpec((None, None, rows, n), index)

        in_specs += [spec(1), spec(1), spec(0), spec(0)]
        values += [keep, got, keep, got]
        out_specs += [pl.BlockSpec((None, None, rows, n), lambda i, j: (i, j, 0, 0))] * 2
        shapes += [jax.ShapeDtypeStruct((count, blocks // 2, rows, n), BF)] * 2
    found = pl.pallas_call(
        add_split_kernel,
        grid=shapes[0].shape[:2],
        in_specs=in_specs,
        out_specs=out_specs,
        out_shape=shapes,
        name="add_split",
    )(*values)
    return found[0::2], found[1::2]


class Plan:
    def __init__(self):
        self.wide = lax.axis_size("wide")
        self.narrow = lax.axis_size("narrow")
        self.count = self.wide * self.narrow
        self.w = lax.axis_index("wide")
        self.z = lax.axis_index("narrow")
        self.me = self.w * self.narrow + self.z
        bits = self.wide.bit_length() - 1
        rest = [1 << b for b in range(1, bits)]
        half = len(rest) // 2
        self.core = self.narrow
        xs = [m * self.narrow for m in rest[:half]]
        ys = [m * self.narrow for m in rest[half:]]
        self.across = sorted([*xs, *ys], reverse=True)
        self.routes = ([*xs, *ys], [*ys, *xs])
        self.zs = [1 << b for b in range(self.narrow.bit_length() - 1)]
        self.order = [r for r in range(self.wide) if r % 2 == 0] + [
            r for r in range(self.wide) if r % 2 == 1
        ]

    def bit(self, index, mask):
        return (index // mask) % 2

    def step(self, stream, after=None, during=None):
        sends = [value for value, _ in stream.sends]
        if after is not None:
            sends, _ = lax.optimization_barrier((sends, after))
        got = [
            lax.ppermute(v, AXES, [(i, i ^ m) for i in range(self.count)])
            for v, (_, m) in zip(sends, stream.sends)
        ]
        if during is not None:
            got, during = lax.optimization_barrier((got, during))
        stream.feed(got)
        return got if during is None else (got, during)

    def across_steps(self, stream, after, during):
        for _ in self.across[1:]:
            after, during = self.step(stream, after, during)
        return after, during

    def finish(self, stream):
        while stream.result is None:
            self.step(stream)

    def relative(self, rows):
        size = rows.shape[1] // self.wide
        pieces = [
            lax.dynamic_slice_in_dim(rows, (jnp.int32(r) ^ self.w) * size, size, axis=1)
            for r in self.order
        ]
        half = self.wide // 2
        return jnp.concatenate(pieces[:half], axis=1), jnp.concatenate(pieces[half:], axis=1)

    def natural(self, rows):
        size = rows.shape[1] // self.wide
        pieces = []
        for i in range(self.wide):
            r = jnp.int32(i) ^ self.w
            place = (r % 2) * (self.wide // 2) + r // 2
            pieces.append(lax.dynamic_slice_in_dim(rows, place * size, size, axis=1))
        return jnp.concatenate(pieces, axis=1)

    def places(self):
        r = lax.iota(jnp.int32, self.wide) ^ self.w
        return (r % 2) * (self.wide // 2) + r // 2

    def blocks(self):
        return jnp.array(self.order, jnp.int32) ^ self.w

    def gather(self, part, split, join):
        k, rows, n = part.shape
        have = part.reshape(k, 1, rows, n)
        for mask in reversed(self.zs):
            (other,) = yield [(have, mask)]
            low = self.bit(self.z, mask) == 0
            have = jnp.stack(
                [jnp.where(low, have, other), jnp.where(low, other, have)], axis=2
            ).reshape(k, -1, rows, n)
        sets = [piece for piece in split(have.reshape(k, -1, n))]
        bits = len(self.across)
        for step in range(bits):
            got = yield [(s, route[step]) for s, route in zip(sets, self.routes)]
            sets = [jnp.stack([s, g]) for s, g in zip(sets, got)]
        whole = []
        for s, route in zip(sets, self.routes):
            axes = [list(reversed(route)).index(mask) for mask in self.across]
            s = jnp.transpose(s, [bits, *axes, bits + 1, bits + 2])
            whole.append(s.reshape(s.shape[0], -1, s.shape[-1]))
        near = join(*whole)
        (far,) = yield [(near, self.core)]
        return near, far

    def scatter(self, lefts, rights, products):
        keep, send = stack_grads(lefts, rights, products)
        (got,) = yield [(send, self.core)]
        count, r, n = keep.shape
        bits = len(self.across)
        shape = (count, 1 << bits, r >> bits, n)
        keep, got = keep.reshape(shape), got.reshape(shape)
        pairs = [(keep, got, 0, count // 2), (keep, got, count // 2, count // 2)]
        lefts = [list(self.across) for _ in pairs]
        for step in reversed(range(bits)):
            masks, parts = [], []
            for i, pair in enumerate(pairs):
                mask = self.routes[i][step]
                axis = lefts[i].index(mask)
                parts.append((*pair, len(lefts[i]) - 1 - axis))
                lefts[i].pop(axis)
                masks.append(mask)
            sends, keeps = add_split(parts)
            gots = yield list(zip(sends, masks))
            pairs = [(k, g, 0, count // 2) for k, g in zip(keeps, gots)]
        acc = jnp.concatenate([k.astype(F32) + g.astype(F32) for k, g, _, _ in pairs], axis=0)
        own = (r >> bits) // self.narrow
        acc = acc.reshape((count,) + (2,) * len(self.zs) + (own, n))
        for mask in self.zs:
            axis = len(acc.shape) - 3
            place = self.bit(self.z, mask)
            send = lax.dynamic_index_in_dim(acc, 1 - place, axis, keepdims=False).astype(BF)
            acc = lax.dynamic_index_in_dim(acc, place, axis, keepdims=False)
            (got,) = yield [(send, mask)]
            acc = acc + got.astype(F32)
        return acc

    def gather_small(self, vector):
        n = vector.shape[0]
        have = vector.reshape(1, n // 128, 128)
        for mask in [1 << b for b in range(self.count.bit_length() - 1)]:
            (other,) = yield [(have, mask)]
            low = self.bit(self.me, mask) == 0
            have = jnp.concatenate(
                [jnp.where(low, have, other), jnp.where(low, other, have)], axis=0
            )
        return have.reshape(self.count, n)

    def scatter_small(self, table):
        n = table.shape[1]
        have = table.reshape(self.count, n // 128, 128)
        for mask in [1 << b for b in reversed(range(self.count.bit_length() - 1))]:
            place = self.bit(self.me, mask)
            keep = lax.dynamic_slice_in_dim(have, place * mask, mask, axis=0)
            send = lax.dynamic_slice_in_dim(have, (1 - place) * mask, mask, axis=0)
            (got,) = yield [(send, mask)]
            have = keep + got
        return have.reshape(n)


class Stream:
    def __init__(self, steps):
        self.steps, self.result = steps, None
        self.sends = next(steps)

    def values(self):
        return [value for value, _ in self.sends]

    def replace(self, values):
        self.sends = [(v, mask) for v, (_, mask) in zip(values, self.sends)]

    def feed(self, got):
        try:
            self.sends = self.steps.send(list(got))
        except StopIteration as end:
            self.result = end.value


def pad_lanes(table):
    return jnp.pad(table, ((0, 0), (0, -table.shape[1] % 1024)))


def local(
    inputs,
    memory,
    mem_lengths,
    self_qkv,
    self_out,
    self_bias,
    self_gain,
    cross_qkv,
    cross_out,
    cross_bias,
    cross_gain,
    ffn_in,
    ffn_out,
    ffn_bias_in,
    ffn_bias_out,
    ffn_gain,
    out_grad,
):
    plan = Plan()
    scaling = HD ** (-0.5)
    item_count, mem_slots, model_width = memory.shape
    row_count = inputs.shape[0]
    pairs = model_width // PAIR
    paired = plan.wide == pairs
    place = plan.places() if paired else lax.iota(jnp.int32, pairs)

    def context_back(rows, weights):
        if paired:
            here = lax.iota(jnp.int32, plan.wide)
            return back_natural([rows], weights, [3], here, row_count, BF)
        return plan.natural(backward(rows, (weights[0][3], weights[1][3]))).astype(BF)

    def to_relative(context):
        half = model_width // 2
        return (context[:, :half], context[:, half:]) if paired else plan.relative(context)

    def back(lefts, weights, picks, rows, dtype=F32):
        if (model_width // plan.wide) % 128 == 0:
            return back_natural(lefts, weights, picks, plan.blocks(), rows, dtype)
        total = 0.0
        for i, left in enumerate(lefts):
            near, far = weights if picks is None else (weights[0][picks[i]], weights[1][picks[i]])
            total = total + backward(left, (near, far))
        return plan.natural(total).astype(dtype)

    def forward(rows, weight):
        return project(rows[0], weight[0]) + project(rows[1], weight[1])

    def backward(rows, weight):
        return jnp.concatenate(
            [project_back(rows, weight[0]), project_back(rows, weight[1])], axis=1
        )


    def add_norm(branch, residual, gain, shift):
        if (model_width // plan.wide) % 128 == 0:
            return norm(branch, residual, gain[None], shift[None], plan.blocks())
        pre = residual.astype(F32) + branch
        out = layer_norm(pre, gain, shift)
        return pre, out, plan.relative(out.astype(BF))


    share, hidden_share = self_gain.shape[0], ffn_bias_in.shape[0]
    small_rows = jnp.concatenate(
        [self_bias, self_gain[None], cross_bias, cross_gain[None], ffn_bias_out, ffn_gain[None]],
        axis=0,
    )
    vector_count = small_rows.shape[0]
    small = Stream(
        plan.gather_small(
            pad_lanes(jnp.concatenate([small_rows.reshape(1, -1), ffn_bias_in[None]], axis=1))[0]
        )
    )

    def four(have):
        return have[:2], have[2:]

    def each(a, b):
        return jnp.concatenate([a, b], axis=0)

    def columns(have):
        half = have.shape[-1] // 2
        return have[..., :half], have[..., half:]

    def one(a, b):
        return jnp.concatenate([a[0], b[0]], axis=1)

    selfs = Stream(
        plan.gather(jnp.concatenate([self_qkv, self_out[None]], axis=0), four, each)
    )
    crosses = Stream(
        plan.gather(jnp.concatenate([cross_qkv, cross_out[None]], axis=0), four, each)
    )
    fins = Stream(plan.gather(ffn_in[None], columns, one))
    fouts = Stream(plan.gather(ffn_out[None], columns, one))
    after = plan.step(small)
    for _ in plan.zs:
        after = (plan.step(selfs, after), plan.step(small))
    after = (after, plan.step(small))
    for _ in plan.across[2:]:
        after = plan.step(selfs, after)
    last = plan.step(selfs, after)
    plan.finish(small)
    cross_z = plan.step(crosses, after)
    last = plan.step(selfs, (last, cross_z, small.result))
    for _ in plan.zs[1:]:
        cross_z = plan.step(crosses, cross_z)
    self_core = plan.step(selfs, cross_z)
    fin_z = plan.step(fins, cross_z)
    last, fin_z = plan.step(crosses, last, fin_z)
    table = small.result.astype(F32)
    vectors = table[:, : vector_count * share].reshape(plan.count, vector_count, share)
    vectors = jnp.swapaxes(vectors, 0, 1).reshape(vector_count, model_width)
    sbias, sgain, cbias, cgain, fbout, fgain = (
        vectors[:4],
        vectors[4],
        vectors[5:9],
        vectors[9],
        vectors[10:12],
        vectors[12],
    )
    fbin = table[:, vector_count * share :][:, :hidden_share].reshape(-1)

    x_rel = plan.relative(inputs)
    no_bias = jnp.zeros((model_width,), F32)
    qkv = stack_project(
        x_rel,
        selfs.result,
        0,
        jnp.stack([sbias[0], no_bias, sbias[1]])[:, None],
        (scaling, 1.0, 1.0),
        BF,
    )
    self_ctx, self_lse = self_attend(qkv, item_count, place)
    self_rel = to_relative(self_ctx)
    branch = stack_project(self_rel, selfs.result, 3, sbias[None, 2:3], (1.0,), F32)[0]
    after = (last, self_core, fin_z)
    for _ in plan.zs[1:]:
        fin_z = plan.step(fins, fin_z)
    fout_z = plan.step(fouts, fin_z)
    last, (branch, fout_z) = plan.across_steps(crosses, after, (branch, fout_z))
    first_pre, first, first_rel = add_norm(branch, inputs, sgain, sbias[3])
    cross_core = plan.step(crosses)
    for _ in plan.zs[1:]:
        fout_z = plan.step(fouts, fout_z)
    last, _ = plan.step(fins, last, (cross_core, fout_z))

    queries_two = stack_project(first_rel, crosses.result, 0, cbias[None, 0:1], (scaling,), BF)[0]
    mem_rel = plan.relative(memory.reshape(item_count * mem_slots, model_width))
    mem_keys, mem_values = memory_project(mem_rel, crosses.result, 1, 2, cbias[1:2], 512)
    cross_out = ()
    for item in range(item_count):
        cross_out = cross_attend(
            queries_two, mem_keys, mem_values, mem_lengths, place, item, cross_out
        )
        if item == 0:
            last, cross_out = plan.across_steps(fins, last, cross_out)
    fin_core = plan.step(fins)
    last, (cross_out, _) = plan.step(fouts, last, (cross_out, fin_core))
    cross_ctx, cross_lse = cross_out
    fin = fins.result
    cross_rel = to_relative(cross_ctx)
    branch = stack_project(cross_rel, crosses.result, 3, cbias[None, 2:3], (1.0,), F32)[0]
    second_pre, second, second_rel = add_norm(branch, first, cgain, cbias[3])

    places = plan.places()
    hidden, slope = ffn_up(second_rel, fin, fbin[None], places)
    _, (hidden, slope) = plan.across_steps(fouts, last, (hidden, slope))
    half = hidden.shape[1] // 2
    hidden_rel = (hidden[:, :half], hidden[:, half:])
    plan.step(fouts)
    fout = fouts.result
    third_pre = second + (forward(hidden_rel, fout) + fbout[0])

    layer_out, d_third, e_three, third_sums = norm_back(
        [out_grad], third_pre, fgain[None], fbout[1:2]
    )
    half = model_width // 2
    to_fout = Stream(
        plan.scatter([hidden_rel], [e_three], [(0, 0, 0, half), (0, 0, half, half)])
    )
    d_pre = ffn_down_back(e_three, fout, slope, plan.blocks())
    _, d_pre = plan.step(to_fout, None, d_pre)
    half = d_pre.shape[1] // 2
    to_fin = Stream(plan.scatter([second_rel], [d_pre], [(0, 0, 0, half), (0, 0, half, half)]))
    d_hidden = back([d_pre], fin, None, row_count)
    last, (d_hidden, fin_sends) = plan.step(to_fout, None, (d_hidden, to_fin.values()))
    to_fin.replace(fin_sends)
    fin_core = plan.step(to_fin)

    d_second_pre, e_two, second_sums = norm_back([d_third, d_hidden], second_pre, cgain[None])
    d_cross_ctx = context_back(e_two, crosses.result)
    cross_back = ()
    for item in range(item_count):
        cross_back = cross_attend_back(
            queries_two, mem_keys, mem_values, cross_lse, d_cross_ctx, mem_lengths, place,
            item, cross_back,
        )
        if item == 0:
            last, (cross_back, _) = plan.across_steps(to_fout, last, (cross_back, fin_core))
    dq_scaled, dk_flat, dv_flat = cross_back
    to_cross = Stream(
        plan.scatter(
            [first_rel, mem_rel, cross_rel],
            [dq_scaled, dk_flat, dv_flat, e_two],
            [(0, 0, 0, model_width), (1, 1, 0, model_width), (1, 2, 0, model_width), (2, 3, 0, model_width)],
        )
    )
    d_queries = back([dq_scaled], crosses.result, [0], row_count)
    for _ in plan.zs[1:]:
        fout_last = plan.step(to_fout)
    last, (d_queries, _, cross_sends) = plan.step(
        to_fin, last, (d_queries, fout_last, to_cross.values())
    )
    to_cross.replace(cross_sends)
    cross_core = plan.step(to_cross)
    fout_last = plan.step(to_fout)

    d_first_pre, e_one, first_sums = norm_back([d_second_pre, d_queries], first_pre, sgain[None])
    d_self_ctx = context_back(e_one, selfs.result)
    last, (d_self_ctx, *_) = plan.across_steps(
        to_fin, last, (d_self_ctx, cross_core, fout_last)
    )
    dq_self, dk_self, dv_self = self_attend_back(qkv, self_lse, d_self_ctx, item_count, place)
    to_self = Stream(
        plan.scatter(
            [x_rel, self_rel],
            [dq_self, dk_self, dv_self, e_one],
            [(0, 0, 0, model_width), (0, 1, 0, model_width), (0, 2, 0, model_width), (1, 3, 0, model_width)],
        )
    )
    for _ in plan.zs[1:]:
        fin_last = plan.step(to_fin)
    last, (_, self_sends) = plan.step(to_cross, last, (fin_last, to_self.values()))
    to_self.replace(self_sends)
    self_core = plan.step(to_self)
    fin_last = plan.step(to_fin)
    late, _ = lax.optimization_barrier(((dq_self, dk_self, dv_self), last))
    d_inputs = back(late, selfs.result, [0, 1, 2], row_count)
    last, (d_inputs, *_) = plan.across_steps(
        to_cross, last, (d_inputs, self_core, fin_last)
    )
    input_grad = d_first_pre + d_inputs
    late, _ = lax.optimization_barrier(((dk_flat, dv_flat), last))
    memory_grad = back(late, crosses.result, [1, 2], 512).reshape(memory.shape)
    for _ in plan.zs[1:]:
        cross_last = plan.step(to_cross)
    last, _ = plan.step(to_self, last, (memory_grad, cross_last))
    cross_last = plan.step(to_cross)
    last, _ = plan.across_steps(to_self, last, cross_last)
    sums, _ = lax.optimization_barrier(((dq_self, dv_self, dq_scaled, dv_flat, d_pre), last))
    sum_dq, sum_dv, sum_dq2, sum_dv2, sum_hidden = [column_sums(v) for v in sums]
    grads = jnp.concatenate(
        [
            sum_dq[None],
            sum_dv[None],
            first_sums[:3],
            sum_dq2[None],
            sum_dv2[None],
            second_sums[:3],
            third_sums[:3],
        ],
        axis=0,
    )
    grads = jnp.swapaxes(grads.reshape(vector_count, plan.count, share), 0, 1)
    to_small = Stream(
        plan.scatter_small(
            pad_lanes(
                jnp.concatenate(
                    [grads.reshape(plan.count, -1), sum_hidden.reshape(plan.count, -1)], axis=1
                )
            )
        )
    )
    for _ in plan.zs[1:]:
        plan.step(to_small)
        plan.step(to_small)
        plan.step(to_small, plan.step(to_self))
    for stream in (to_self, to_cross, to_fin, to_fout):
        plan.finish(stream)
    plan.finish(to_small)
    small_sums = to_small.result
    found = small_sums[: vector_count * share].reshape(vector_count, share)
    g_hidden = small_sums[vector_count * share :][:hidden_share]
    g_self, g_cross = to_self.result, to_cross.result
    g_fout = jnp.concatenate([to_fout.result[0], to_fout.result[1]], axis=1)
    g_fin = jnp.concatenate([to_fin.result[0], to_fin.result[1]], axis=1)
    return (
        layer_out,
        input_grad,
        memory_grad,
        g_self[:3],
        g_self[3],
        found[:4],
        found[4],
        g_cross[:3],
        g_cross[3],
        found[5:9],
        found[9],
        g_fin,
        g_fout,
        g_hidden,
        found[10:12],
        found[12],
    )


def solution(mesh):
    both = ("wide", "narrow")
    placed = (
        P(both, None),
        P(both, None, None),
        P(both),
        P(None, both, None),
        P(both, None),
        P(None, both),
        P(both),
        P(None, both, None),
        P(both, None),
        P(None, both),
        P(both),
        P(both, None),
        P(both, None),
        P(both),
        P(None, both),
        P(both),
        P(both, None),
    )
    return jax.shard_map(
        local,
        mesh=mesh,
        in_specs=placed,
        out_specs=(
            P(both, None),
            P(both, None),
            P(both, None, None),
            P(None, both, None),
            P(both, None),
            P(None, both),
            P(both),
            P(None, both, None),
            P(both, None),
            P(None, both),
            P(both),
            P(both, None),
            P(both, None),
            P(both),
            P(None, both),
            P(both),
        ),
        check_vma=False,
    )
```

```python
import functools
import math

import jax
import jax.numpy as jnp
from jax import lax
from jax.experimental import pallas as pl
from jax.experimental.pallas import tpu as pltpu
from jax.sharding import PartitionSpec as P

HD = 64
EPSILON = 1e-05
MASKED = -1e30
AXES = ("wide", "narrow")
BF = jnp.bfloat16
F32 = jnp.float32


def project(left_rows, weight):
    return jnp.dot(left_rows, weight, preferred_element_type=F32)


def project_back(gradient, weight):
    return lax.dot_general(gradient, weight, (((1,), (1,)), ((), ())), preferred_element_type=F32)


def weight_grad(left_rows, gradient):
    return lax.dot_general(left_rows, gradient, (((0,), (0,)), ((), ())), preferred_element_type=F32)


def column_sums(gradient):
    return jnp.sum(gradient.astype(F32), axis=0)


def layer_norm(hidden, gain_row, shift_row):
    average = jnp.mean(hidden, axis=-1, keepdims=True)
    centred = hidden - average
    variance = jnp.mean(centred * centred, axis=-1, keepdims=True)
    return centred * lax.rsqrt(variance + EPSILON) * gain_row + shift_row


def pair_stack(rows):
    lane = lax.broadcasted_iota(jnp.int32, rows.shape, 1)
    zero = jnp.zeros_like(rows)
    return jnp.concatenate(
        [jnp.where(lane < HD, rows, zero), jnp.where(lane >= HD, rows, zero)], axis=0
    )


def pair_merge(stacked):
    t = stacked.shape[0] // 2
    lane = lax.broadcasted_iota(jnp.int32, (t, 2 * HD), 1)
    return jnp.where(lane < HD, stacked[:t], stacked[t:])


def dot_nt(a, b):
    return lax.dot_general(a, b, (((1,), (1,)), ((), ())), preferred_element_type=F32)


def dot_tn(a, b):
    return lax.dot_general(a, b, (((0,), (0,)), ((), ())), preferred_element_type=F32)


def dot_nn(a, b):
    return lax.dot_general(a, b, (((1,), (0,)), ((), ())), preferred_element_type=F32)


def masked_scores(k, qs, length):
    scores = dot_nt(k, qs)
    slot = lax.broadcasted_iota(jnp.int32, scores.shape, 0)
    if length is None:
        seen = lax.broadcasted_iota(jnp.int32, scores.shape, 1) % (scores.shape[1] // 2)
        return jnp.where(slot <= seen, scores, MASKED)
    return jnp.where(slot < length, scores, MASKED)


def attend_pair(q, k, v, length):
    scores = masked_scores(k, pair_stack(q), length)
    top = jnp.max(scores, axis=0, keepdims=True)
    weights = jnp.exp(scores - top)
    total = jnp.sum(weights, axis=0, keepdims=True)
    chances = (weights * (1.0 / total)).astype(BF)
    return pair_merge(dot_tn(chances, v)).astype(BF), top + jnp.log(total)


def attend_pair_back(q, k, v, lse, d_out, length):
    qs, ds_out = pair_stack(q), pair_stack(d_out)
    chances = jnp.exp(masked_scores(k, qs, length) - lse)
    d_chances = dot_nt(v, ds_out)
    row = jnp.sum(d_chances * chances, axis=0, keepdims=True)
    d_scores = (chances * (d_chances - row)).astype(BF)
    d_q = pair_merge(dot_tn(d_scores, k)).astype(BF)
    d_k = dot_nn(d_scores, qs).astype(BF)
    d_v = dot_nn(chances.astype(BF), ds_out).astype(BF)
    return d_q, d_k, d_v


PAIR = 2 * HD
UNROLL = 2


def lane_block(at):
    return pl.ds(pl.multiple_of(at * PAIR, PAIR), PAIR)


def cross_kernel(place, length, q, k, v, *refs):
    out, lse = refs[-2:]
    for u in range(UNROLL):
        cut = slice(u * PAIR, (u + 1) * PAIR)
        found, lse[0, u] = attend_pair(q[:, cut], k[:, cut], v[:, cut], length[0])
        out[:, lane_block(place[pl.program_id(0) * UNROLL + u])] = found


def cross_back_kernel(place, length, q, k, v, lse, d_out, *refs):
    d_q, d_k, d_v = refs[-3:]
    for u in range(UNROLL):
        cut = slice(u * PAIR, (u + 1) * PAIR)
        cotangent = d_out[:, lane_block(place[pl.program_id(0) * UNROLL + u])]
        found = attend_pair_back(
            q[:, cut], k[:, cut], v[:, cut], lse[0, u], cotangent, length[0]
        )
        d_q[:, cut] = found[0] * jnp.asarray(HD**-0.5, BF)
        d_k[:, cut] = found[1]
        d_v[:, cut] = found[2]


def cross_call(kernel, q, k, lengths, place, item, values, in_specs, out_specs, out_shape, so_far):
    return pl.pallas_call(
        kernel,
        grid_spec=pltpu.PrefetchScalarGridSpec(
            num_scalar_prefetch=2,
            grid=(q.shape[1] // PAIR // UNROLL,),
            in_specs=in_specs + [pl.BlockSpec(memory_space=pl.ANY)] * len(so_far),
            out_specs=out_specs,
        ),
        out_shape=out_shape,
        input_output_aliases={2 + len(values) + i: i for i in range(len(so_far))},
        name="cross_attend",
    )(place, lax.slice_in_dim(lengths, item, item + 1), *values, *so_far)


def cross_specs(q, k, items, item):
    t, s, n = q.shape[0] // items, k.shape[0] // items, PAIR * UNROLL
    rows = pl.BlockSpec((t, n), lambda j, *_: (item, j))
    slots = pl.BlockSpec((s, n), lambda j, *_: (item, j))
    placed = pl.BlockSpec((t, q.shape[1]), lambda j, *_: (item, 0))
    lse = pl.BlockSpec((1, UNROLL, 1, 2 * t), lambda j, *_: (item, j, 0, 0))
    return rows, slots, placed, lse


def cross_attend(q, k, v, lengths, place, item, so_far):
    items = lengths.shape[0]
    rows, slots, placed, lse = cross_specs(q, k, items, item)
    out_shape = [
        jax.ShapeDtypeStruct(q.shape, BF),
        jax.ShapeDtypeStruct((items, q.shape[1] // PAIR, 1, 2 * q.shape[0] // items), F32),
    ]
    return cross_call(
        cross_kernel, q, k, lengths, place, item, (q, k, v),
        [rows, slots, slots], [placed, lse], out_shape, so_far,
    )


def cross_attend_back(q, k, v, lse, d_out, lengths, place, item, so_far):
    rows, slots, placed, lse_spec = cross_specs(q, k, lengths.shape[0], item)
    out_shape = [jax.ShapeDtypeStruct(a.shape, BF) for a in (q, k, k)]
    return cross_call(
        cross_back_kernel, q, k, lengths, place, item, (q, k, v, lse, d_out),
        [rows, slots, slots, lse_spec, placed], [rows, slots, slots], out_shape, so_far,
    )


def lanes(ref, at):
    return ref[:, pl.ds(pl.multiple_of(at * PAIR, PAIR), PAIR)]


def self_kernel(place, q, k, v, out, lse):
    for j in range(q.shape[1] // PAIR):
        cut = slice(j * PAIR, (j + 1) * PAIR)
        found, lse[0, j] = attend_pair(q[:, cut], k[:, cut], v[:, cut], None)
        out[:, pl.ds(pl.multiple_of(place[j] * PAIR, PAIR), PAIR)] = found


def self_back_kernel(place, q, k, v, lse, d_out, d_q, d_k, d_v):
    for j in range(q.shape[1] // PAIR):
        cut = slice(j * PAIR, (j + 1) * PAIR)
        found = attend_pair_back(
            q[:, cut], k[:, cut], v[:, cut], lse[0, j], lanes(d_out, place[j]), None
        )
        d_q[:, cut] = found[0] * jnp.asarray(HD**-0.5, BF)
        d_k[:, cut] = found[1]
        d_v[:, cut] = found[2]


def self_attend(qkv, items, place):
    _, rows, width = qkv.shape
    t = rows // items

    def part(i):
        return pl.BlockSpec((None, t, width), lambda b, *_: (i, b, 0))

    lse = pl.BlockSpec((1, width // PAIR, 1, 2 * t), lambda b, *_: (b, 0, 0, 0))
    return pl.pallas_call(
        self_kernel,
        grid_spec=pltpu.PrefetchScalarGridSpec(
            num_scalar_prefetch=1,
            grid=(items,),
            in_specs=[part(0), part(1), part(2)],
            out_specs=[pl.BlockSpec((t, width), lambda b, *_: (b, 0)), lse],
        ),
        out_shape=[
            jax.ShapeDtypeStruct((rows, width), BF),
            jax.ShapeDtypeStruct((items, width // PAIR, 1, 2 * t), F32),
        ],
        name="self_attend",
    )(place, qkv, qkv, qkv)


def self_attend_back(qkv, lse, d_out, items, place):
    _, m, width = qkv.shape
    t = m // items

    def part(i):
        return pl.BlockSpec((None, t, width), lambda b, *_: (i, b, 0))

    rows = pl.BlockSpec((t, width), lambda b, *_: (b, 0))
    lse_spec = pl.BlockSpec((1, width // PAIR, 1, 2 * t), lambda b, *_: (b, 0, 0, 0))
    return pl.pallas_call(
        self_back_kernel,
        grid_spec=pltpu.PrefetchScalarGridSpec(
            num_scalar_prefetch=1,
            grid=(items,),
            in_specs=[part(0), part(1), part(2), lse_spec, rows],
            out_specs=[rows] * 3,
        ),
        out_shape=[jax.ShapeDtypeStruct((m, width), BF)] * 3,
        name="self_attend_back",
    )(place, qkv, qkv, qkv, lse, d_out)


def row_of(row):
    return pl.BlockSpec((None, 1, row[0].shape[2]), lambda *_: (row[1], 0, 0))


def stacked(array, i, **kw):
    return pl.BlockSpec((None,) + array.shape[1:], lambda *_: (i, 0, 0), **kw)


def project_kernel(scales, x0, x1, near, far, bias, out):
    total = dot_nn(x0[...], near[...]) + dot_nn(x1[...], far[...]) + bias[...]
    j = pl.program_id(0)
    scale = scales[0]
    for i in range(1, len(scales)):
        scale = jnp.where(j == i, scales[i], scale)
    out[...] = (total * scale).astype(out.dtype)


def stack_project(rows, weights, first, bias, scales, dtype):
    near, far = weights
    bias, start = bias
    m, h = rows[0].shape
    n = near.shape[2]
    count = len(scales)
    whole = pl.BlockSpec((m, h), lambda j: (0, 0))
    weight = pl.BlockSpec((None, h, n), lambda j: (first + j, 0, 0))
    return pl.pallas_call(
        functools.partial(project_kernel, scales),
        grid=(count,),
        in_specs=[whole, whole, weight, weight, pl.BlockSpec((None, 1, n), lambda j: (start + j, 0, 0))],
        out_specs=pl.BlockSpec((None, m, n), lambda j: (j, 0, 0)),
        out_shape=jax.ShapeDtypeStruct((count, m, n), dtype),
        name="stack_project",
    )(*rows, near, far, bias)


def grads_kernel(products, *refs):
    ins, (keep, send) = refs[:-2], refs[-2:]
    for i, (left, right, start) in enumerate(products):

        @pl.when(pl.program_id(0) == i)
        def _():
            to = ins[right][:, start : start + keep.shape[1]]
            keep[...] = dot_tn(ins[left][...], to).astype(BF)
            send[...] = dot_tn(ins[left + 1][...], to).astype(BF)


def stack_grads(lefts, rights, products):
    arrays = [half for left in lefts for half in left] + list(rights)
    n = products[0][3]
    r = lefts[0][0].shape[1]
    table = [(2 * left, 2 * len(lefts) + right, start) for left, right, start, _ in products]
    out = pl.BlockSpec((None, r, n), lambda i: (i, 0, 0))
    shape = jax.ShapeDtypeStruct((len(products), r, n), BF)
    return pl.pallas_call(
        functools.partial(grads_kernel, table),
        grid=(len(products),),
        in_specs=[
            pl.BlockSpec(a.shape, lambda i: (0, 0), pipeline_mode=pl.Buffered(1)) for a in arrays
        ],
        out_specs=[out, out],
        out_shape=[shape, shape],
        name="stack_grads",
    )(*arrays)


def back_kernel(blocks, *refs):
    count = (len(refs) - 1) // 3
    out = refs[-1]
    size = out.shape[1] // blocks.shape[0]
    for half in range(2):
        total = dot_nt(refs[0][...], refs[count + half][...])
        for i in range(1, count):
            total = total + dot_nt(refs[i][...], refs[count + 2 * i + half][...])
        for i in range(total.shape[1] // size):
            to = blocks[half * (blocks.shape[0] // 2) + i]
            at = pl.ds(pl.multiple_of(to * size, 128), size)
            out[:, at] = total[:, i * size : (i + 1) * size].astype(out.dtype)


def back_natural(lefts, weights, picks, blocks, rows, dtype):
    m = lefts[0].shape[0]
    near, far = weights
    if picks is None:
        near, far, picks = near[None], far[None], [0]
    n = 2 * near.shape[1]
    in_specs = [pl.BlockSpec((rows, a.shape[1]), lambda i, *_: (i, 0)) for a in lefts]
    values = []
    for p in picks:
        in_specs += [stacked(near, p, pipeline_mode=pl.Buffered(1))] * 2
        values += [near, far]
    return pl.pallas_call(
        back_kernel,
        grid_spec=pltpu.PrefetchScalarGridSpec(
            num_scalar_prefetch=1,
            grid=(m // rows,),
            in_specs=in_specs,
            out_specs=pl.BlockSpec((rows, n), lambda i, *_: (i, 0)),
        ),
        out_shape=jax.ShapeDtypeStruct((m, n), dtype),
        name="back_natural",
    )(blocks, *lefts, *values)


def normed(hidden):
    centred = hidden - jnp.mean(hidden, axis=-1, keepdims=True)
    scale = lax.rsqrt(jnp.mean(centred * centred, axis=-1, keepdims=True) + EPSILON)
    return centred * scale, scale


def norm_kernel(blocks, branch, residual, gain, shift, pre, out, rel0, rel1):
    pre[...] = residual[...].astype(F32) + branch[...]
    out[...] = normed(pre[...])[0] * gain[...] + shift[...]
    half = blocks.shape[0] // 2
    size = out.shape[1] // blocks.shape[0]
    for i in range(2 * half):
        rel, at = (rel0, i) if i < half else (rel1, i - half)
        block = out[:, pl.ds(pl.multiple_of(blocks[i] * size, 128), size)]
        rel[:, at * size : (at + 1) * size] = block.astype(BF)


def norm(branch, residual, gain, shift, blocks):
    m, n = branch.shape
    rows = m // 2
    full = pl.BlockSpec((rows, n), lambda i, *_: (i, 0))
    halves = pl.BlockSpec((rows, n // 2), lambda i, *_: (i, 0))
    pre, out, rel0, rel1 = pl.pallas_call(
        norm_kernel,
        grid_spec=pltpu.PrefetchScalarGridSpec(
            num_scalar_prefetch=1,
            grid=(2,),
            in_specs=[full, full, row_of(gain), row_of(shift)],
            out_specs=[full, full, halves, halves],
        ),
        out_shape=[
            jax.ShapeDtypeStruct((m, n), F32),
            jax.ShapeDtypeStruct((m, n), F32),
            jax.ShapeDtypeStruct((m, n // 2), BF),
            jax.ShapeDtypeStruct((m, n // 2), BF),
        ],
        name="norm",
    )(blocks, branch, residual, gain[0], shift[0])
    return pre, out, (rel0, rel1)


def norm_back_kernel(count, *refs):
    pre, gain = refs[count : count + 2]
    d_pre, low, sums = refs[-3:]
    cotangent = refs[0][...].astype(F32)
    for ref in refs[1:count]:
        cotangent = cotangent + ref[...]
    z, scale = normed(pre[...])
    if len(refs) > count + 5:
        shift, out = refs[count + 2], refs[-4]
        out[...] = (z * gain[...] + shift[...]).astype(BF)
    inner = cotangent * gain[...]
    found = scale * (
        inner
        - jnp.mean(inner, axis=-1, keepdims=True)
        - z * jnp.mean(inner * z, axis=-1, keepdims=True)
    )
    d_pre[...] = found
    low[...] = found.astype(BF)

    @pl.when(pl.program_id(0) == 0)
    def _():
        sums[...] = jnp.zeros_like(sums)

    rows = [found.astype(BF).astype(F32), cotangent, cotangent * z]
    for i, value in enumerate(rows):
        sums[i : i + 1, :] += jnp.sum(value, axis=0, keepdims=True)


def norm_back(cotangents, pre, gain, shift=None):
    m, n = pre.shape
    rows = m // 2
    full = pl.BlockSpec((rows, n), lambda i: (i, 0))
    extra = [gain] if shift is None else [gain, shift]
    out_specs = [full, full, pl.BlockSpec((8, n), lambda i: (0, 0))]
    out_shape = [
        jax.ShapeDtypeStruct((m, n), F32),
        jax.ShapeDtypeStruct((m, n), BF),
        jax.ShapeDtypeStruct((8, n), F32),
    ]
    if shift is not None:
        out_specs, out_shape = [full] + out_specs, [jax.ShapeDtypeStruct((m, n), BF)] + out_shape
    return pl.pallas_call(
        functools.partial(norm_back_kernel, len(cotangents)),
        grid=(2,),
        in_specs=[full] * (len(cotangents) + 1) + [row_of(row) for row in extra],
        out_specs=out_specs,
        out_shape=out_shape,
        name="norm_back",
    )(*cotangents, pre, *[row[0] for row in extra])


def gelu_parts(u):
    half_erf = 0.5 * (1.0 + lax.erf(u * (0.5**0.5)))
    return u * half_erf, half_erf + u * jnp.exp(-0.5 * u * u) * (0.5 / math.pi) ** 0.5


def ffn_up_kernel(places, x0, x1, near, far, bias, hidden, slope):
    u = dot_nn(x0[...], near[...]) + dot_nn(x1[...], far[...]) + bias[...]
    value, slope[...] = gelu_parts(u)
    hidden[...] = value.astype(BF)


def ffn_up(rows, weight, bias, places):
    near, far = weight
    m, h = rows[0].shape
    n = near.shape[1]
    size = n // places.shape[0]
    whole = pl.BlockSpec((m, h), lambda j, *_: (0, 0))
    columns = pl.BlockSpec((h, size), lambda j, *_: (0, j))
    return pl.pallas_call(
        ffn_up_kernel,
        grid_spec=pltpu.PrefetchScalarGridSpec(
            num_scalar_prefetch=1,
            grid=(n // size,),
            in_specs=[whole, whole, columns, columns, pl.BlockSpec((1, size), lambda j, *_: (0, j))],
            out_specs=[
                pl.BlockSpec((m, size), lambda j, places: (0, places[j])),
                pl.BlockSpec((m, size), lambda j, places: (0, j)),
            ],
        ),
        out_shape=[jax.ShapeDtypeStruct((m, n), BF), jax.ShapeDtypeStruct((m, n), F32)],
        name="ffn_up",
    )(places, *rows, near, far, bias)


def ffn_down_back_kernel(blocks, cotangent, near, far, slope, out):
    chosen = pl.program_id(0) < pl.num_programs(0) // 2

    @pl.when(chosen)
    def _():
        out[...] = (dot_nt(cotangent[...], near[...]) * slope[...]).astype(BF)

    @pl.when(jnp.logical_not(chosen))
    def _():
        out[...] = (dot_nt(cotangent[...], far[...]) * slope[...]).astype(BF)


def ffn_down_back(cotangent, weight, slope, blocks):
    near, far = weight
    m, k = cotangent.shape
    count = blocks.shape[0]
    half = count // 2
    size = near.shape[0] // half
    natural = pl.BlockSpec((m, size), lambda j, blocks: (0, blocks[j]))
    return pl.pallas_call(
        ffn_down_back_kernel,
        grid_spec=pltpu.PrefetchScalarGridSpec(
            num_scalar_prefetch=1,
            grid=(count,),
            in_specs=[
                pl.BlockSpec((m, k), lambda j, *_: (0, 0)),
                pl.BlockSpec((size, k), lambda j, *_: (jnp.minimum(j, half - 1), 0)),
                pl.BlockSpec((size, k), lambda j, *_: (jnp.maximum(j - half, 0), 0)),
                natural,
            ],
            out_specs=natural,
        ),
        out_shape=jax.ShapeDtypeStruct((m, count * size), BF),
        name="ffn_down_back",
    )(blocks, cotangent, near, far, slope)


def memory_kernel(x0, x1, k0, k1, v0, v1, bias, keys, values):
    keys[...] = (dot_nn(x0[...], k0[...]) + dot_nn(x1[...], k1[...])).astype(BF)
    total = dot_nn(x0[...], v0[...]) + dot_nn(x1[...], v1[...])
    values[...] = (total + bias[...]).astype(BF)


def memory_project(rows, weights, key_pick, value_pick, bias, block):
    near, far = weights
    m, h = rows[0].shape
    n = near.shape[2]
    once = pl.Buffered(1)
    return pl.pallas_call(
        memory_kernel,
        grid=(m // block,),
        in_specs=[pl.BlockSpec((block, h), lambda i: (i, 0))] * 2
        + [stacked(near, key_pick, pipeline_mode=once)] * 2
        + [stacked(near, value_pick, pipeline_mode=once)] * 2
        + [row_of(bias)],
        out_specs=[pl.BlockSpec((block, n), lambda i: (i, 0))] * 2,
        out_shape=[jax.ShapeDtypeStruct((m, n), BF)] * 2,
        name="memory_project",
    )(*rows, near, far, near, far, bias[0])


def add_split_kernel(*refs):
    count = len(refs) // 6
    for i in range(count):
        keep_s, got_s, keep_k, got_k = refs[4 * i : 4 * i + 4]
        send, keep = refs[4 * count + 2 * i : 4 * count + 2 * i + 2]
        send[...] = (keep_s[...].astype(F32) + got_s[...].astype(F32)).astype(BF)
        keep[...] = (keep_k[...].astype(F32) + got_k[...].astype(F32)).astype(BF)


def add_split(parts):
    in_specs, out_specs, shapes, values = [], [], [], []
    for keep, got, first, count, low in parts:
        _, blocks, rows, n = keep.shape

        def spec(value, first=first, low=low, rows=rows, n=n):
            def index(i, j):
                high, rest = j >> low, j & ((1 << low) - 1)
                return first + i, (high << (low + 1)) | (value << low) | rest, 0, 0

            return pl.BlockSpec((None, None, rows, n), index)

        in_specs += [spec(1), spec(1), spec(0), spec(0)]
        values += [keep, got, keep, got]
        out_specs += [pl.BlockSpec((None, None, rows, n), lambda i, j: (i, j, 0, 0))] * 2
        shapes += [jax.ShapeDtypeStruct((count, blocks // 2, rows, n), BF)] * 2
    found = pl.pallas_call(
        add_split_kernel,
        grid=shapes[0].shape[:2],
        in_specs=in_specs,
        out_specs=out_specs,
        out_shape=shapes,
        name="add_split",
    )(*values)
    return found[0::2], found[1::2]


class Plan:
    def __init__(self):
        self.wide = lax.axis_size("wide")
        self.narrow = lax.axis_size("narrow")
        self.count = self.wide * self.narrow
        self.w = lax.axis_index("wide")
        self.z = lax.axis_index("narrow")
        self.me = self.w * self.narrow + self.z
        bits = self.wide.bit_length() - 1
        rest = [1 << b for b in range(1, bits)]
        half = len(rest) // 2
        self.core = self.narrow
        xs = [m * self.narrow for m in rest[:half]]
        ys = [m * self.narrow for m in rest[half:]]
        self.across = sorted([*xs, *ys], reverse=True)
        self.routes = ([*xs, *ys], [*ys, *xs])
        self.zs = [1 << b for b in range(self.narrow.bit_length() - 1)]
        self.order = [r for r in range(self.wide) if r % 2 == 0] + [
            r for r in range(self.wide) if r % 2 == 1
        ]

    def bit(self, index, mask):
        return (index // mask) % 2

    def step(self, stream, after=None, during=None):
        sends = [value for value, _ in stream.sends]
        if after is not None:
            sends, _ = lax.optimization_barrier((sends, after))
        got = [
            lax.ppermute(v, AXES, [(i, i ^ m) for i in range(self.count)])
            for v, (_, m) in zip(sends, stream.sends)
        ]
        if during is not None:
            got, during = lax.optimization_barrier((got, during))
        stream.feed(got)
        return got if during is None else (got, during)

    def across_steps(self, stream, after, during):
        for _ in self.across[1:]:
            after, during = self.step(stream, after, during)
        return after, during

    def finish(self, stream):
        while stream.result is None:
            self.step(stream)

    def relative(self, rows):
        size = rows.shape[1] // self.wide
        pieces = [
            lax.dynamic_slice_in_dim(rows, (jnp.int32(r) ^ self.w) * size, size, axis=1)
            for r in self.order
        ]
        half = self.wide // 2
        return jnp.concatenate(pieces[:half], axis=1), jnp.concatenate(pieces[half:], axis=1)

    def natural(self, rows):
        size = rows.shape[1] // self.wide
        pieces = []
        for i in range(self.wide):
            r = jnp.int32(i) ^ self.w
            place = (r % 2) * (self.wide // 2) + r // 2
            pieces.append(lax.dynamic_slice_in_dim(rows, place * size, size, axis=1))
        return jnp.concatenate(pieces, axis=1)

    def places(self):
        r = lax.iota(jnp.int32, self.wide) ^ self.w
        return (r % 2) * (self.wide // 2) + r // 2

    def blocks(self):
        return jnp.array(self.order, jnp.int32) ^ self.w

    def gather(self, part, split, join):
        k, rows, n = part.shape
        have = part.reshape(k, 1, rows, n)
        for mask in reversed(self.zs):
            (other,) = yield [(have, mask)]
            low = self.bit(self.z, mask) == 0
            have = jnp.stack(
                [jnp.where(low, have, other), jnp.where(low, other, have)], axis=2
            ).reshape(k, -1, rows, n)
        sets = [piece for piece in split(have.reshape(k, -1, n))]
        bits = len(self.across)
        for step in range(bits):
            got = yield [(s, route[step]) for s, route in zip(sets, self.routes)]
            sets = [jnp.stack([s, g]) for s, g in zip(sets, got)]
        whole = []
        for s, route in zip(sets, self.routes):
            axes = [list(reversed(route)).index(mask) for mask in self.across]
            s = jnp.transpose(s, [bits, *axes, bits + 1, bits + 2])
            whole.append(s.reshape(s.shape[0], -1, s.shape[-1]))
        near = join(*whole)
        (far,) = yield [(near, self.core)]
        return near, far

    def scatter(self, lefts, rights, products):
        keep, send = stack_grads(lefts, rights, products)
        (got,) = yield [(send, self.core)]
        count, r, n = keep.shape
        bits = len(self.across)
        shape = (count, 1 << bits, r >> bits, n)
        keep, got = keep.reshape(shape), got.reshape(shape)
        pairs = [(keep, got, 0, count // 2), (keep, got, count // 2, count // 2)]
        lefts = [list(self.across) for _ in pairs]
        for step in reversed(range(bits)):
            masks, parts = [], []
            for i, pair in enumerate(pairs):
                mask = self.routes[i][step]
                axis = lefts[i].index(mask)
                parts.append((*pair, len(lefts[i]) - 1 - axis))
                lefts[i].pop(axis)
                masks.append(mask)
            sends, keeps = add_split(parts)
            gots = yield list(zip(sends, masks))
            pairs = [(k, g, 0, count // 2) for k, g in zip(keeps, gots)]
        acc = jnp.concatenate([k.astype(F32) + g.astype(F32) for k, g, _, _ in pairs], axis=0)
        own = (r >> bits) // self.narrow
        acc = acc.reshape((count,) + (2,) * len(self.zs) + (own, n))
        for mask in self.zs:
            axis = len(acc.shape) - 3
            place = self.bit(self.z, mask)
            if mask != self.zs[0]:
                acc = acc + got.astype(F32)
            send = lax.dynamic_index_in_dim(acc, 1 - place, axis, keepdims=False).astype(BF)
            acc = lax.dynamic_index_in_dim(acc, place, axis, keepdims=False)
            (got,) = yield [(send, mask)]
        return acc, got

    def gather_small(self, vector):
        n = vector.shape[0]
        have = vector.reshape(n // 128, 128)
        masks = [*self.across, self.core, *reversed(self.zs)]
        for mask in masks:
            (other,) = yield [(have, mask)]
            low = self.bit(self.me, mask) == 0
            have = jnp.stack([jnp.where(low, have, other), jnp.where(low, other, have)])
        count = len(masks)
        axes = [list(reversed(masks)).index(mask) for mask in sorted(masks, reverse=True)]
        have = jnp.transpose(have, [*axes, count, count + 1])
        return have.reshape(self.count, n)

    def scatter_small(self, table):
        n = table.shape[1]
        have = table.reshape(self.count, n // 128, 128)
        for mask in [1 << b for b in reversed(range(self.count.bit_length() - 1))]:
            place = self.bit(self.me, mask)
            keep = lax.dynamic_slice_in_dim(have, place * mask, mask, axis=0)
            send = lax.dynamic_slice_in_dim(have, (1 - place) * mask, mask, axis=0)
            (got,) = yield [(send, mask)]
            have = keep + got
        return have.reshape(n)


class Stream:
    def __init__(self, steps):
        self.steps, self.result = steps, None
        self.sends = next(steps)

    def values(self):
        return [value for value, _ in self.sends]

    def replace(self, values):
        self.sends = [(v, mask) for v, (_, mask) in zip(values, self.sends)]

    def feed(self, got):
        try:
            self.sends = self.steps.send(list(got))
        except StopIteration as end:
            self.result = end.value


def pad_lanes(table):
    return jnp.pad(table, ((0, 0), (0, -table.shape[1] % 1024)))


def local(
    inputs,
    memory,
    mem_lengths,
    self_qkv,
    self_out,
    self_bias,
    self_gain,
    cross_qkv,
    cross_out,
    cross_bias,
    cross_gain,
    ffn_in,
    ffn_out,
    ffn_bias_in,
    ffn_bias_out,
    ffn_gain,
    out_grad,
):
    plan = Plan()
    scaling = HD ** (-0.5)
    item_count, mem_slots, model_width = memory.shape
    row_count = inputs.shape[0]
    pairs = model_width // PAIR
    paired = plan.wide == pairs
    place = plan.places() if paired else lax.iota(jnp.int32, pairs)

    def context_back(rows, weights):
        if paired:
            here = lax.iota(jnp.int32, plan.wide)
            return back_natural([rows], weights, [3], here, row_count, BF)
        return plan.natural(backward(rows, (weights[0][3], weights[1][3]))).astype(BF)

    def to_relative(context):
        half = model_width // 2
        return (context[:, :half], context[:, half:]) if paired else plan.relative(context)

    def back(lefts, weights, picks, rows, dtype=F32):
        if (model_width // plan.wide) % 128 == 0:
            return back_natural(lefts, weights, picks, plan.blocks(), rows, dtype)
        total = 0.0
        for i, left in enumerate(lefts):
            near, far = weights if picks is None else (weights[0][picks[i]], weights[1][picks[i]])
            total = total + backward(left, (near, far))
        return plan.natural(total).astype(dtype)

    def forward(rows, weight):
        return project(rows[0], weight[0]) + project(rows[1], weight[1])

    def backward(rows, weight):
        return jnp.concatenate(
            [project_back(rows, weight[0]), project_back(rows, weight[1])], axis=1
        )


    def add_norm(branch, residual, gain, shift):
        if (model_width // plan.wide) % 128 == 0:
            return norm(branch, residual, gain, shift, plan.blocks())
        pre = residual.astype(F32) + branch
        out = layer_norm(pre, gain[0][gain[1], 0], shift[0][shift[1], 0])
        return pre, out, plan.relative(out.astype(BF))


    share, hidden_share = self_gain.shape[0], ffn_bias_in.shape[0]
    small_rows = jnp.concatenate(
        [self_bias, self_gain[None], cross_bias, cross_gain[None], ffn_bias_out, ffn_gain[None]],
        axis=0,
    )
    vector_count = small_rows.shape[0]
    small = Stream(
        plan.gather_small(
            pad_lanes(jnp.concatenate([small_rows.reshape(1, -1), ffn_bias_in[None]], axis=1))[0]
        )
    )

    def four(have):
        return have[:2], have[2:]

    def each(a, b):
        return jnp.concatenate([a, b], axis=0)

    def columns(have):
        half = have.shape[-1] // 2
        return have[..., :half], have[..., half:]

    def one(a, b):
        return jnp.concatenate([a[0], b[0]], axis=1)

    selfs = Stream(
        plan.gather(jnp.concatenate([self_qkv, self_out[None]], axis=0), four, each)
    )
    crosses = Stream(
        plan.gather(jnp.concatenate([cross_qkv, cross_out[None]], axis=0), four, each)
    )
    fins = Stream(plan.gather(ffn_in[None], columns, one))
    fouts = Stream(plan.gather(ffn_out[None], columns, one))
    x_rel = plan.relative(inputs)
    mem_rel = plan.relative(memory.reshape(item_count * mem_slots, model_width))
    after = plan.step(selfs)
    small_last = plan.step(small, after)
    for _ in plan.across:
        small_last = plan.step(small)
    for _ in plan.zs[1:]:
        after = plan.step(selfs, after)
    for _ in plan.across[2:]:
        after = plan.step(selfs, after)
    last, (x_rel, _) = plan.step(selfs, after, (x_rel, small_last))
    plan.finish(small)
    cross_z = plan.step(crosses, after)
    last, (mem_rel, small_sum) = plan.step(selfs, (last, cross_z), (mem_rel, small.result))
    table = small_sum.astype(F32)
    vectors = table[:, : vector_count * share].reshape(plan.count, vector_count, share)
    vectors = jnp.swapaxes(vectors, 0, 1).reshape(vector_count, 1, model_width)
    first_bias = jnp.stack([vectors[0], jnp.zeros_like(vectors[0]), vectors[1]])
    fbin = table[:, vector_count * share :][:, :hidden_share].reshape(-1)
    for _ in plan.zs[1:]:
        cross_z = plan.step(crosses, cross_z)
    self_core = plan.step(selfs, cross_z)
    fin_z = plan.step(fins, cross_z)
    last, fin_z = plan.step(crosses, last, fin_z)

    qkv = stack_project(
        x_rel,
        selfs.result,
        0,
        (first_bias, 0),
        (scaling, 1.0, 1.0),
        BF,
    )
    self_ctx, self_lse = self_attend(qkv, item_count, place)
    self_rel = to_relative(self_ctx)
    branch = stack_project(self_rel, selfs.result, 3, (vectors, 2), (1.0,), F32)[0]
    after = (last, self_core, fin_z)
    for _ in plan.zs[1:]:
        fin_z = plan.step(fins, fin_z)
    fout_z = plan.step(fouts, (fin_z, self_ctx))
    last, (branch, fout_z) = plan.across_steps(crosses, after, (branch, fout_z))
    first_pre, first, first_rel = add_norm(branch, inputs, (vectors, 4), (vectors, 3))
    cross_core = plan.step(crosses)
    for _ in plan.zs[1:]:
        fout_z = plan.step(fouts, fout_z)
    last, _ = plan.step(fins, last, (cross_core, fout_z))

    queries_two = stack_project(first_rel, crosses.result, 0, (vectors, 5), (scaling,), BF)[0]
    mem_keys, mem_values = memory_project(mem_rel, crosses.result, 1, 2, (vectors, 6), 512)
    cross_out = ()
    for item in range(item_count):
        cross_out = cross_attend(
            queries_two, mem_keys, mem_values, mem_lengths, place, item, cross_out
        )
        if item == 0:
            last, cross_out = plan.across_steps(fins, last, cross_out)
    fin_core = plan.step(fins)
    last, (cross_out, _) = plan.step(fouts, last, (cross_out, fin_core))
    cross_ctx, cross_lse = cross_out
    fin = fins.result
    cross_rel = to_relative(cross_ctx)
    branch = stack_project(cross_rel, crosses.result, 3, (vectors, 7), (1.0,), F32)[0]
    second_pre, second, second_rel = add_norm(branch, first, (vectors, 9), (vectors, 8))

    places = plan.places()
    hidden, slope = ffn_up(second_rel, fin, fbin[None], places)
    _, (hidden, slope) = plan.across_steps(fouts, last, (hidden, slope))
    half = hidden.shape[1] // 2
    hidden_rel = (hidden[:, :half], hidden[:, half:])
    plan.step(fouts)
    fout = fouts.result
    third_pre = second + (forward(hidden_rel, fout) + vectors[10, 0])

    layer_out, d_third, e_three, third_sums = norm_back(
        [out_grad], third_pre, (vectors, 12), (vectors, 11)
    )
    half = model_width // 2
    to_fout = Stream(
        plan.scatter([hidden_rel], [e_three], [(0, 0, 0, half), (0, 0, half, half)])
    )
    d_pre = ffn_down_back(e_three, fout, slope, plan.blocks())
    _, d_pre = plan.step(to_fout, None, d_pre)
    half = d_pre.shape[1] // 2
    to_fin = Stream(plan.scatter([second_rel], [d_pre], [(0, 0, 0, half), (0, 0, half, half)]))
    d_hidden = back([d_pre], fin, None, row_count)
    last, (d_hidden, fin_sends) = plan.step(to_fout, None, (d_hidden, to_fin.values()))
    to_fin.replace(fin_sends)
    fin_core = plan.step(to_fin)

    d_second_pre, e_two, second_sums = norm_back([d_third, d_hidden], second_pre, (vectors, 9))
    d_cross_ctx = context_back(e_two, crosses.result)
    cross_back = ()
    for item in range(item_count):
        cross_back = cross_attend_back(
            queries_two, mem_keys, mem_values, cross_lse, d_cross_ctx, mem_lengths, place,
            item, cross_back,
        )
        if item == 0:
            last, (cross_back, _) = plan.across_steps(to_fout, last, (cross_back, fin_core))
    dq_scaled, dk_flat, dv_flat = cross_back
    to_cross = Stream(
        plan.scatter(
            [first_rel, mem_rel, cross_rel],
            [dq_scaled, dk_flat, dv_flat, e_two],
            [(0, 0, 0, model_width), (1, 1, 0, model_width), (1, 2, 0, model_width), (2, 3, 0, model_width)],
        )
    )
    d_queries = back([dq_scaled], crosses.result, [0], row_count)
    for _ in plan.zs[1:]:
        fout_last = plan.step(to_fout)
    last, (d_queries, _, cross_sends) = plan.step(
        to_fin, last, (d_queries, fout_last, to_cross.values())
    )
    to_cross.replace(cross_sends)
    cross_core = plan.step(to_cross)
    fout_last = plan.step(to_fout)

    d_first_pre, e_one, first_sums = norm_back([d_second_pre, d_queries], first_pre, (vectors, 4))
    d_self_ctx = context_back(e_one, selfs.result)
    last, (d_self_ctx, *_) = plan.across_steps(
        to_fin, last, (d_self_ctx, cross_core, fout_last)
    )
    dq_self, dk_self, dv_self = self_attend_back(qkv, self_lse, d_self_ctx, item_count, place)
    to_self = Stream(
        plan.scatter(
            [x_rel, self_rel],
            [dq_self, dk_self, dv_self, e_one],
            [(0, 0, 0, model_width), (0, 1, 0, model_width), (0, 2, 0, model_width), (1, 3, 0, model_width)],
        )
    )
    for _ in plan.zs[1:]:
        fin_last = plan.step(to_fin)
    last, (_, self_sends) = plan.step(to_cross, last, (fin_last, to_self.values()))
    to_self.replace(self_sends)
    self_core = plan.step(to_self)
    fin_last = plan.step(to_fin)
    late, _ = lax.optimization_barrier(((dq_self, dk_self, dv_self), last))
    d_inputs = back(late, selfs.result, [0, 1, 2], row_count)
    last, (d_inputs, *_) = plan.across_steps(
        to_cross, last, (d_inputs, self_core, fin_last)
    )
    input_grad = d_first_pre + d_inputs
    late, _ = lax.optimization_barrier(((dk_flat, dv_flat), last))
    memory_grad = back(late, crosses.result, [1, 2], 512).reshape(memory.shape)
    for _ in plan.zs[1:]:
        cross_last = plan.step(to_cross)
    last, _ = plan.step(to_self, last, (memory_grad, cross_last))
    cross_last = plan.step(to_cross)
    last, _ = plan.across_steps(to_self, last, cross_last)
    sums, _ = lax.optimization_barrier(((dq_self, dv_self, dq_scaled, dv_flat, d_pre), last))
    sum_dq, sum_dv, sum_dq2, sum_dv2, sum_hidden = [column_sums(v) for v in sums]
    grads = jnp.concatenate(
        [
            sum_dq[None],
            sum_dv[None],
            first_sums[:3],
            sum_dq2[None],
            sum_dv2[None],
            second_sums[:3],
            third_sums[:3],
        ],
        axis=0,
    )
    grads = jnp.swapaxes(grads.reshape(vector_count, plan.count, share), 0, 1)
    to_small = Stream(
        plan.scatter_small(
            pad_lanes(
                jnp.concatenate(
                    [grads.reshape(plan.count, -1), sum_hidden.reshape(plan.count, -1)], axis=1
                )
            )
        )
    )
    for _ in plan.zs[1:]:
        plan.step(to_small)
        plan.step(to_small)
        plan.step(to_small, plan.step(to_self))
    for stream in (to_self, to_cross, to_fin, to_fout):
        plan.finish(stream)
    plan.finish(to_small)
    small_sums = to_small.result
    found = small_sums[: vector_count * share].reshape(vector_count, share)
    g_hidden = small_sums[vector_count * share :][:hidden_share]
    early = [stream.result for stream in (to_cross, to_fin, to_fout)]
    early, _ = lax.optimization_barrier((early, last))
    g_self, g_cross, g_fin, g_fout = [
        keep + got.astype(F32) for keep, got in (to_self.result, *early)
    ]
    g_fout = jnp.concatenate([g_fout[0], g_fout[1]], axis=1)
    g_fin = jnp.concatenate([g_fin[0], g_fin[1]], axis=1)
    return (
        layer_out,
        input_grad,
        memory_grad,
        g_self[:3],
        g_self[3],
        found[:4],
        found[4],
        g_cross[:3],
        g_cross[3],
        found[5:9],
        found[9],
        g_fin,
        g_fout,
        g_hidden,
        found[10:12],
        found[12],
    )


def solution(mesh):
    both = ("wide", "narrow")
    placed = (
        P(both, None),
        P(both, None, None),
        P(both),
        P(None, both, None),
        P(both, None),
        P(None, both),
        P(both),
        P(None, both, None),
        P(both, None),
        P(None, both),
        P(both),
        P(both, None),
        P(both, None),
        P(both),
        P(None, both),
        P(both),
        P(both, None),
    )
    return jax.shard_map(
        local,
        mesh=mesh,
        in_specs=placed,
        out_specs=(
            P(both, None),
            P(both, None),
            P(both, None, None),
            P(None, both, None),
            P(both, None),
            P(None, both),
            P(both),
            P(None, both, None),
            P(both, None),
            P(None, both),
            P(both),
            P(both, None),
            P(both, None),
            P(both),
            P(None, both),
            P(both),
        ),
        check_vma=False,
    )
```

```python
import functools
import math

import jax
import jax.numpy as jnp
from jax import lax
from jax.experimental import pallas as pl
from jax.experimental.pallas import tpu as pltpu
from jax.sharding import PartitionSpec as P

HD = 64
EPSILON = 1e-05
MASKED = -1e30
AXES = ("wide", "narrow")
BF = jnp.bfloat16
F32 = jnp.float32


def project(left_rows, weight):
    return jnp.dot(left_rows, weight, preferred_element_type=F32)


def project_back(gradient, weight):
    return lax.dot_general(gradient, weight, (((1,), (1,)), ((), ())), preferred_element_type=F32)


def weight_grad(left_rows, gradient):
    return lax.dot_general(left_rows, gradient, (((0,), (0,)), ((), ())), preferred_element_type=F32)


def column_sums(gradient):
    return jnp.sum(gradient.astype(F32), axis=0)


def layer_norm(hidden, gain_row, shift_row):
    average = jnp.mean(hidden, axis=-1, keepdims=True)
    centred = hidden - average
    variance = jnp.mean(centred * centred, axis=-1, keepdims=True)
    return centred * lax.rsqrt(variance + EPSILON) * gain_row + shift_row


def pair_stack(rows):
    lane = lax.broadcasted_iota(jnp.int32, rows.shape, 1)
    zero = jnp.zeros_like(rows)
    return jnp.concatenate(
        [jnp.where(lane < HD, rows, zero), jnp.where(lane >= HD, rows, zero)], axis=0
    )


def pair_merge(stacked):
    t = stacked.shape[0] // 2
    lane = lax.broadcasted_iota(jnp.int32, (t, 2 * HD), 1)
    return jnp.where(lane < HD, stacked[:t], stacked[t:])


def dot_nt(a, b):
    return lax.dot_general(a, b, (((1,), (1,)), ((), ())), preferred_element_type=F32)


def dot_tn(a, b):
    return lax.dot_general(a, b, (((0,), (0,)), ((), ())), preferred_element_type=F32)


def dot_nn(a, b):
    return lax.dot_general(a, b, (((1,), (0,)), ((), ())), preferred_element_type=F32)


def masked_scores(k, qs, length):
    scores = dot_nt(k, qs)
    slot = lax.broadcasted_iota(jnp.int32, scores.shape, 0)
    if length is None:
        seen = lax.broadcasted_iota(jnp.int32, scores.shape, 1) % (scores.shape[1] // 2)
        return jnp.where(slot <= seen, scores, MASKED)
    return jnp.where(slot < length, scores, MASKED)


def attend_pair(q, k, v, length):
    scores = masked_scores(k, pair_stack(q), length)
    top = jnp.max(scores, axis=0, keepdims=True)
    weights = jnp.exp(scores - top)
    total = jnp.sum(weights, axis=0, keepdims=True)
    chances = (weights * (1.0 / total)).astype(BF)
    return pair_merge(dot_tn(chances, v)).astype(BF), top + jnp.log(total)


def attend_pair_back(q, k, v, lse, d_out, length):
    qs, ds_out = pair_stack(q), pair_stack(d_out)
    chances = jnp.exp(masked_scores(k, qs, length) - lse)
    d_chances = dot_nt(v, ds_out)
    row = jnp.sum(d_chances * chances, axis=0, keepdims=True)
    d_scores = (chances * (d_chances - row)).astype(BF)
    d_q = pair_merge(dot_tn(d_scores, k)).astype(BF)
    d_k = dot_nn(d_scores, qs).astype(BF)
    d_v = dot_nn(chances.astype(BF), ds_out).astype(BF)
    return d_q, d_k, d_v


PAIR = 2 * HD
UNROLL = 2


def lane_block(at):
    return pl.ds(pl.multiple_of(at * PAIR, PAIR), PAIR)


def cross_kernel(place, length, q, k, v, *refs):
    out, lse = refs[-2:]
    for u in range(UNROLL):
        cut = slice(u * PAIR, (u + 1) * PAIR)
        found, lse[0, u] = attend_pair(q[:, cut], k[:, cut], v[:, cut], length[0])
        out[:, lane_block(place[pl.program_id(0) * UNROLL + u])] = found


def cross_back_kernel(place, length, q, k, v, lse, d_out, *refs):
    d_q, d_k, d_v = refs[-3:]
    for u in range(UNROLL):
        cut = slice(u * PAIR, (u + 1) * PAIR)
        cotangent = d_out[:, lane_block(place[pl.program_id(0) * UNROLL + u])]
        found = attend_pair_back(
            q[:, cut], k[:, cut], v[:, cut], lse[0, u], cotangent, length[0]
        )
        d_q[:, cut] = found[0] * jnp.asarray(HD**-0.5, BF)
        d_k[:, cut] = found[1]
        d_v[:, cut] = found[2]


def cross_call(kernel, q, k, lengths, place, item, values, in_specs, out_specs, out_shape, so_far):
    return pl.pallas_call(
        kernel,
        grid_spec=pltpu.PrefetchScalarGridSpec(
            num_scalar_prefetch=2,
            grid=(q.shape[1] // PAIR // UNROLL,),
            in_specs=in_specs + [pl.BlockSpec(memory_space=pl.ANY)] * len(so_far),
            out_specs=out_specs,
        ),
        out_shape=out_shape,
        input_output_aliases={2 + len(values) + i: i for i in range(len(so_far))},
        name="cross_attend",
    )(place, lax.slice_in_dim(lengths, item, item + 1), *values, *so_far)


def cross_specs(q, k, items, item):
    t, s, n = q.shape[0] // items, k.shape[0] // items, PAIR * UNROLL
    rows = pl.BlockSpec((t, n), lambda j, *_: (item, j))
    slots = pl.BlockSpec((s, n), lambda j, *_: (item, j))
    placed = pl.BlockSpec((t, q.shape[1]), lambda j, *_: (item, 0))
    lse = pl.BlockSpec((1, UNROLL, 1, 2 * t), lambda j, *_: (item, j, 0, 0))
    return rows, slots, placed, lse


def cross_attend(q, k, v, lengths, place, item, so_far):
    items = lengths.shape[0]
    rows, slots, placed, lse = cross_specs(q, k, items, item)
    out_shape = [
        jax.ShapeDtypeStruct(q.shape, BF),
        jax.ShapeDtypeStruct((items, q.shape[1] // PAIR, 1, 2 * q.shape[0] // items), F32),
    ]
    return cross_call(
        cross_kernel, q, k, lengths, place, item, (q, k, v),
        [rows, slots, slots], [placed, lse], out_shape, so_far,
    )


def cross_attend_back(q, k, v, lse, d_out, lengths, place, item, so_far):
    rows, slots, placed, lse_spec = cross_specs(q, k, lengths.shape[0], item)
    out_shape = [jax.ShapeDtypeStruct(a.shape, BF) for a in (q, k, k)]
    return cross_call(
        cross_back_kernel, q, k, lengths, place, item, (q, k, v, lse, d_out),
        [rows, slots, slots, lse_spec, placed], [rows, slots, slots], out_shape, so_far,
    )


def lanes(ref, at):
    return ref[:, pl.ds(pl.multiple_of(at * PAIR, PAIR), PAIR)]


def self_kernel(place, q, k, v, out, lse):
    for j in range(q.shape[1] // PAIR):
        cut = slice(j * PAIR, (j + 1) * PAIR)
        found, lse[0, j] = attend_pair(q[:, cut], k[:, cut], v[:, cut], None)
        out[:, pl.ds(pl.multiple_of(place[j] * PAIR, PAIR), PAIR)] = found


def self_back_kernel(place, q, k, v, lse, d_out, d_q, d_k, d_v):
    for j in range(q.shape[1] // PAIR):
        cut = slice(j * PAIR, (j + 1) * PAIR)
        found = attend_pair_back(
            q[:, cut], k[:, cut], v[:, cut], lse[0, j], lanes(d_out, place[j]), None
        )
        d_q[:, cut] = found[0] * jnp.asarray(HD**-0.5, BF)
        d_k[:, cut] = found[1]
        d_v[:, cut] = found[2]


def self_attend(qkv, items, place):
    _, rows, width = qkv.shape
    t = rows // items

    def part(i):
        return pl.BlockSpec((None, t, width), lambda b, *_: (i, b, 0))

    lse = pl.BlockSpec((1, width // PAIR, 1, 2 * t), lambda b, *_: (b, 0, 0, 0))
    return pl.pallas_call(
        self_kernel,
        grid_spec=pltpu.PrefetchScalarGridSpec(
            num_scalar_prefetch=1,
            grid=(items,),
            in_specs=[part(0), part(1), part(2)],
            out_specs=[pl.BlockSpec((t, width), lambda b, *_: (b, 0)), lse],
        ),
        out_shape=[
            jax.ShapeDtypeStruct((rows, width), BF),
            jax.ShapeDtypeStruct((items, width // PAIR, 1, 2 * t), F32),
        ],
        name="self_attend",
    )(place, qkv, qkv, qkv)


def self_attend_back(qkv, lse, d_out, items, place):
    _, m, width = qkv.shape
    t = m // items

    def part(i):
        return pl.BlockSpec((None, t, width), lambda b, *_: (i, b, 0))

    rows = pl.BlockSpec((t, width), lambda b, *_: (b, 0))
    lse_spec = pl.BlockSpec((1, width // PAIR, 1, 2 * t), lambda b, *_: (b, 0, 0, 0))
    return pl.pallas_call(
        self_back_kernel,
        grid_spec=pltpu.PrefetchScalarGridSpec(
            num_scalar_prefetch=1,
            grid=(items,),
            in_specs=[part(0), part(1), part(2), lse_spec, rows],
            out_specs=[rows] * 3,
        ),
        out_shape=[jax.ShapeDtypeStruct((m, width), BF)] * 3,
        name="self_attend_back",
    )(place, qkv, qkv, qkv, lse, d_out)


def row_of(row):
    return pl.BlockSpec((None, 1, row[0].shape[2]), lambda *_: (row[1], 0, 0))


def stacked(array, i, **kw):
    return pl.BlockSpec((None,) + array.shape[1:], lambda *_: (i, 0, 0), **kw)


def project_kernel(scales, x0, x1, near, far, bias, out):
    total = dot_nn(x0[...], near[...]) + dot_nn(x1[...], far[...]) + bias[...]
    j = pl.program_id(0)
    scale = scales[0]
    for i in range(1, len(scales)):
        scale = jnp.where(j == i, scales[i], scale)
    out[...] = (total * scale).astype(out.dtype)


def stack_project(rows, weights, first, bias, scales, dtype):
    near, far = weights
    bias, start = bias
    m, h = rows[0].shape
    n = near.shape[2]
    count = len(scales)
    whole = pl.BlockSpec((m, h), lambda j: (0, 0))
    weight = pl.BlockSpec((None, h, n), lambda j: (first + j, 0, 0))
    return pl.pallas_call(
        functools.partial(project_kernel, scales),
        grid=(count,),
        in_specs=[whole, whole, weight, weight, pl.BlockSpec((None, 1, n), lambda j: (start + j, 0, 0))],
        out_specs=pl.BlockSpec((None, m, n), lambda j: (j, 0, 0)),
        out_shape=jax.ShapeDtypeStruct((count, m, n), dtype),
        name="stack_project",
    )(*rows, near, far, bias)


def grads_kernel(products, *refs):
    ins, (keep, send) = refs[:-2], refs[-2:]
    for i, (left, right, start) in enumerate(products):

        @pl.when(pl.program_id(0) == i)
        def _():
            to = ins[right][:, start : start + keep.shape[1]]
            keep[...] = dot_tn(ins[left][...], to).astype(BF)
            send[...] = dot_tn(ins[left + 1][...], to).astype(BF)


def stack_grads(lefts, rights, products):
    arrays = [half for left in lefts for half in left] + list(rights)
    n = products[0][3]
    r = lefts[0][0].shape[1]
    table = [(2 * left, 2 * len(lefts) + right, start) for left, right, start, _ in products]
    out = pl.BlockSpec((None, r, n), lambda i: (i, 0, 0))
    shape = jax.ShapeDtypeStruct((len(products), r, n), BF)
    return pl.pallas_call(
        functools.partial(grads_kernel, table),
        grid=(len(products),),
        in_specs=[
            pl.BlockSpec(a.shape, lambda i: (0, 0), pipeline_mode=pl.Buffered(1)) for a in arrays
        ],
        out_specs=[out, out],
        out_shape=[shape, shape],
        name="stack_grads",
    )(*arrays)


def back_kernel(blocks, *refs):
    count = (len(refs) - 1) // 3
    out = refs[-1]
    size = out.shape[1] // blocks.shape[0]
    for half in range(2):
        total = dot_nt(refs[0][...], refs[count + half][...])
        for i in range(1, count):
            total = total + dot_nt(refs[i][...], refs[count + 2 * i + half][...])
        for i in range(total.shape[1] // size):
            to = blocks[half * (blocks.shape[0] // 2) + i]
            at = pl.ds(pl.multiple_of(to * size, 128), size)
            out[:, at] = total[:, i * size : (i + 1) * size].astype(out.dtype)


def back_natural(lefts, weights, picks, blocks, rows, dtype):
    m = lefts[0].shape[0]
    near, far = weights
    if picks is None:
        near, far, picks = near[None], far[None], [0]
    n = 2 * near.shape[1]
    in_specs = [pl.BlockSpec((rows, a.shape[1]), lambda i, *_: (i, 0)) for a in lefts]
    values = []
    for p in picks:
        in_specs += [stacked(near, p, pipeline_mode=pl.Buffered(1))] * 2
        values += [near, far]
    return pl.pallas_call(
        back_kernel,
        grid_spec=pltpu.PrefetchScalarGridSpec(
            num_scalar_prefetch=1,
            grid=(m // rows,),
            in_specs=in_specs,
            out_specs=pl.BlockSpec((rows, n), lambda i, *_: (i, 0)),
        ),
        out_shape=jax.ShapeDtypeStruct((m, n), dtype),
        name="back_natural",
    )(blocks, *lefts, *values)


def normed(hidden):
    centred = hidden - jnp.mean(hidden, axis=-1, keepdims=True)
    scale = lax.rsqrt(jnp.mean(centred * centred, axis=-1, keepdims=True) + EPSILON)
    return centred * scale, scale


def norm_kernel(blocks, branch, residual, gain, shift, pre, out, rel0, rel1):
    pre[...] = residual[...].astype(F32) + branch[...]
    out[...] = normed(pre[...])[0] * gain[...] + shift[...]
    half = blocks.shape[0] // 2
    size = out.shape[1] // blocks.shape[0]
    for i in range(2 * half):
        rel, at = (rel0, i) if i < half else (rel1, i - half)
        block = out[:, pl.ds(pl.multiple_of(blocks[i] * size, 128), size)]
        rel[:, at * size : (at + 1) * size] = block.astype(BF)


def norm(branch, residual, gain, shift, blocks):
    m, n = branch.shape
    rows = m // 2
    full = pl.BlockSpec((rows, n), lambda i, *_: (i, 0))
    halves = pl.BlockSpec((rows, n // 2), lambda i, *_: (i, 0))
    pre, out, rel0, rel1 = pl.pallas_call(
        norm_kernel,
        grid_spec=pltpu.PrefetchScalarGridSpec(
            num_scalar_prefetch=1,
            grid=(2,),
            in_specs=[full, full, row_of(gain), row_of(shift)],
            out_specs=[full, full, halves, halves],
        ),
        out_shape=[
            jax.ShapeDtypeStruct((m, n), F32),
            jax.ShapeDtypeStruct((m, n), F32),
            jax.ShapeDtypeStruct((m, n // 2), BF),
            jax.ShapeDtypeStruct((m, n // 2), BF),
        ],
        name="norm",
    )(blocks, branch, residual, gain[0], shift[0])
    return pre, out, (rel0, rel1)


def norm_back_kernel(count, *refs):
    pre, gain = refs[count : count + 2]
    d_pre, low, sums = refs[-3:]
    cotangent = refs[0][...].astype(F32)
    for ref in refs[1:count]:
        cotangent = cotangent + ref[...]
    z, scale = normed(pre[...])
    if len(refs) > count + 5:
        shift, out = refs[count + 2], refs[-4]
        out[...] = (z * gain[...] + shift[...]).astype(BF)
    inner = cotangent * gain[...]
    found = scale * (
        inner
        - jnp.mean(inner, axis=-1, keepdims=True)
        - z * jnp.mean(inner * z, axis=-1, keepdims=True)
    )
    d_pre[...] = found
    low[...] = found.astype(BF)

    @pl.when(pl.program_id(0) == 0)
    def _():
        sums[...] = jnp.zeros_like(sums)

    rows = [found.astype(BF).astype(F32), cotangent, cotangent * z]
    for i, value in enumerate(rows):
        sums[i : i + 1, :] += jnp.sum(value, axis=0, keepdims=True)


def norm_back(cotangents, pre, gain, shift=None):
    m, n = pre.shape
    rows = m // 2
    full = pl.BlockSpec((rows, n), lambda i: (i, 0))
    extra = [gain] if shift is None else [gain, shift]
    out_specs = [full, full, pl.BlockSpec((8, n), lambda i: (0, 0))]
    out_shape = [
        jax.ShapeDtypeStruct((m, n), F32),
        jax.ShapeDtypeStruct((m, n), BF),
        jax.ShapeDtypeStruct((8, n), F32),
    ]
    if shift is not None:
        out_specs, out_shape = [full] + out_specs, [jax.ShapeDtypeStruct((m, n), BF)] + out_shape
    return pl.pallas_call(
        functools.partial(norm_back_kernel, len(cotangents)),
        grid=(2,),
        in_specs=[full] * (len(cotangents) + 1) + [row_of(row) for row in extra],
        out_specs=out_specs,
        out_shape=out_shape,
        name="norm_back",
    )(*cotangents, pre, *[row[0] for row in extra])


def gelu_parts(u):
    half_erf = 0.5 * (1.0 + lax.erf(u * (0.5**0.5)))
    return u * half_erf, half_erf + u * jnp.exp(-0.5 * u * u) * (0.5 / math.pi) ** 0.5


def ffn_up_kernel(places, x0, x1, near, far, bias, hidden, slope):
    u = dot_nn(x0[...], near[...]) + dot_nn(x1[...], far[...]) + bias[...]
    value, slope[...] = gelu_parts(u)
    hidden[...] = value.astype(BF)


def ffn_up(rows, weight, bias, places):
    near, far = weight
    m, h = rows[0].shape
    n = near.shape[1]
    size = n // places.shape[0]
    whole = pl.BlockSpec((m, h), lambda j, *_: (0, 0))
    columns = pl.BlockSpec((h, size), lambda j, *_: (0, j))
    return pl.pallas_call(
        ffn_up_kernel,
        grid_spec=pltpu.PrefetchScalarGridSpec(
            num_scalar_prefetch=1,
            grid=(n // size,),
            in_specs=[whole, whole, columns, columns, pl.BlockSpec((1, size), lambda j, *_: (0, j))],
            out_specs=[
                pl.BlockSpec((m, size), lambda j, places: (0, places[j])),
                pl.BlockSpec((m, size), lambda j, places: (0, j)),
            ],
        ),
        out_shape=[jax.ShapeDtypeStruct((m, n), BF), jax.ShapeDtypeStruct((m, n), F32)],
        name="ffn_up",
    )(places, *rows, near, far, bias)


def ffn_down_back_kernel(blocks, cotangent, near, far, slope, out):
    chosen = pl.program_id(0) < pl.num_programs(0) // 2

    @pl.when(chosen)
    def _():
        out[...] = (dot_nt(cotangent[...], near[...]) * slope[...]).astype(BF)

    @pl.when(jnp.logical_not(chosen))
    def _():
        out[...] = (dot_nt(cotangent[...], far[...]) * slope[...]).astype(BF)


def ffn_down_back(cotangent, weight, slope, blocks):
    near, far = weight
    m, k = cotangent.shape
    count = blocks.shape[0]
    half = count // 2
    size = near.shape[0] // half
    natural = pl.BlockSpec((m, size), lambda j, blocks: (0, blocks[j]))
    return pl.pallas_call(
        ffn_down_back_kernel,
        grid_spec=pltpu.PrefetchScalarGridSpec(
            num_scalar_prefetch=1,
            grid=(count,),
            in_specs=[
                pl.BlockSpec((m, k), lambda j, *_: (0, 0)),
                pl.BlockSpec((size, k), lambda j, *_: (jnp.minimum(j, half - 1), 0)),
                pl.BlockSpec((size, k), lambda j, *_: (jnp.maximum(j - half, 0), 0)),
                natural,
            ],
            out_specs=natural,
        ),
        out_shape=jax.ShapeDtypeStruct((m, count * size), BF),
        name="ffn_down_back",
    )(blocks, cotangent, near, far, slope)


def memory_kernel(x0, x1, k0, k1, v0, v1, bias, keys, values):
    keys[...] = (dot_nn(x0[...], k0[...]) + dot_nn(x1[...], k1[...])).astype(BF)
    total = dot_nn(x0[...], v0[...]) + dot_nn(x1[...], v1[...])
    values[...] = (total + bias[...]).astype(BF)


def memory_project(rows, weights, key_pick, value_pick, bias, block):
    near, far = weights
    m, h = rows[0].shape
    n = near.shape[2]
    once = pl.Buffered(1)
    return pl.pallas_call(
        memory_kernel,
        grid=(m // block,),
        in_specs=[pl.BlockSpec((block, h), lambda i: (i, 0))] * 2
        + [stacked(near, key_pick, pipeline_mode=once)] * 2
        + [stacked(near, value_pick, pipeline_mode=once)] * 2
        + [row_of(bias)],
        out_specs=[pl.BlockSpec((block, n), lambda i: (i, 0))] * 2,
        out_shape=[jax.ShapeDtypeStruct((m, n), BF)] * 2,
        name="memory_project",
    )(*rows, near, far, near, far, bias[0])


def add_split_kernel(*refs):
    count = len(refs) // 6
    for i in range(count):
        keep_s, got_s, keep_k, got_k = refs[4 * i : 4 * i + 4]
        send, keep = refs[4 * count + 2 * i : 4 * count + 2 * i + 2]
        send[...] = (keep_s[...].astype(F32) + got_s[...].astype(F32)).astype(BF)
        keep[...] = (keep_k[...].astype(F32) + got_k[...].astype(F32)).astype(BF)


def add_split(parts):
    in_specs, out_specs, shapes, values = [], [], [], []
    for keep, got, first, count, low in parts:
        _, blocks, rows, n = keep.shape

        def spec(value, first=first, low=low, rows=rows, n=n):
            def index(i, j):
                high, rest = j >> low, j & ((1 << low) - 1)
                return first + i, (high << (low + 1)) | (value << low) | rest, 0, 0

            return pl.BlockSpec((None, None, rows, n), index)

        in_specs += [spec(1), spec(1), spec(0), spec(0)]
        values += [keep, got, keep, got]
        out_specs += [pl.BlockSpec((None, None, rows, n), lambda i, j: (i, j, 0, 0))] * 2
        shapes += [jax.ShapeDtypeStruct((count, blocks // 2, rows, n), BF)] * 2
    found = pl.pallas_call(
        add_split_kernel,
        grid=shapes[0].shape[:2],
        in_specs=in_specs,
        out_specs=out_specs,
        out_shape=shapes,
        name="add_split",
    )(*values)
    return found[0::2], found[1::2]


class Plan:
    def __init__(self):
        self.wide = lax.axis_size("wide")
        self.narrow = lax.axis_size("narrow")
        self.count = self.wide * self.narrow
        self.w = lax.axis_index("wide")
        self.z = lax.axis_index("narrow")
        self.me = self.w * self.narrow + self.z
        bits = self.wide.bit_length() - 1
        rest = [1 << b for b in range(1, bits)]
        half = len(rest) // 2
        self.core = self.narrow
        xs = [m * self.narrow for m in rest[:half]]
        ys = [m * self.narrow for m in rest[half:]]
        self.across = sorted([*xs, *ys], reverse=True)
        self.routes = ([*xs, *ys], [*ys, *xs])
        self.zs = [1 << b for b in range(self.narrow.bit_length() - 1)]
        self.order = [r for r in range(self.wide) if r % 2 == 0] + [
            r for r in range(self.wide) if r % 2 == 1
        ]

    def bit(self, index, mask):
        return (index // mask) % 2

    def step(self, stream, after=None, during=None):
        sends = [value for value, _ in stream.sends]
        if after is not None:
            sends, _ = lax.optimization_barrier((sends, after))
        got = [
            lax.ppermute(v, AXES, [(i, i ^ m) for i in range(self.count)])
            for v, (_, m) in zip(sends, stream.sends)
        ]
        if during is not None:
            got, during = lax.optimization_barrier((got, during))
        stream.feed(got)
        return got if during is None else (got, during)

    def across_steps(self, stream, after, during):
        for _ in self.across[1:]:
            after, during = self.step(stream, after, during)
        return after, during

    def finish(self, stream):
        while stream.result is None:
            self.step(stream)

    def relative(self, rows):
        size = rows.shape[1] // self.wide
        pieces = [
            lax.dynamic_slice_in_dim(rows, (jnp.int32(r) ^ self.w) * size, size, axis=1)
            for r in self.order
        ]
        half = self.wide // 2
        return jnp.concatenate(pieces[:half], axis=1), jnp.concatenate(pieces[half:], axis=1)

    def natural(self, rows):
        size = rows.shape[1] // self.wide
        pieces = []
        for i in range(self.wide):
            r = jnp.int32(i) ^ self.w
            place = (r % 2) * (self.wide // 2) + r // 2
            pieces.append(lax.dynamic_slice_in_dim(rows, place * size, size, axis=1))
        return jnp.concatenate(pieces, axis=1)

    def places(self):
        r = lax.iota(jnp.int32, self.wide) ^ self.w
        return (r % 2) * (self.wide // 2) + r // 2

    def blocks(self):
        return jnp.array(self.order, jnp.int32) ^ self.w

    def gather(self, part, split, join):
        k, rows, n = part.shape
        have = part.reshape(k, 1, rows, n)
        for mask in reversed(self.zs):
            (other,) = yield [(have, mask)]
            low = self.bit(self.z, mask) == 0
            have = jnp.stack(
                [jnp.where(low, have, other), jnp.where(low, other, have)], axis=2
            ).reshape(k, -1, rows, n)
        sets = [piece for piece in split(have.reshape(k, -1, n))]
        bits = len(self.across)
        for step in range(bits):
            got = yield [(s, route[step]) for s, route in zip(sets, self.routes)]
            sets = [jnp.stack([s, g]) for s, g in zip(sets, got)]
        whole = []
        for s, route in zip(sets, self.routes):
            axes = [list(reversed(route)).index(mask) for mask in self.across]
            s = jnp.transpose(s, [bits, *axes, bits + 1, bits + 2])
            whole.append(s.reshape(s.shape[0], -1, s.shape[-1]))
        near = join(*whole)
        (far,) = yield [(near, self.core)]
        return near, far

    def scatter(self, lefts, rights, products):
        keep, send = stack_grads(lefts, rights, products)
        (got,) = yield [(send, self.core)]
        count, r, n = keep.shape
        bits = len(self.across)
        shape = (count, 1 << bits, r >> bits, n)
        keep, got = keep.reshape(shape), got.reshape(shape)
        pairs = [(keep, got, 0, count // 2), (keep, got, count // 2, count // 2)]
        lefts = [list(self.across) for _ in pairs]
        for step in reversed(range(bits)):
            masks, parts = [], []
            for i, pair in enumerate(pairs):
                mask = self.routes[i][step]
                axis = lefts[i].index(mask)
                parts.append((*pair, len(lefts[i]) - 1 - axis))
                lefts[i].pop(axis)
                masks.append(mask)
            sends, keeps = add_split(parts)
            gots = yield list(zip(sends, masks))
            pairs = [(k, g, 0, count // 2) for k, g in zip(keeps, gots)]
        acc = jnp.concatenate([k.astype(F32) + g.astype(F32) for k, g, _, _ in pairs], axis=0)
        own = (r >> bits) // self.narrow
        acc = acc.reshape((count,) + (2,) * len(self.zs) + (own, n))
        for mask in self.zs:
            axis = len(acc.shape) - 3
            place = self.bit(self.z, mask)
            if mask != self.zs[0]:
                acc = acc + got.astype(F32)
            send = lax.dynamic_index_in_dim(acc, 1 - place, axis, keepdims=False).astype(BF)
            acc = lax.dynamic_index_in_dim(acc, place, axis, keepdims=False)
            (got,) = yield [(send, mask)]
        return acc, got

    def gather_small(self, vector):
        n = vector.shape[0]
        have = vector.reshape(n // 128, 128)
        masks = [*self.across, self.core, *reversed(self.zs)]
        for mask in masks:
            (other,) = yield [(have, mask)]
            low = self.bit(self.me, mask) == 0
            have = jnp.stack([jnp.where(low, have, other), jnp.where(low, other, have)])
        count = len(masks)
        axes = [list(reversed(masks)).index(mask) for mask in sorted(masks, reverse=True)]
        have = jnp.transpose(have, [*axes, count, count + 1])
        return have.reshape(self.count, n)

    def scatter_small(self, table):
        n = table.shape[1]
        have = table.reshape(self.count, n // 128, 128)
        for mask in [1 << b for b in reversed(range(self.count.bit_length() - 1))]:
            place = self.bit(self.me, mask)
            keep = lax.dynamic_slice_in_dim(have, place * mask, mask, axis=0)
            send = lax.dynamic_slice_in_dim(have, (1 - place) * mask, mask, axis=0)
            (got,) = yield [(send, mask)]
            have = keep + got
        return have.reshape(n)


class Stream:
    def __init__(self, steps):
        self.steps, self.result = steps, None
        self.sends = next(steps)

    def values(self):
        return [value for value, _ in self.sends]

    def replace(self, values):
        self.sends = [(v, mask) for v, (_, mask) in zip(values, self.sends)]

    def feed(self, got):
        try:
            self.sends = self.steps.send(list(got))
        except StopIteration as end:
            self.result = end.value


def pad_lanes(table):
    return jnp.pad(table, ((0, 0), (0, -table.shape[1] % 1024)))


def local(
    inputs,
    memory,
    mem_lengths,
    self_qkv,
    self_out,
    self_bias,
    self_gain,
    cross_qkv,
    cross_out,
    cross_bias,
    cross_gain,
    ffn_in,
    ffn_out,
    ffn_bias_in,
    ffn_bias_out,
    ffn_gain,
    out_grad,
):
    plan = Plan()
    scaling = HD ** (-0.5)
    item_count, mem_slots, model_width = memory.shape
    row_count = inputs.shape[0]
    pairs = model_width // PAIR
    paired = plan.wide == pairs
    place = plan.places() if paired else lax.iota(jnp.int32, pairs)

    def context_back(rows, weights):
        if paired:
            here = lax.iota(jnp.int32, plan.wide)
            return back_natural([rows], weights, [3], here, row_count, BF)
        return plan.natural(backward(rows, (weights[0][3], weights[1][3]))).astype(BF)

    def to_relative(context):
        half = model_width // 2
        return (context[:, :half], context[:, half:]) if paired else plan.relative(context)

    def back(lefts, weights, picks, rows, dtype=F32):
        if (model_width // plan.wide) % 128 == 0:
            return back_natural(lefts, weights, picks, plan.blocks(), rows, dtype)
        total = 0.0
        for i, left in enumerate(lefts):
            near, far = weights if picks is None else (weights[0][picks[i]], weights[1][picks[i]])
            total = total + backward(left, (near, far))
        return plan.natural(total).astype(dtype)

    def forward(rows, weight):
        return project(rows[0], weight[0]) + project(rows[1], weight[1])

    def backward(rows, weight):
        return jnp.concatenate(
            [project_back(rows, weight[0]), project_back(rows, weight[1])], axis=1
        )


    def add_norm(branch, residual, gain, shift):
        if (model_width // plan.wide) % 128 == 0:
            return norm(branch, residual, gain, shift, plan.blocks())
        pre = residual.astype(F32) + branch
        out = layer_norm(pre, gain[0][gain[1], 0], shift[0][shift[1], 0])
        return pre, out, plan.relative(out.astype(BF))


    share, hidden_share = self_gain.shape[0], ffn_bias_in.shape[0]
    small_rows = jnp.concatenate(
        [self_bias, self_gain[None], cross_bias, cross_gain[None], ffn_bias_out, ffn_gain[None]],
        axis=0,
    )
    vector_count = small_rows.shape[0]
    small = Stream(
        plan.gather_small(
            pad_lanes(jnp.concatenate([small_rows.reshape(1, -1), ffn_bias_in[None]], axis=1))[0]
        )
    )

    def four(have):
        return have[:2], have[2:]

    def each(a, b):
        return jnp.concatenate([a, b], axis=0)

    def columns(have):
        half = have.shape[-1] // 2
        return have[..., :half], have[..., half:]

    def one(a, b):
        return jnp.concatenate([a[0], b[0]], axis=1)

    selfs = Stream(
        plan.gather(jnp.concatenate([self_qkv, self_out[None]], axis=0), four, each)
    )
    crosses = Stream(
        plan.gather(jnp.concatenate([cross_qkv, cross_out[None]], axis=0), four, each)
    )
    fins = Stream(plan.gather(ffn_in[None], columns, one))
    fouts = Stream(plan.gather(ffn_out[None], columns, one))
    x_rel = plan.relative(inputs)
    mem_rel = plan.relative(memory.reshape(item_count * mem_slots, model_width))
    after = plan.step(selfs)
    small_last = plan.step(small, after)
    for _ in plan.across:
        small_last = plan.step(small)
    for _ in plan.zs[1:]:
        after = plan.step(selfs, after)
    for _ in plan.across[2:]:
        after = plan.step(selfs, after)
    last, (x_rel, _) = plan.step(selfs, after, (x_rel, small_last))
    plan.finish(small)
    cross_z = plan.step(crosses, after)
    last, (mem_rel, small_sum) = plan.step(selfs, (last, cross_z), (mem_rel, small.result))
    table = small_sum.astype(F32)
    vectors = table[:, : vector_count * share].reshape(plan.count, vector_count, share)
    vectors = jnp.swapaxes(vectors, 0, 1).reshape(vector_count, 1, model_width)
    first_bias = jnp.stack([vectors[0], jnp.zeros_like(vectors[0]), vectors[1]])
    fbin = table[:, vector_count * share :][:, :hidden_share].reshape(-1)
    for _ in plan.zs[1:]:
        cross_z = plan.step(crosses, cross_z)
    self_core = plan.step(selfs, cross_z)
    fin_z = plan.step(fins, cross_z)
    last, fin_z = plan.step(crosses, last, fin_z)

    qkv = stack_project(
        x_rel,
        selfs.result,
        0,
        (first_bias, 0),
        (scaling, 1.0, 1.0),
        BF,
    )
    self_ctx, self_lse = self_attend(qkv, item_count, place)
    self_rel = to_relative(self_ctx)
    branch = stack_project(self_rel, selfs.result, 3, (vectors, 2), (1.0,), F32)[0]
    after = (last, self_core, fin_z)
    for _ in plan.zs[1:]:
        fin_z = plan.step(fins, fin_z)
    fout_z = plan.step(fouts, (fin_z, self_ctx))
    last, (branch, fout_z) = plan.across_steps(crosses, after, (branch, fout_z))
    first_pre, first, first_rel = add_norm(branch, inputs, (vectors, 4), (vectors, 3))
    cross_core = plan.step(crosses)
    for _ in plan.zs[1:]:
        fout_z = plan.step(fouts, fout_z)
    last, (_, _, first_rel) = plan.step(fins, last, (cross_core, fout_z, first_rel))

    queries_two = stack_project(first_rel, crosses.result, 0, (vectors, 5), (scaling,), BF)[0]
    mem_keys, mem_values = memory_project(mem_rel, crosses.result, 1, 2, (vectors, 6), 512)
    cross_out = ()
    for item in range(item_count):
        cross_out = cross_attend(
            queries_two, mem_keys, mem_values, mem_lengths, place, item, cross_out
        )
        if item == 0:
            last, cross_out = plan.across_steps(fins, last, cross_out)
    fin_core = plan.step(fins)
    last, (cross_out, _) = plan.step(fouts, last, (cross_out, fin_core))
    cross_ctx, cross_lse = cross_out
    fin = fins.result
    cross_rel = to_relative(cross_ctx)
    branch = stack_project(cross_rel, crosses.result, 3, (vectors, 7), (1.0,), F32)[0]
    second_pre, second, second_rel = add_norm(branch, first, (vectors, 9), (vectors, 8))

    places = plan.places()
    hidden, slope = ffn_up(second_rel, fin, fbin[None], places)
    _, (hidden, slope) = plan.across_steps(fouts, last, (hidden, slope))
    half = hidden.shape[1] // 2
    hidden_rel = (hidden[:, :half], hidden[:, half:])
    plan.step(fouts)
    fout = fouts.result
    third_pre = second + (forward(hidden_rel, fout) + vectors[10, 0])

    layer_out, d_third, e_three, third_sums = norm_back(
        [out_grad], third_pre, (vectors, 12), (vectors, 11)
    )
    half = model_width // 2
    to_fout = Stream(
        plan.scatter([hidden_rel], [e_three], [(0, 0, 0, half), (0, 0, half, half)])
    )
    d_pre = ffn_down_back(e_three, fout, slope, plan.blocks())
    _, d_pre = plan.step(to_fout, None, d_pre)
    half = d_pre.shape[1] // 2
    to_fin = Stream(plan.scatter([second_rel], [d_pre], [(0, 0, 0, half), (0, 0, half, half)]))
    d_hidden = back([d_pre], fin, None, row_count)
    last, (d_hidden, fin_sends) = plan.step(to_fout, None, (d_hidden, to_fin.values()))
    to_fin.replace(fin_sends)
    fin_core = plan.step(to_fin)

    d_second_pre, e_two, second_sums = norm_back([d_third, d_hidden], second_pre, (vectors, 9))
    d_cross_ctx = context_back(e_two, crosses.result)
    cross_back = ()
    for item in range(item_count):
        cross_back = cross_attend_back(
            queries_two, mem_keys, mem_values, cross_lse, d_cross_ctx, mem_lengths, place,
            item, cross_back,
        )
        if item == 0:
            last, (cross_back, _) = plan.across_steps(to_fout, last, (cross_back, fin_core))
    dq_scaled, dk_flat, dv_flat = cross_back
    to_cross = Stream(
        plan.scatter(
            [first_rel, mem_rel, cross_rel],
            [dq_scaled, dk_flat, dv_flat, e_two],
            [(0, 0, 0, model_width), (1, 1, 0, model_width), (1, 2, 0, model_width), (2, 3, 0, model_width)],
        )
    )
    for _ in plan.zs[1:]:
        fout_last = plan.step(to_fout)
    last, (dq_late, _, cross_sends) = plan.step(
        to_fin, last, (dq_scaled, fout_last, to_cross.values())
    )
    d_queries = back([dq_late], crosses.result, [0], row_count)
    to_cross.replace(cross_sends)
    cross_core = plan.step(to_cross)
    fout_last = plan.step(to_fout)

    d_first_pre, e_one, first_sums = norm_back([d_second_pre, d_queries], first_pre, (vectors, 4))
    d_self_ctx = context_back(e_one, selfs.result)
    last, (d_self_ctx, *_) = plan.across_steps(
        to_fin, last, (d_self_ctx, cross_core, fout_last)
    )
    dq_self, dk_self, dv_self = self_attend_back(qkv, self_lse, d_self_ctx, item_count, place)
    to_self = Stream(
        plan.scatter(
            [x_rel, self_rel],
            [dq_self, dk_self, dv_self, e_one],
            [(0, 0, 0, model_width), (0, 1, 0, model_width), (0, 2, 0, model_width), (1, 3, 0, model_width)],
        )
    )
    for _ in plan.zs[1:]:
        fin_last = plan.step(to_fin)
    last, (_, self_sends) = plan.step(to_cross, last, (fin_last, to_self.values()))
    to_self.replace(self_sends)
    self_core = plan.step(to_self)
    fin_last = plan.step(to_fin)
    late, _ = lax.optimization_barrier(((dq_self, dk_self, dv_self), last))
    d_inputs = back(late, selfs.result, [0, 1, 2], row_count)
    last, (d_inputs, *_) = plan.across_steps(
        to_cross, last, (d_inputs, self_core, fin_last)
    )
    input_grad = d_first_pre + d_inputs
    late, _ = lax.optimization_barrier(((dk_flat, dv_flat), last))
    memory_grad = back(late, crosses.result, [1, 2], 512).reshape(memory.shape)
    for _ in plan.zs[1:]:
        cross_last = plan.step(to_cross)
    last, _ = plan.step(to_self, last, (memory_grad, cross_last))
    cross_last = plan.step(to_cross)
    last, _ = plan.across_steps(to_self, last, cross_last)
    sums, _ = lax.optimization_barrier(((dq_self, dv_self, dq_scaled, dv_flat, d_pre), last))
    sum_dq, sum_dv, sum_dq2, sum_dv2, sum_hidden = [column_sums(v) for v in sums]
    grads = jnp.concatenate(
        [
            sum_dq[None],
            sum_dv[None],
            first_sums[:3],
            sum_dq2[None],
            sum_dv2[None],
            second_sums[:3],
            third_sums[:3],
        ],
        axis=0,
    )
    grads = jnp.swapaxes(grads.reshape(vector_count, plan.count, share), 0, 1)
    to_small = Stream(
        plan.scatter_small(
            pad_lanes(
                jnp.concatenate(
                    [grads.reshape(plan.count, -1), sum_hidden.reshape(plan.count, -1)], axis=1
                )
            )
        )
    )
    for _ in plan.zs[1:]:
        plan.step(to_small)
        plan.step(to_small)
        plan.step(to_small, plan.step(to_self))
    for stream in (to_self, to_cross, to_fin, to_fout):
        plan.finish(stream)
    plan.finish(to_small)
    small_sums = to_small.result
    found = small_sums[: vector_count * share].reshape(vector_count, share)
    g_hidden = small_sums[vector_count * share :][:hidden_share]
    early = [stream.result for stream in (to_cross, to_fin, to_fout)]
    early, _ = lax.optimization_barrier((early, last))
    g_self, g_cross, g_fin, g_fout = [
        keep + got.astype(F32) for keep, got in (to_self.result, *early)
    ]
    g_fout = jnp.concatenate([g_fout[0], g_fout[1]], axis=1)
    g_fin = jnp.concatenate([g_fin[0], g_fin[1]], axis=1)
    return (
        layer_out,
        input_grad,
        memory_grad,
        g_self[:3],
        g_self[3],
        found[:4],
        found[4],
        g_cross[:3],
        g_cross[3],
        found[5:9],
        found[9],
        g_fin,
        g_fout,
        g_hidden,
        found[10:12],
        found[12],
    )


def solution(mesh):
    both = ("wide", "narrow")
    placed = (
        P(both, None),
        P(both, None, None),
        P(both),
        P(None, both, None),
        P(both, None),
        P(None, both),
        P(both),
        P(None, both, None),
        P(both, None),
        P(None, both),
        P(both),
        P(both, None),
        P(both, None),
        P(both),
        P(None, both),
        P(both),
        P(both, None),
    )
    return jax.shard_map(
        local,
        mesh=mesh,
        in_specs=placed,
        out_specs=(
            P(both, None),
            P(both, None),
            P(both, None, None),
            P(None, both, None),
            P(both, None),
            P(None, both),
            P(both),
            P(None, both, None),
            P(both, None),
            P(None, both),
            P(both),
            P(both, None),
            P(both, None),
            P(both),
            P(None, both),
            P(both),
        ),
        check_vma=False,
    )
```
